256 devices in a mesh: blk: 32 (over y, z_hi, core), head: 8 (over x, z_lo).
Axes of the slice: x: 4, y: 4, z: 8 (z_hi: 4, z_lo: 2; z = z_hi * 2 + z_lo), core: 2. Of those that a mesh axis runs over, the one named last changes fastest.
Arguments:
- queries: bfloat16 [8192, 40, 128], P('blk', 'head'), may hold values from -8 to 8
- new_keys: bfloat16 [8192, 8, 128], P('blk', 'head'), may hold values from -6.5 to 6.5
- new_values: bfloat16 [8192, 8, 128], P('blk', 'head'), may hold values from -6 to 6
- cache_keys: bfloat16 [192, 128, 8, 128], P('blk', None, 'head'), may hold values from -6 to 6
- cache_values: bfloat16 [192, 128, 8, 128], P('blk', None, 'head'), may hold values from -6 to 6
- out_weight: bfloat16 [5120, 5120], P('blk', 'head'), may hold values from -0.078125 to 0.078125
- cache_len: int32 [8], replicated, may hold values from 128 to 6144, as said below
- span_len: int32 [8], replicated, may hold values from 128 to 2048, as said below
- block_table: int32 [8, 64], replicated, may hold values from 0 to 191, as said below
- window: int32 [8], replicated, may hold values from 2048 to 4096, as said below
Outputs:
- attn_output: bfloat16 [8192, 5120], P('blk', 'head')
- new_cache_keys: bfloat16 [192, 128, 8, 128], P('blk', None, 'head')
- new_cache_values: bfloat16 [192, 128, 8, 128], P('blk', None, 'head')
The draws below stay inside these ranges and needn't reach their ends.
Inputs may be any that keep to these rules, and one draw needn't show every extreme that they name: `cache_len`: multiples of 128; two requests hold 6144 tokens each, the other six fewer. `span_len`: multiples of 128 that sum to 8192; some request's is 2048. `block_table`: row r lists, in order of position, the slots of the cache_len[r] // 128 cached blocks of request r and then of the span_len[r] // 128 blocks of its span; every slot of the cache appears exactly once among these entries; a slot whose index modulo 6 is below 4 holds a cached block, the others receive blocks of the spans. Later entries of a row are arbitrary slots and unused. Some request's window is 4096.
All inputs are finite; a program needn't handle non-finite values.
Results may differ from the reference program's by a relative error of at most 0.015.
Values may be sent and summed in bfloat16 or wider, within the bound.
No kernel may reach another device: no remote copies, remote signals or barrier semaphores. Data moves between devices by JAX's collectives and lax.ppermute only.
A program may use at most 128 MiB of HBM per device.

```python
import math
import jax
import jax.numpy as jnp
from jax import lax

D = 5120
QH = 40
KVH = 8
HD = 128
BLOCK = 128
SINK = 4
REQ = 8
OLD_DEV = 4
GROUP = 5
NQB = 2
CB_DEV = 6
TOKENS = 8192
NEWB = 64
OLDB = 128
POOL = 192
MOSTB = 16
LONGB = 48
WLO = 2048
WHI = 4096
MAXB = 64
KB = 34
N_HEAD = 8


def split_evenly(key, total_count, parts):
    base_size = total_count // parts
    extra_count = total_count - parts * base_size
    sizes = base_size + (jnp.arange(parts, dtype=jnp.int32) < extra_count).astype(jnp.int32)
    moves = jax.random.randint(key, (parts // 2,), 0, base_size)
    sizes = sizes.at[0:2 * (parts // 2):2].add(-moves)
    sizes = sizes.at[1:2 * (parts // 2):2].add(moves)
    return sizes.astype(jnp.int32)


def layout(key):
    keys = jax.random.split(jax.random.fold_in(key, 4242), 9)
    span_blocks = jnp.concatenate([jnp.full((1,), MOSTB, jnp.int32), split_evenly(keys[0], NEWB - MOSTB, REQ - 1)])
    span_blocks = span_blocks[jax.random.permutation(keys[1], REQ)]
    cached_blocks = jnp.concatenate([jnp.full((2,), LONGB, jnp.int32), split_evenly(keys[2], OLDB - 2 * LONGB, REQ - 2)])
    cached_blocks = cached_blocks[jax.random.permutation(keys[3], REQ)]
    windows = jax.random.randint(keys[4], (REQ,), WLO, WHI + 1)
    windows = windows.at[jax.random.randint(keys[5], (), 0, REQ)].set(WHI).astype(jnp.int32)
    old_ids = jnp.arange(OLDB, dtype=jnp.int32)
    old_slots = old_ids // OLD_DEV * CB_DEV + old_ids % OLD_DEV
    old_slots = jax.random.permutation(keys[6], old_slots)
    new_ids = jnp.arange(NEWB, dtype=jnp.int32)
    new_slots = new_ids // NQB * CB_DEV + OLD_DEV + new_ids % NQB
    new_slots = jax.random.permutation(keys[7], new_slots)
    old_offset = (jnp.cumsum(cached_blocks) - cached_blocks).astype(jnp.int32)
    new_offset = (jnp.cumsum(span_blocks) - span_blocks).astype(jnp.int32)
    columns = jnp.arange(MAXB, dtype=jnp.int32)[None, :]
    old_pick = old_slots[jnp.clip(old_offset[:, None] + columns, 0, OLDB - 1)]
    new_pick = new_slots[jnp.clip(new_offset[:, None] + columns - cached_blocks[:, None], 0, NEWB - 1)]
    filler = jax.random.randint(keys[8], (REQ, MAXB), 0, POOL)
    table = jnp.where(columns < cached_blocks[:, None], old_pick, jnp.where(columns < (cached_blocks + span_blocks)[:, None], new_pick, filler))
    return (cached_blocks * BLOCK, span_blocks * BLOCK, table.astype(jnp.int32), windows)


def draw_queries(key, part):
    base_key = jax.random.fold_in(key, 1)
    result = jnp.clip(2.5 * jax.random.normal(base_key, (TOKENS, QH, HD), jnp.float32), -8.0, 8.0)
    return result.astype(jnp.bfloat16)


def draw_new_keys(key, part):
    base_key = jax.random.fold_in(key, 2)
    result = jnp.clip(jax.random.normal(base_key, (TOKENS, KVH, HD), jnp.float32), -6.0, 6.0)
    return result.astype(jnp.bfloat16)


def draw_cache_len(key, part):
    return layout(key)[0]


def draw_span_len(key, part):
    return layout(key)[1]


def draw_block_table(key, part):
    return layout(key)[2]


def draw_window(key, part):
    return layout(key)[3]


def shard_levels(rng, dims, pieces, smallest, top_value):
    loudness = 1.0
    for position, blocks in pieces:
        steps = jax.random.uniform(jax.random.fold_in(jax.random.fold_in(rng, 6), position), (blocks,), jnp.float32, smallest / len(pieces), top_value / len(pieces))
        loudness = loudness * jnp.repeat(jnp.exp(steps), dims[position] // blocks).reshape((-1,) + (1,) * (len(dims) - 1 - position))
    return loudness


def normal_values(stream_key, dims, scale, most, shards=(), kind=jnp.bfloat16):
    drawn = jax.random.normal(stream_key, dims, jnp.float32) * scale
    if len(shards) > 0:
        drawn = shard_levels(stream_key, dims, shards, -0.22, 0.18) * drawn
    return jnp.clip(drawn, min=-most, max=most).astype(kind)


def setup_inputs(seed: int = 0) -> dict:
    streams_of = jax.random.split(jax.random.key(seed), 11)
    queries = draw_queries(jax.random.fold_in(streams_of[10], 71), 0)
    new_keys = draw_new_keys(jax.random.fold_in(streams_of[10], 71), 0)
    new_values = normal_values(streams_of[2], (TOKENS, KVH, HD), 1.0, 6.0, ((0, 32), (1, 8)))
    cache_keys = normal_values(streams_of[3], (POOL, BLOCK, KVH, HD), 1.0, 6.0, ((0, 32), (2, 8)))
    cache_values = normal_values(streams_of[4], (POOL, BLOCK, KVH, HD), 1.0, 6.0, ((0, 32), (2, 8)))
    out_weight = normal_values(streams_of[5], (D, QH * HD), (QH * HD) ** -0.5, 0.078125, ((0, 32), (1, 8)))
    cache_len = draw_cache_len(jax.random.fold_in(streams_of[10], 71), 0)
    span_len = draw_span_len(jax.random.fold_in(streams_of[10], 71), 0)
    block_table = draw_block_table(jax.random.fold_in(streams_of[10], 71), 0)
    window = draw_window(jax.random.fold_in(streams_of[10], 71), 0)
    return {"queries": queries, "new_keys": new_keys, "new_values": new_values, "cache_keys": cache_keys, "cache_values": cache_values, "out_weight": out_weight, "cache_len": cache_len, "span_len": span_len, "block_table": block_table, "window": window}


def reference(queries, new_keys, new_values, cache_keys, cache_values, out_weight, cache_len, span_len, block_table, window):
    block_total = TOKENS // BLOCK
    span_end = jnp.cumsum(span_len).astype(jnp.int32)
    span_begin = (span_end - span_len).astype(jnp.int32)
    block_ids = jnp.arange(block_total, dtype=jnp.int32)
    first_token = block_ids * BLOCK
    requests = lax.optimization_barrier(jnp.sum((first_token[:, None] >= span_end[None, :]).astype(jnp.int32), axis=1))
    positions = (cache_len[requests] + first_token - span_begin[requests]).astype(jnp.int32)
    targets = block_table[requests, positions // BLOCK]
    pool_keys = cache_keys.at[targets].set(new_keys.reshape(block_total, BLOCK, KVH, HD))
    pool_values = cache_values.at[targets].set(new_values.reshape(block_total, BLOCK, KVH, HD))
    score_scale = 1.0 / math.sqrt(HD)

    def one_block(block_index):
        request = requests[block_index]
        first_pos = positions[block_index]
        reach_len = window[request]
        lowest = jnp.maximum((first_pos - reach_len + 1) // BLOCK, 0)
        lowest = jnp.minimum(lowest, MAXB - KB).astype(jnp.int32)
        table_row = block_table[request]
        chosen = lax.dynamic_slice_in_dim(table_row, lowest, KB)
        keys_seen = jnp.concatenate([pool_keys[chosen].reshape(KB * BLOCK, KVH, HD), pool_keys[table_row[0], :SINK]], axis=0)
        values_seen = jnp.concatenate([pool_values[chosen].reshape(KB * BLOCK, KVH, HD), pool_values[table_row[0], :SINK]], axis=0)
        key_pos = jnp.concatenate([lowest * BLOCK + jnp.arange(KB * BLOCK, dtype=jnp.int32), jnp.arange(SINK, dtype=jnp.int32)])
        sink_live = jnp.concatenate([jnp.ones((KB * BLOCK,), dtype=bool), jnp.full((SINK,), lowest > 0)])
        query_pos = first_pos + jnp.arange(BLOCK, dtype=jnp.int32)
        distance = query_pos[:, None] - key_pos[None, :]
        allowed = sink_live[None, :] & (distance >= 0) & ((distance < reach_len) | (key_pos[None, :] < SINK))
        query_rows = lax.dynamic_slice_in_dim(queries, block_index * BLOCK, BLOCK).reshape(BLOCK, KVH, GROUP, HD).astype(jnp.float32)
        scores = jnp.einsum('tkgd,skd->kgts', query_rows, keys_seen.astype(jnp.float32)) * score_scale
        highest = lax.optimization_barrier(jnp.max(jnp.where(allowed, scores, -jnp.inf), axis=-1))
        weights = jnp.where(allowed, jnp.exp(scores - highest[..., None]), 0.0)
        totals = lax.optimization_barrier(jnp.sum(weights, axis=-1))
        rounded = lax.optimization_barrier(weights.astype(jnp.bfloat16)).astype(jnp.float32)
        mixed_rows = jnp.einsum('kgts,skd->kgtd', rounded, values_seen.astype(jnp.float32)) / totals[..., None]
        mixed_rows = mixed_rows.astype(jnp.bfloat16)
        return jnp.transpose(mixed_rows, (2, 0, 1, 3)).reshape(BLOCK, QH * HD)
    attention = lax.map(one_block, block_ids).reshape(TOKENS, QH * HD)
    group_width = QH * HD // N_HEAD

    def add_group(running, group_index):
        columns = lax.dynamic_slice_in_dim(attention, group_index * group_width, group_width, axis=1)
        weight_cols = lax.dynamic_slice_in_dim(out_weight, group_index * group_width, group_width, axis=1)
        partial_out = lax.dot_general(columns, weight_cols, (((1,), (1,)), ((), ())), preferred_element_type=jnp.float32)
        partial_out = lax.optimization_barrier(partial_out.astype(jnp.bfloat16)).astype(jnp.float32)
        return (running + partial_out, None)
    summed, unused = lax.scan(add_group, jnp.zeros((TOKENS, D), jnp.float32), jnp.arange(N_HEAD, dtype=jnp.int32))
    return (summed.astype(jnp.bfloat16), pool_keys, pool_values)
```

```python
import functools
import math

import jax
import jax.numpy as jnp
from jax import lax
from jax.experimental import pallas as pl
from jax.experimental.pallas import tpu as pltpu
from jax.sharding import PartitionSpec as P

NY, NZ, NC = 4, 4, 2
SINK = 4
LOWEST = -1e30
FLOOR = -1e25
FAR = 1 << 29
SHIFTS = (0, 1, -1, 2)


def blk_perm(dy, dz, dc):
    pairs = []
    for y in range(NY):
        for z in range(NZ):
            for c in range(NC):
                src = (y * NZ + z) * NC + c
                dst = ((y + dy) % NY * NZ + (z + dz) % NZ) * NC + (c + dc) % NC
                pairs.append((src, dst))
    return pairs


def shift(value, dy=0, dz=0, dc=0):
    return lax.ppermute(value, "blk", blk_perm(dy, dz, dc))


def lookup(table_row, wanted):
    places = jnp.arange(table_row.shape[0], dtype=jnp.int32)
    return jnp.sum(jnp.where(places[None, :] == wanted[:, None], table_row[None, :], 0), axis=1)


def block_start(global_block, span_len, cache_len, block_size):
    lower = jnp.arange(span_len.shape[0], dtype=jnp.int32)
    span_end = jnp.sum(jnp.where(lower[:, None] >= lower[None, :], span_len[None, :], 0), axis=1)
    first_token = global_block * block_size
    request = jnp.sum((first_token[:, None] >= span_end[None, :]).astype(jnp.int32), axis=1)
    return (request, lookup(cache_len - span_end + span_len, request) + first_token)


def table_entry(block_table, request, logical):
    row_ids = jnp.arange(block_table.shape[0], dtype=jnp.int32)
    col_ids = jnp.arange(block_table.shape[1], dtype=jnp.int32)
    match = (row_ids[None, :, None] == request[:, None, None]) & (
        col_ids[None, None, :] == logical[:, None, None]
    )
    return jnp.sum(jnp.where(match, block_table[None], 0), axis=(1, 2))


def slot_owner(block_table, limit, slot_ids):
    row_ids = jnp.arange(block_table.shape[0], dtype=jnp.int32)
    col_ids = jnp.arange(block_table.shape[1], dtype=jnp.int32)
    match = (block_table[None] == slot_ids[:, None, None]) & (
        col_ids[None, None, :] < limit[None, :, None]
    )
    packed = row_ids[:, None] * 4096 + col_ids[None, :] + 1
    found = jnp.sum(jnp.where(match, packed[None], 0), axis=(1, 2))
    place = jnp.maximum(found - 1, 0)
    return (place // 4096, place % 4096, found > 0)


def pack_kernel(ck, cv, nk, nv, out, sem):
    old = 4
    new = nk.shape[0]
    copies = [
        pltpu.make_async_copy(ck.at[pl.ds(0, old)], out.at[pl.ds(0, old)], sem.at[0]),
        pltpu.make_async_copy(nk, out.at[pl.ds(old, new)], sem.at[1]),
        pltpu.make_async_copy(cv.at[pl.ds(0, old)], out.at[pl.ds(old + new, old)], sem.at[2]),
        pltpu.make_async_copy(nv, out.at[pl.ds(2 * old + new, new)], sem.at[3]),
    ]
    for copy in copies:
        copy.start()
    for copy in copies:
        copy.wait()


def pack(ck, cv, nk, nv):
    anywhere = pl.BlockSpec(memory_space=pl.ANY)
    return pl.pallas_call(
        pack_kernel,
        out_shape=jax.ShapeDtypeStruct((2 * ck.shape[0],) + ck.shape[1:], ck.dtype),
        in_specs=[anywhere] * 4,
        out_specs=anywhere,
        scratch_shapes=[pltpu.SemaphoreType.DMA((4,))],
        name="pack",
    )(ck, cv, nk, nv)


def attend_kernel(
    log_scale,
    nkv,
    nq,
    count,
    chosen,
    partial_view,
    first_key,
    first_query,
    reach,
    moves,
    *refs,
):
    kv_in = refs[:nkv]
    q_in = refs[nkv : nkv + nq]
    out_refs = refs[nkv + nq : nkv + 2 * nq]
    move_refs = refs[nkv + 2 * nq : nkv + 3 * nq]
    kv, queries, scores, high, total, result, in_sem, out_sem, move_sem = refs[nkv + 3 * nq :]
    slots = kv_in[0].shape[0]
    half = slots // 2
    heads, rows, width = q_in[0].shape
    size = kv_in[0].shape[1]
    per = rows // size
    wide = heads * size
    longest = chosen.shape[0] // (nq * per)
    loads = []
    for a in range(nkv):
        loads.append(
            pltpu.make_async_copy(kv_in[a], kv.at[pl.ds(a * slots, slots)], in_sem.at[a])
        )
    for r in range(nq):
        loads.append(pltpu.make_async_copy(q_in[r], queries.at[r], in_sem.at[nkv + r]))
    for load in loads:
        load.start()
    for load in loads:
        load.wait()

    def place(j):
        return j // half * slots + j % half

    sends = []
    for r in range(nq):
        for s in range(per):
            at = place(moves[r * per + s])
            for side in range(2):
                sends.append(
                    pltpu.make_async_copy(
                        kv.at[at + side * half],
                        move_refs[r].at[2 * s + side],
                        move_sem.at[(r * per + s) * 2 + side],
                    )
                )
    for send in sends:
        send.start()

    row_ids = lax.broadcasted_iota(jnp.int32, (size, width), 0)
    col_ids = lax.broadcasted_iota(jnp.int32, (size, width), 1)
    ones = jnp.ones((2 * size, width), jnp.bfloat16)

    def one_block(i, unused):
        r = i // per
        s = i % per
        begin = pl.multiple_of(s * size, size)
        query = jnp.concatenate(
            [queries[r, h, pl.ds(begin, size), :] for h in range(heads)], axis=0
        )
        pairs = (count[i] + 1) // 2
        high[...] = jnp.full_like(high, LOWEST)

        def score(t, unused):
            at = i * longest + 2 * t
            keys = jnp.concatenate([kv[place(chosen[at])], kv[place(chosen[at + 1])]], axis=0)
            raw = lax.dot_general(
                query, keys, (((1,), (1,)), ((), ())), preferred_element_type=jnp.float32
            )
            edge = partial_view[at] + partial_view[at + 1]

            @pl.when(edge > 0)
            def _():
                for side in range(2):
                    key_pos = first_key[at + side] + col_ids
                    distance = first_query[i] + row_ids - key_pos
                    allowed = (distance >= 0) & ((distance < reach[i]) | (key_pos < SINK))
                    bias = jnp.where(allowed, 0.0, LOWEST)
                    for h in range(heads):
                        lines = slice(h * size, (h + 1) * size)
                        part = raw[lines, side * size : (side + 1) * size]
                        part = jnp.where(bias < 0.0, LOWEST, part)
                        scores[t, lines, side * size : (side + 1) * size] = part
                        high[lines, :] = jnp.maximum(high[lines, :], part)

            @pl.when(edge == 0)
            def _():
                scores[t] = raw
                high[...] = jnp.maximum(
                    high[...], jnp.maximum(raw[:, :size], raw[:, size:])
                )

            return unused

        lax.fori_loop(0, pairs, score, 0)
        top = jnp.maximum(jnp.max(high[...], axis=1, keepdims=True), FLOOR)
        high[...] = jnp.broadcast_to(top, high.shape)
        total[...] = jnp.zeros_like(total)

        def blend(t, unused):
            at = i * longest + 2 * t
            values = jnp.concatenate(
                [kv[place(chosen[at]) + half], kv[place(chosen[at + 1]) + half]], axis=0
            )
            values = jnp.concatenate([values, ones], axis=1)
            level = high[...]
            level = jnp.concatenate([level, level], axis=1)
            weights = jnp.exp2((scores[t] - level) * log_scale).astype(jnp.bfloat16)
            total[...] += jnp.dot(weights, values, preferred_element_type=jnp.float32)
            return unused

        lax.fori_loop(0, pairs, blend, 0)
        summed = total[:, width:]
        live = summed > 0.0
        safe = jnp.where(live, summed, 1.0)
        result[i, 0:wide, :] = (total[:, :width] / safe).astype(jnp.bfloat16)
        level = jnp.where(live, high[...] * log_scale + jnp.log2(safe), LOWEST)
        line_ids = lax.broadcasted_iota(jnp.int32, (16, width), 0)
        stats = jnp.zeros((16, width), jnp.float32)
        for h in range(heads):
            tile = level[h * size : (h + 1) * size, :]
            row = jnp.sum(jnp.where(row_ids == col_ids, tile, 0.0), axis=0, keepdims=True)
            for part in range(3):
                piece = row.astype(jnp.bfloat16).astype(jnp.float32)
                row = row - piece
                stats = jnp.where(line_ids == part * heads + h, piece, stats)
        result[i, wide : wide + 16, :] = stats.astype(jnp.bfloat16)
        return unused

    lax.fori_loop(0, nq * per, one_block, 0)
    backs = []
    for r in range(nq):
        backs.append(
            pltpu.make_async_copy(result.at[pl.ds(r * per, per)], out_refs[r], out_sem.at[r])
        )
    for back in backs:
        back.start()
    for send in sends:
        send.wait()
    for back in backs:
        back.wait()


def attend(meta, kv_parts, q_parts, log_scale):
    slots, size, width = kv_parts[0].shape
    heads, rows, _ = q_parts[0].shape
    nkv, nq, per = len(kv_parts), len(q_parts), rows // size
    wide = heads * size
    longest = meta[1].shape[0] // (nq * per)
    smem = pl.BlockSpec(memory_space=pltpu.SMEM)
    anywhere = pl.BlockSpec(memory_space=pl.ANY)
    parts = jax.ShapeDtypeStruct((per, wide + 16, width), jnp.bfloat16)
    moved = jax.ShapeDtypeStruct((2 * per, size, width), jnp.bfloat16)
    return pl.pallas_call(
        functools.partial(attend_kernel, log_scale, nkv, nq),
        out_shape=(parts,) * nq + (moved,) * nq,
        in_specs=[smem] * len(meta) + [anywhere] * (nkv + nq),
        out_specs=(anywhere,) * (2 * nq),
        scratch_shapes=[
            pltpu.VMEM((nkv * slots, size, width), jnp.bfloat16),
            pltpu.VMEM((nq, heads, rows, width), jnp.bfloat16),
            pltpu.VMEM((longest // 2, wide, 2 * size), jnp.float32),
            pltpu.VMEM((wide, size), jnp.float32),
            pltpu.VMEM((wide, 2 * width), jnp.float32),
            pltpu.VMEM((nq * per, wide + 16, width), jnp.bfloat16),
            pltpu.SemaphoreType.DMA((nkv + nq,)),
            pltpu.SemaphoreType.DMA((nq,)),
            pltpu.SemaphoreType.DMA((2 * nq * per,)),
        ],
        compiler_params=pltpu.CompilerParams(vmem_limit_bytes=40 << 20),
        cost_estimate=pl.CostEstimate(
            flops=5_000_000_000, bytes_accessed=8_000_000, transcendentals=8_000_000
        ),
        name="attend",
    )(*meta, *kv_parts, *q_parts)


def merge_kernel(heads, *refs):
    parts = refs[:-1]
    out = refs[-1]
    per, lines, width = parts[0].shape
    size = (lines - 16) // heads
    row_ids = lax.broadcasted_iota(jnp.int32, (size, width), 0)
    col_ids = lax.broadcasted_iota(jnp.int32, (size, width), 1)
    for s in range(per):
        levels = []
        for part in parts:
            stats = part[s, heads * size :, :].astype(jnp.float32)
            levels.append(
                stats[0:heads] + stats[heads : 2 * heads] + stats[2 * heads : 3 * heads]
            )
        top = functools.reduce(jnp.maximum, levels)
        shares = [jnp.exp2(level - top) for level in levels]
        whole = functools.reduce(jnp.add, shares)
        shares = [share / whole for share in shares]
        for h in range(heads):
            mixed = jnp.zeros((size, width), jnp.float32)
            for part, share in zip(parts, shares):
                spread = jnp.where(row_ids == col_ids, share[h : h + 1, :], 0.0)
                column = jnp.sum(spread, axis=1, keepdims=True)
                mixed += column * part[s, h * size : (h + 1) * size, :].astype(jnp.float32)
            out[s * size : (s + 1) * size, h * width : (h + 1) * width] = mixed.astype(
                jnp.bfloat16
            )


def merge(parts, heads):
    per, lines, width = parts[0].shape
    size = (lines - 16) // heads
    return pl.pallas_call(
        functools.partial(merge_kernel, heads),
        out_shape=jax.ShapeDtypeStruct((per * size, heads * width), jnp.bfloat16),
        name="merge",
    )(*parts)


def refill_kernel(nq, source, ck, cv, *refs):
    moved = refs[:nq]
    new_ck, new_cv, sem = refs[nq:]
    old = 4
    per = ck.shape[0] - old
    keeps = [
        pltpu.make_async_copy(ck.at[pl.ds(0, old)], new_ck.at[pl.ds(0, old)], sem.at[0]),
        pltpu.make_async_copy(cv.at[pl.ds(0, old)], new_cv.at[pl.ds(0, old)], sem.at[1]),
    ]
    for keep in keeps:
        keep.start()
    for s in range(per):
        for r in range(nq):

            @pl.when(source[s] == r)
            def _():
                fills = [
                    pltpu.make_async_copy(moved[r].at[2 * s], new_ck.at[old + s], sem.at[2]),
                    pltpu.make_async_copy(moved[r].at[2 * s + 1], new_cv.at[old + s], sem.at[3]),
                ]
                for fill in fills:
                    fill.start()
                for fill in fills:
                    fill.wait()

    for keep in keeps:
        keep.wait()


def refill(source, ck, cv, moved):
    anywhere = pl.BlockSpec(memory_space=pl.ANY)
    shape = jax.ShapeDtypeStruct(ck.shape, ck.dtype)
    return pl.pallas_call(
        functools.partial(refill_kernel, len(moved)),
        out_shape=(shape, shape),
        in_specs=[pl.BlockSpec(memory_space=pltpu.SMEM)] + [anywhere] * (2 + len(moved)),
        out_specs=(anywhere, anywhere),
        scratch_shapes=[pltpu.SemaphoreType.DMA((4,))],
        name="refill",
    )(source, ck, cv, *moved)


def plan(device, per, slots, size, cache_len, span_len, block_table, window):
    old = slots - per
    c = device % NC
    z = device // NC % NZ
    y = device // (NC * NZ)
    ring = jnp.array([-k for k in SHIFTS], jnp.int32)
    q_dev = ((y + ring) % NY * NZ + z) * NC + c
    pair = jnp.arange(NC, dtype=jnp.int32)
    k_dev = ((y * NZ + (z + ring[:, None]) % NZ) * NC + (c + pair[None, :]) % NC).reshape(-1)
    slot = jnp.arange(slots, dtype=jnp.int32)
    step = jnp.arange(per, dtype=jnp.int32)
    q_ids = (q_dev[:, None] * per + step[None, :]).reshape(-1)
    q_request, q_first = block_start(q_ids, span_len, cache_len, size)
    q_window = lookup(window, q_request)
    within = jnp.tile(slot, k_dev.shape[0])
    owner = jnp.repeat(k_dev, slots)
    is_old = within < old
    o_request, o_logical, o_live = slot_owner(block_table, cache_len // size, owner * slots + within)
    n_request, n_first = block_start(
        owner * per + jnp.maximum(within - old, 0), span_len, cache_len, size
    )
    k_request = jnp.where(is_old, o_request, n_request)
    k_first = jnp.where(is_old, o_logical * size, n_first)
    live = jnp.where(is_old, o_live, True)
    last = q_first + size - 1
    seen = (
        live[None, :]
        & (q_request[:, None] == k_request[None, :])
        & (k_first[None, :] <= last[:, None])
        & (
            (k_first[None, :] < SINK)
            | (q_first[:, None] - (k_first[None, :] + size - 1) < q_window[:, None])
        )
    )
    inside = (k_first[None, :] + size - 1 <= q_first[:, None]) & (
        last[:, None] - k_first[None, :] < q_window[:, None]
    )
    total = k_first.shape[0]
    ids = jnp.arange(total, dtype=jnp.int32)
    hits = seen.astype(jnp.int32)
    count = jnp.sum(hits, axis=1)
    rank = jnp.sum(jnp.where(ids[None, None, :] < ids[None, :, None], hits[:, None, :], 0), axis=2)
    at = seen[:, None, :] & (rank[:, None, :] == ids[None, :, None])
    pick = lambda x: jnp.sum(jnp.where(at, x, 0), axis=2)
    filled = ids[None, :] < count[:, None]
    chosen = pick(ids[None, None, :])
    edge = jnp.where(filled, pick(1 - inside.astype(jnp.int32)[:, None, :]), 1)
    first_key = jnp.where(filled, pick(k_first[None, None, :]), FAR)
    targets = table_entry(block_table, n_request, n_first // size)
    wanted = (q_dev[:, None] * slots + old + step[None, :]).reshape(-1)
    hit = (targets[None, :] == wanted[:, None]) & ~is_old[None, :]
    moves = jnp.sum(jnp.where(hit, ids[None, :], 0), axis=1)
    all_new = jnp.arange(NY * NZ * NC * per, dtype=jnp.int32)
    a_request, a_first = block_start(all_new, span_len, cache_len, size)
    a_target = table_entry(block_table, a_request, a_first // size)
    mine = a_target[None, :] == (device * slots + old + step)[:, None]
    from_y = jnp.sum(jnp.where(mine, (all_new // (per * NC * NZ))[None, :], 0), axis=1)
    ahead = (from_y - y) % NY
    source = jnp.where(ahead == NY - 1, 2, jnp.where(ahead == 2, 3, ahead))
    meta = (
        count,
        chosen.reshape(-1),
        edge.reshape(-1),
        first_key.reshape(-1),
        q_first,
        q_window,
        moves,
    )
    return meta, source


def shards(
    queries,
    new_keys,
    new_values,
    cache_keys,
    cache_values,
    out_weight,
    cache_len,
    span_len,
    block_table,
    window,
):
    device = lax.axis_index("blk")
    tokens, heads, width = queries.shape
    slots, size = cache_keys.shape[:2]
    per = tokens // size
    log_scale = math.log2(math.e) / math.sqrt(width)
    ck = cache_keys.reshape(slots, size, width)
    cv = cache_values.reshape(slots, size, width)
    own_kv = pack(
        ck, cv, new_keys.reshape(per, size, width), new_values.reshape(per, size, width)
    )
    own_q = jnp.transpose(queries, (1, 0, 2))
    lines = [own_kv] + [shift(own_kv, dz=k) for k in SHIFTS[1:]]
    q_parts = [own_q] + [shift(own_q, dy=k) for k in SHIFTS[1:]]
    kv_parts = []
    for part in lines:
        kv_parts += [part, shift(part, dc=1)]
    weight = lax.all_gather(out_weight, "blk", axis=0, tiled=True)
    meta, source = plan(device, per, slots, size, cache_len, span_len, block_table, window)
    outs = attend(meta, kv_parts, q_parts, log_scale)
    parts, moved = outs[: len(SHIFTS)], outs[len(SHIFTS) :]
    parts = [parts[0]] + [shift(p, dy=-k) for p, k in zip(parts[1:], SHIFTS[1:])]
    moved = [moved[0]] + [shift(p, dy=-k) for p, k in zip(moved[1:], SHIFTS[1:])]
    attention = merge(parts, heads)
    partial_out = lax.dot_general(
        attention, weight, (((1,), (1,)), ((), ())), preferred_element_type=jnp.float32
    ).astype(jnp.bfloat16)
    n_head = lax.axis_size("head")
    blocks = jnp.moveaxis(partial_out.reshape(tokens, n_head, -1), 1, 0)
    arrived = lax.all_to_all(blocks, "head", split_axis=0, concat_axis=0, tiled=True)
    attn_output = arrived.astype(jnp.float32).sum(axis=0).astype(jnp.bfloat16)
    new_ck, new_cv = refill(source, ck, cv, moved)
    return (
        attn_output,
        new_ck.reshape(cache_keys.shape),
        new_cv.reshape(cache_values.shape),
    )


def solution(mesh):
    placed = (
        P("blk", "head", None),
        P("blk", "head", None),
        P("blk", "head", None),
        P("blk", None, "head", None),
        P("blk", None, "head", None),
        P("blk", "head"),
        P(),
        P(),
        P(),
        P(),
    )
    return jax.shard_map(
        shards,
        mesh=mesh,
        in_specs=placed,
        out_specs=(P("blk", "head"), P("blk", None, "head", None), P("blk", None, "head", None)),
        check_vma=False,
    )
```

```python
import functools
import math

import jax
import jax.numpy as jnp
from jax import lax
from jax.experimental import pallas as pl
from jax.experimental.pallas import tpu as pltpu
from jax.sharding import PartitionSpec as P

NY, NZ, NC = 4, 4, 2
SINK = 4
LOWEST = -1e30
FLOOR = -1e25
FAR = 1 << 29
SHIFTS = (0, 1, -1, 2)


def blk_perm(dy, dz, dc):
    pairs = []
    for y in range(NY):
        for z in range(NZ):
            for c in range(NC):
                src = (y * NZ + z) * NC + c
                dst = ((y + dy) % NY * NZ + (z + dz) % NZ) * NC + (c + dc) % NC
                pairs.append((src, dst))
    return pairs


def shift(value, dy=0, dz=0, dc=0):
    return lax.ppermute(value, "blk", blk_perm(dy, dz, dc))


def lookup(table_row, wanted):
    places = jnp.arange(table_row.shape[0], dtype=jnp.int32)
    return jnp.sum(jnp.where(places[None, :] == wanted[:, None], table_row[None, :], 0), axis=1)


def block_start(global_block, span_len, cache_len, block_size):
    lower = jnp.arange(span_len.shape[0], dtype=jnp.int32)
    span_end = jnp.sum(jnp.where(lower[:, None] >= lower[None, :], span_len[None, :], 0), axis=1)
    first_token = global_block * block_size
    request = jnp.sum((first_token[:, None] >= span_end[None, :]).astype(jnp.int32), axis=1)
    return (request, lookup(cache_len - span_end + span_len, request) + first_token)


def table_entry(block_table, request, logical):
    row_ids = jnp.arange(block_table.shape[0], dtype=jnp.int32)
    col_ids = jnp.arange(block_table.shape[1], dtype=jnp.int32)
    match = (row_ids[None, :, None] == request[:, None, None]) & (
        col_ids[None, None, :] == logical[:, None, None]
    )
    return jnp.sum(jnp.where(match, block_table[None], 0), axis=(1, 2))


def slot_owner(block_table, limit, slot_ids):
    row_ids = jnp.arange(block_table.shape[0], dtype=jnp.int32)
    col_ids = jnp.arange(block_table.shape[1], dtype=jnp.int32)
    match = (block_table[None] == slot_ids[:, None, None]) & (
        col_ids[None, None, :] < limit[None, :, None]
    )
    packed = row_ids[:, None] * 4096 + col_ids[None, :] + 1
    found = jnp.sum(jnp.where(match, packed[None], 0), axis=(1, 2))
    place = jnp.maximum(found - 1, 0)
    return (place // 4096, place % 4096, found > 0)


def pack_kernel(ck, cv, nk, nv, out):
    new = nk.shape[0]
    old = ck.shape[0] - new
    out[0:old] = ck[0:old]
    out[old : old + new] = nk[...]
    out[old + new : 2 * old + new] = cv[0:old]
    out[2 * old + new :] = nv[...]


def pack(ck, cv, nk, nv):
    return pl.pallas_call(
        pack_kernel,
        out_shape=jax.ShapeDtypeStruct((2 * ck.shape[0],) + ck.shape[1:], ck.dtype),
        name="pack",
    )(ck, cv, nk, nv)


def attend_kernel(
    log_scale,
    nkv,
    nq,
    count,
    chosen,
    edges,
    first_key,
    first_query,
    reach,
    moves,
    *refs,
):
    kv_in = refs[:nkv]
    q_in = refs[nkv : nkv + nq]
    out_refs = refs[nkv + nq : nkv + 2 * nq]
    move_refs = refs[nkv + 2 * nq : nkv + 3 * nq]
    kv, queries, scores, high, total, result, in_sem, out_sem, move_sem = refs[nkv + 3 * nq :]
    slots = kv_in[0].shape[0]
    half = slots // 2
    heads, rows, width = q_in[0].shape
    size = kv_in[0].shape[1]
    per = rows // size
    wide = heads * size
    longest = chosen.shape[0] // (nq * per)
    loads = []
    for a in range(nkv):
        loads.append(
            pltpu.make_async_copy(kv_in[a], kv.at[pl.ds(a * slots, slots)], in_sem.at[a])
        )
    for r in range(nq):
        loads.append(pltpu.make_async_copy(q_in[r], queries.at[r], in_sem.at[nkv + r]))
    for load in loads:
        load.start()
    for load in loads:
        load.wait()

    def place(j):
        return j // half * slots + j % half

    sends = []
    for r in range(nq):
        for s in range(per):
            at = place(moves[r * per + s])
            for side in range(2):
                sends.append(
                    pltpu.make_async_copy(
                        kv.at[at + side * half],
                        move_refs[r].at[2 * s + side],
                        move_sem.at[(r * per + s) * 2 + side],
                    )
                )
    for send in sends:
        send.start()

    row_ids = lax.broadcasted_iota(jnp.int32, (size, width), 0)
    col_ids = lax.broadcasted_iota(jnp.int32, (size, width), 1)
    ones = jnp.ones((2 * size, width), jnp.bfloat16)

    def one_block(i, unused):
        r = i // per
        s = i % per
        begin = pl.multiple_of(s * size, size)
        query = jnp.concatenate(
            [queries[r, h, pl.ds(begin, size), :] for h in range(heads)], axis=0
        )
        pairs = (count[i] + 1) // 2
        high[...] = jnp.full_like(high, LOWEST)

        def raw_scores(t):
            at = i * longest + 2 * t
            keys = jnp.concatenate([kv[place(chosen[at])], kv[place(chosen[at + 1])]], axis=0)
            return lax.dot_general(
                query, keys, (((1,), (1,)), ((), ())), preferred_element_type=jnp.float32
            )

        def score_edge(t, unused):
            raw = raw_scores(t)
            for side in range(2):
                key_pos = first_key[i * longest + 2 * t + side] + col_ids
                distance = first_query[i] + row_ids - key_pos
                allowed = (distance >= 0) & ((distance < reach[i]) | (key_pos < SINK))
                hidden = jnp.where(allowed, 0.0, LOWEST)
                for h in range(heads):
                    lines = slice(h * size, (h + 1) * size)
                    part = raw[lines, side * size : (side + 1) * size]
                    part = jnp.where(hidden < 0.0, LOWEST, part)
                    scores[t, lines, side * size : (side + 1) * size] = part
                    high[lines, :] = jnp.maximum(high[lines, :], part)
            return unused

        def score_full(t, unused):
            raw = raw_scores(t)
            scores[t] = raw
            high[...] = jnp.maximum(high[...], jnp.maximum(raw[:, :size], raw[:, size:]))
            return unused

        lax.fori_loop(0, edges[i], score_edge, 0)
        lax.fori_loop(edges[i], pairs, score_full, 0)
        top = jnp.maximum(jnp.max(high[...], axis=1, keepdims=True), FLOOR)
        high[...] = jnp.broadcast_to(top, high.shape)
        total[...] = jnp.zeros_like(total)

        def blend(t, unused):
            at = i * longest + 2 * t
            values = jnp.concatenate(
                [kv[place(chosen[at]) + half], kv[place(chosen[at + 1]) + half]], axis=0
            )
            values = jnp.concatenate([values, ones], axis=1)
            level = high[...]
            level = jnp.concatenate([level, level], axis=1)
            weights = jnp.exp2((scores[t] - level) * log_scale).astype(jnp.bfloat16)
            total[...] += jnp.dot(weights, values, preferred_element_type=jnp.float32)
            return unused

        lax.fori_loop(0, pairs, blend, 0)
        summed = total[:, width:]
        safe = jnp.where(summed > 0.0, summed, 1.0)
        result[i, 0:wide, :] = (total[:, :width] / safe).astype(jnp.bfloat16)
        line_ids = lax.broadcasted_iota(jnp.int32, (16, width), 0)
        tops = jnp.zeros((16, width), jnp.float32)
        sums = jnp.zeros((16, width), jnp.float32)
        for h in range(heads):
            lines = slice(h * size, (h + 1) * size)
            row = jnp.sum(jnp.where(row_ids == col_ids, high[lines, :], 0.0), axis=0, keepdims=True)
            tops = jnp.where(line_ids % heads == h, row, tops)
            row = jnp.sum(
                jnp.where(row_ids == col_ids, total[lines, width:], 0.0), axis=0, keepdims=True
            )
            sums = jnp.where(line_ids % heads == h, row, sums)
        live = sums > 0.0
        level = tops * log_scale + jnp.log2(jnp.where(live, sums, 1.0))
        level = jnp.where(live, level, LOWEST)
        first = level.astype(jnp.bfloat16).astype(jnp.float32)
        second = (level - first).astype(jnp.bfloat16).astype(jnp.float32)
        third = level - first - second
        stats = jnp.where(line_ids < heads, first, jnp.where(line_ids < 2 * heads, second, third))
        result[i, wide : wide + 16, :] = stats.astype(jnp.bfloat16)
        return unused

    lax.fori_loop(0, nq * per, one_block, 0)
    backs = []
    for r in range(nq):
        backs.append(
            pltpu.make_async_copy(result.at[pl.ds(r * per, per)], out_refs[r], out_sem.at[r])
        )
    for back in backs:
        back.start()
    for send in sends:
        send.wait()
    for back in backs:
        back.wait()


def attend(meta, kv_parts, q_parts, log_scale):
    slots, size, width = kv_parts[0].shape
    heads, rows, _ = q_parts[0].shape
    nkv, nq, per = len(kv_parts), len(q_parts), rows // size
    wide = heads * size
    longest = meta[1].shape[0] // (nq * per)
    smem = pl.BlockSpec(memory_space=pltpu.SMEM)
    anywhere = pl.BlockSpec(memory_space=pl.ANY)
    parts = jax.ShapeDtypeStruct((per, wide + 16, width), jnp.bfloat16)
    moved = jax.ShapeDtypeStruct((2 * per, size, width), jnp.bfloat16)
    return pl.pallas_call(
        functools.partial(attend_kernel, log_scale, nkv, nq),
        out_shape=(parts,) * nq + (moved,) * nq,
        in_specs=[smem] * len(meta) + [anywhere] * (nkv + nq),
        out_specs=(pl.BlockSpec(memory_space=pltpu.HBM),) * (2 * nq),
        scratch_shapes=[
            pltpu.VMEM((nkv * slots, size, width), jnp.bfloat16),
            pltpu.VMEM((nq, heads, rows, width), jnp.bfloat16),
            pltpu.VMEM((longest // 2, wide, 2 * size), jnp.float32),
            pltpu.VMEM((wide, size), jnp.float32),
            pltpu.VMEM((wide, 2 * width), jnp.float32),
            pltpu.VMEM((nq * per, wide + 16, width), jnp.bfloat16),
            pltpu.SemaphoreType.DMA((nkv + nq,)),
            pltpu.SemaphoreType.DMA((nq,)),
            pltpu.SemaphoreType.DMA((2 * nq * per,)),
        ],
        compiler_params=pltpu.CompilerParams(vmem_limit_bytes=40 << 20),
        cost_estimate=pl.CostEstimate(
            flops=5_000_000_000, bytes_accessed=8_000_000, transcendentals=8_000_000
        ),
        name="attend",
    )(*meta, *kv_parts, *q_parts)


def merge_kernel(heads, *refs):
    parts = refs[:-1]
    out = refs[-1]
    per, lines, width = parts[0].shape
    size = (lines - 16) // heads
    row_ids = lax.broadcasted_iota(jnp.int32, (size, width), 0)
    col_ids = lax.broadcasted_iota(jnp.int32, (size, width), 1)
    for s in range(per):
        levels = []
        for part in parts:
            stats = part[s, heads * size :, :].astype(jnp.float32)
            levels.append(
                stats[0:heads] + stats[heads : 2 * heads] + stats[2 * heads : 3 * heads]
            )
        top = functools.reduce(jnp.maximum, levels)
        shares = [jnp.exp2(level - top) for level in levels]
        whole = functools.reduce(jnp.add, shares)
        shares = [share / whole for share in shares]
        for h in range(heads):
            mixed = jnp.zeros((size, width), jnp.float32)
            for part, share in zip(parts, shares):
                spread = jnp.where(row_ids == col_ids, share[h : h + 1, :], 0.0)
                column = jnp.sum(spread, axis=1, keepdims=True)
                mixed += column * part[s, h * size : (h + 1) * size, :].astype(jnp.float32)
            out[s * size : (s + 1) * size, h * width : (h + 1) * width] = mixed.astype(
                jnp.bfloat16
            )


def merge(parts, heads):
    per, lines, width = parts[0].shape
    size = (lines - 16) // heads
    return pl.pallas_call(
        functools.partial(merge_kernel, heads),
        out_shape=jax.ShapeDtypeStruct((per * size, heads * width), jnp.bfloat16),
        name="merge",
    )(*parts)


def refill_kernel(nq, source, ck, cv, *refs):
    moved = refs[:nq]
    new_ck, new_cv = refs[nq:]
    per = moved[0].shape[0] // 2
    old = ck.shape[0] - per
    new_ck[0:old] = ck[0:old]
    new_cv[0:old] = cv[0:old]
    for s in range(per):
        for r in range(nq):

            @pl.when(source[s] == r)
            def _():
                new_ck[old + s] = moved[r][2 * s]
                new_cv[old + s] = moved[r][2 * s + 1]


def refill(source, ck, cv, moved):
    shape = jax.ShapeDtypeStruct(ck.shape, ck.dtype)
    whole = pl.BlockSpec(memory_space=pltpu.VMEM)
    return pl.pallas_call(
        functools.partial(refill_kernel, len(moved)),
        out_shape=(shape, shape),
        in_specs=[pl.BlockSpec(memory_space=pltpu.SMEM)] + [whole] * (2 + len(moved)),
        out_specs=(whole, whole),
        name="refill",
    )(source, ck, cv, *moved)


def plan(device, per, slots, size, cache_len, span_len, block_table, window):
    old = slots - per
    c = device % NC
    z = device // NC % NZ
    y = device // (NC * NZ)
    ring = jnp.array([-k for k in SHIFTS], jnp.int32)
    q_dev = ((y + ring) % NY * NZ + z) * NC + c
    pair = jnp.arange(NC, dtype=jnp.int32)
    k_dev = ((y * NZ + (z + ring[:, None]) % NZ) * NC + (c + pair[None, :]) % NC).reshape(-1)
    slot = jnp.arange(slots, dtype=jnp.int32)
    step = jnp.arange(per, dtype=jnp.int32)
    q_ids = (q_dev[:, None] * per + step[None, :]).reshape(-1)
    q_request, q_first = block_start(q_ids, span_len, cache_len, size)
    q_window = lookup(window, q_request)
    within = jnp.tile(slot, k_dev.shape[0])
    owner = jnp.repeat(k_dev, slots)
    is_old = within < old
    o_request, o_logical, o_live = slot_owner(block_table, cache_len // size, owner * slots + within)
    n_request, n_first = block_start(
        owner * per + jnp.maximum(within - old, 0), span_len, cache_len, size
    )
    k_request = jnp.where(is_old, o_request, n_request)
    k_first = jnp.where(is_old, o_logical * size, n_first)
    live = jnp.where(is_old, o_live, True)
    last = q_first + size - 1
    seen = (
        live[None, :]
        & (q_request[:, None] == k_request[None, :])
        & (k_first[None, :] <= last[:, None])
        & (
            (k_first[None, :] < SINK)
            | (q_first[:, None] - (k_first[None, :] + size - 1) < q_window[:, None])
        )
    )
    inside = (k_first[None, :] + size - 1 <= q_first[:, None]) & (
        last[:, None] - k_first[None, :] < q_window[:, None]
    )
    total = k_first.shape[0]
    ids = jnp.arange(total, dtype=jnp.int32)
    hits = seen.astype(jnp.int32)
    rim = (seen & ~inside).astype(jnp.int32)
    count = jnp.sum(hits, axis=1)
    rims = jnp.sum(rim, axis=1)
    odd = count % 2
    before = ids[None, None, :] < ids[None, :, None]
    rim_rank = jnp.sum(jnp.where(before, rim[:, None, :], 0), axis=2)
    rank = jnp.sum(jnp.where(before, hits[:, None, :], 0), axis=2)
    rank = odd[:, None] + jnp.where(rim > 0, rim_rank, rims[:, None] + rank - rim_rank)
    at = seen[:, None, :] & (rank[:, None, :] == ids[None, :, None])
    packed = jnp.sum(jnp.where(at, (k_first * total + ids)[None, None, :] + 1, 0), axis=2)
    chosen = jnp.maximum(packed - 1, 0) % total
    first_key = jnp.where(packed > 0, jnp.maximum(packed - 1, 0) // total, FAR)
    edges = (odd + rims + 1) // 2
    targets = table_entry(block_table, n_request, n_first // size)
    wanted = (q_dev[:, None] * slots + old + step[None, :]).reshape(-1)
    hit = (targets[None, :] == wanted[:, None]) & ~is_old[None, :]
    moves = jnp.sum(jnp.where(hit, ids[None, :], 0), axis=1)
    all_new = jnp.arange(NY * NZ * NC * per, dtype=jnp.int32)
    a_request, a_first = block_start(all_new, span_len, cache_len, size)
    a_target = table_entry(block_table, a_request, a_first // size)
    mine = a_target[None, :] == (device * slots + old + step)[:, None]
    from_y = jnp.sum(jnp.where(mine, (all_new // (per * NC * NZ))[None, :], 0), axis=1)
    ahead = (from_y - y) % NY
    source = jnp.where(ahead == NY - 1, 2, jnp.where(ahead == 2, 3, ahead))
    meta = (
        count,
        chosen.reshape(-1),
        edges,
        first_key.reshape(-1),
        q_first,
        q_window,
        moves,
    )
    return meta, source


def shards(
    queries,
    new_keys,
    new_values,
    cache_keys,
    cache_values,
    out_weight,
    cache_len,
    span_len,
    block_table,
    window,
):
    device = lax.axis_index("blk")
    tokens, heads, width = queries.shape
    slots, size = cache_keys.shape[:2]
    per = tokens // size
    log_scale = math.log2(math.e) / math.sqrt(width)
    ck = cache_keys.reshape(slots, size, width)
    cv = cache_values.reshape(slots, size, width)
    own_kv = pack(
        ck, cv, new_keys.reshape(per, size, width), new_values.reshape(per, size, width)
    )
    own_q = jnp.transpose(queries, (1, 0, 2))
    lines = [own_kv] + [shift(own_kv, dz=k) for k in SHIFTS[1:]]
    q_parts = [own_q] + [shift(own_q, dy=k) for k in SHIFTS[1:]]
    kv_parts = []
    for part in lines:
        kv_parts += [part, shift(part, dc=1)]
    weight = lax.all_gather(out_weight, "blk", axis=0, tiled=True)
    meta, source = plan(device, per, slots, size, cache_len, span_len, block_table, window)
    outs = attend(meta, kv_parts, q_parts, log_scale)
    parts, moved = outs[: len(SHIFTS)], outs[len(SHIFTS) :]
    parts = [parts[0]] + [shift(p, dy=-k) for p, k in zip(parts[1:], SHIFTS[1:])]
    moved = [moved[0]] + [shift(p, dy=-k) for p, k in zip(moved[1:], SHIFTS[1:])]
    attention = merge(parts, heads)
    partial_out = lax.dot_general(
        attention, weight, (((1,), (1,)), ((), ())), preferred_element_type=jnp.float32
    ).astype(jnp.bfloat16)
    n_head = lax.axis_size("head")
    blocks = jnp.moveaxis(partial_out.reshape(tokens, n_head, -1), 1, 0)
    arrived = lax.all_to_all(blocks, "head", split_axis=0, concat_axis=0, tiled=True)
    attn_output = arrived.astype(jnp.float32).sum(axis=0).astype(jnp.bfloat16)
    new_ck, new_cv = refill(source, ck, cv, moved)
    return (
        attn_output,
        new_ck.reshape(cache_keys.shape),
        new_cv.reshape(cache_values.shape),
    )


def solution(mesh):
    placed = (
        P("blk", "head", None),
        P("blk", "head", None),
        P("blk", "head", None),
        P("blk", None, "head", None),
        P("blk", None, "head", None),
        P("blk", "head"),
        P(),
        P(),
        P(),
        P(),
    )
    return jax.shard_map(
        shards,
        mesh=mesh,
        in_specs=placed,
        out_specs=(P("blk", "head"), P("blk", None, "head", None), P("blk", None, "head", None)),
        check_vma=False,
    )
```

```python
import functools
import math

import jax
import jax.numpy as jnp
from jax import lax
from jax.experimental import pallas as pl
from jax.experimental.pallas import tpu as pltpu
from jax.sharding import PartitionSpec as P

NY, NZ, NC = 4, 4, 2
NX, NL = 4, 2
SINK = 4
LOWEST = -1e30
FLOOR = -1e25
FAR = 1 << 29
SHIFTS = (0, 1, -1, 2)


def blk_perm(dy, dz, dc):
    pairs = []
    for y in range(NY):
        for z in range(NZ):
            for c in range(NC):
                src = (y * NZ + z) * NC + c
                dst = ((y + dy) % NY * NZ + (z + dz) % NZ) * NC + (c + dc) % NC
                pairs.append((src, dst))
    return pairs


def shift(value, dy=0, dz=0, dc=0):
    return lax.ppermute(value, "blk", blk_perm(dy, dz, dc))


def head_shift(value, dx=0, dz=0):
    pairs = []
    for x in range(NX):
        for z in range(NL):
            pairs.append((x * NL + z, (x + dx) % NX * NL + (z + dz) % NL))
    return lax.ppermute(value, "head", pairs)


def ring_place(distance):
    distance = distance % len(SHIFTS)
    return jnp.where(distance == 3, 2, jnp.where(distance == 2, 3, distance))


def lookup(table_row, wanted):
    places = jnp.arange(table_row.shape[0], dtype=jnp.int32)
    return jnp.sum(jnp.where(places[None, :] == wanted[:, None], table_row[None, :], 0), axis=1)


def block_start(global_block, span_len, cache_len, block_size):
    lower = jnp.arange(span_len.shape[0], dtype=jnp.int32)
    span_end = jnp.sum(jnp.where(lower[:, None] >= lower[None, :], span_len[None, :], 0), axis=1)
    first_token = global_block * block_size
    request = jnp.sum((first_token[:, None] >= span_end[None, :]).astype(jnp.int32), axis=1)
    return (request, lookup(cache_len - span_end + span_len, request) + first_token)


def table_entry(block_table, request, logical):
    row_ids = jnp.arange(block_table.shape[0], dtype=jnp.int32)
    col_ids = jnp.arange(block_table.shape[1], dtype=jnp.int32)
    match = (row_ids[None, :, None] == request[:, None, None]) & (
        col_ids[None, None, :] == logical[:, None, None]
    )
    return jnp.sum(jnp.where(match, block_table[None], 0), axis=(1, 2))


def slot_owner(block_table, limit, slot_ids):
    row_ids = jnp.arange(block_table.shape[0], dtype=jnp.int32)
    col_ids = jnp.arange(block_table.shape[1], dtype=jnp.int32)
    match = (block_table[None] == slot_ids[:, None, None]) & (
        col_ids[None, None, :] < limit[None, :, None]
    )
    packed = row_ids[:, None] * 4096 + col_ids[None, :] + 1
    found = jnp.sum(jnp.where(match, packed[None], 0), axis=(1, 2))
    place = jnp.maximum(found - 1, 0)
    return (place // 4096, place % 4096, found > 0)


def pack_kernel(ck, cv, nk, nv, out):
    new = nk.shape[0]
    old = ck.shape[0] - new
    out[0:old] = ck[0:old]
    out[old : old + new] = nk[...]
    out[old + new : 2 * old + new] = cv[0:old]
    out[2 * old + new :] = nv[...]


def pack(ck, cv, nk, nv):
    return pl.pallas_call(
        pack_kernel,
        out_shape=jax.ShapeDtypeStruct((2 * ck.shape[0],) + ck.shape[1:], ck.dtype),
        name="pack",
    )(ck, cv, nk, nv)


def attend_kernel(
    log_scale,
    nkv,
    nq,
    count,
    chosen,
    edges,
    first_key,
    first_query,
    reach,
    moves,
    *refs,
):
    kv_in = refs[:nkv]
    q_in = refs[nkv : nkv + nq]
    out_refs = refs[nkv + nq : nkv + 2 * nq]
    move_refs = refs[nkv + 2 * nq : nkv + 3 * nq]
    kv, queries, scores, high, total, result, in_sem, out_sem, move_sem = refs[nkv + 3 * nq :]
    slots = kv_in[0].shape[0]
    half = slots // 2
    heads, rows, width = q_in[0].shape
    size = kv_in[0].shape[1]
    per = rows // size
    wide = heads * size
    longest = chosen.shape[0] // (nq * per)
    loads = []
    for a in range(nkv):
        loads.append(
            pltpu.make_async_copy(kv_in[a], kv.at[pl.ds(a * slots, slots)], in_sem.at[a])
        )
    for r in range(nq):
        loads.append(pltpu.make_async_copy(q_in[r], queries.at[r], in_sem.at[nkv + r]))
    for load in loads:
        load.start()
    for load in loads:
        load.wait()

    def place(j):
        return j // half * slots + j % half

    sends = []
    for r in range(nq):
        for s in range(per):
            at = place(moves[r * per + s])
            for side in range(2):
                sends.append(
                    pltpu.make_async_copy(
                        kv.at[at + side * half],
                        move_refs[r].at[2 * s + side],
                        move_sem.at[(r * per + s) * 2 + side],
                    )
                )
    for send in sends:
        send.start()

    row_ids = lax.broadcasted_iota(jnp.int32, (size, width), 0)
    col_ids = lax.broadcasted_iota(jnp.int32, (size, width), 1)
    ones = jnp.ones((2 * size, width), jnp.bfloat16)

    def one_block(i, unused):
        r = i // per
        s = i % per
        begin = pl.multiple_of(s * size, size)
        query = jnp.concatenate(
            [queries[r, h, pl.ds(begin, size), :] for h in range(heads)], axis=0
        )
        pairs = (count[i] + 1) // 2
        high[...] = jnp.full_like(high, LOWEST)

        def raw_scores(t):
            at = i * longest + 2 * t
            keys = jnp.concatenate([kv[place(chosen[at])], kv[place(chosen[at + 1])]], axis=0)
            return lax.dot_general(
                query, keys, (((1,), (1,)), ((), ())), preferred_element_type=jnp.float32
            )

        def score_edge(t, unused):
            raw = raw_scores(t)
            for side in range(2):
                key_pos = first_key[i * longest + 2 * t + side] + col_ids
                distance = first_query[i] + row_ids - key_pos
                allowed = (distance >= 0) & ((distance < reach[i]) | (key_pos < SINK))
                hidden = jnp.where(allowed, 0.0, LOWEST)
                for h in range(heads):
                    lines = slice(h * size, (h + 1) * size)
                    part = raw[lines, side * size : (side + 1) * size]
                    part = jnp.where(hidden < 0.0, LOWEST, part)
                    scores[t, lines, side * size : (side + 1) * size] = part
                    high[lines, :] = jnp.maximum(high[lines, :], part)
            return unused

        def score_full(t, unused):
            raw = raw_scores(t)
            scores[t] = raw
            high[...] = jnp.maximum(high[...], jnp.maximum(raw[:, :size], raw[:, size:]))
            return unused

        lax.fori_loop(0, edges[i], score_edge, 0)
        lax.fori_loop(edges[i], pairs, score_full, 0)
        top = jnp.maximum(jnp.max(high[...], axis=1, keepdims=True), FLOOR)
        high[...] = jnp.broadcast_to(top, high.shape)
        total[...] = jnp.zeros_like(total)

        def blend(t, unused):
            at = i * longest + 2 * t
            values = jnp.concatenate(
                [kv[place(chosen[at]) + half], kv[place(chosen[at + 1]) + half]], axis=0
            )
            values = jnp.concatenate([values, ones], axis=1)
            level = high[...]
            level = jnp.concatenate([level, level], axis=1)
            weights = jnp.exp2((scores[t] - level) * log_scale).astype(jnp.bfloat16)
            total[...] += jnp.dot(weights, values, preferred_element_type=jnp.float32)
            return unused

        lax.fori_loop(0, pairs, blend, 0)
        summed = total[:, width:]
        safe = jnp.where(summed > 0.0, summed, 1.0)
        result[i, 0:wide, :] = (total[:, :width] / safe).astype(jnp.bfloat16)
        line_ids = lax.broadcasted_iota(jnp.int32, (16, width), 0)
        tops = jnp.zeros((16, width), jnp.float32)
        sums = jnp.zeros((16, width), jnp.float32)
        for h in range(heads):
            lines = slice(h * size, (h + 1) * size)
            row = jnp.sum(jnp.where(row_ids == col_ids, high[lines, :], 0.0), axis=0, keepdims=True)
            tops = jnp.where(line_ids % heads == h, row, tops)
            row = jnp.sum(
                jnp.where(row_ids == col_ids, total[lines, width:], 0.0), axis=0, keepdims=True
            )
            sums = jnp.where(line_ids % heads == h, row, sums)
        live = sums > 0.0
        level = tops * log_scale + jnp.log2(jnp.where(live, sums, 1.0))
        level = jnp.where(live, level, LOWEST)
        first = level.astype(jnp.bfloat16).astype(jnp.float32)
        second = (level - first).astype(jnp.bfloat16).astype(jnp.float32)
        third = level - first - second
        stats = jnp.where(line_ids < heads, first, jnp.where(line_ids < 2 * heads, second, third))
        result[i, wide : wide + 16, :] = stats.astype(jnp.bfloat16)
        return unused

    lax.fori_loop(0, nq * per, one_block, 0)
    backs = []
    for r in range(nq):
        backs.append(
            pltpu.make_async_copy(result.at[pl.ds(r * per, per)], out_refs[r], out_sem.at[r])
        )
    for back in backs:
        back.start()
    for send in sends:
        send.wait()
    for back in backs:
        back.wait()


def attend(meta, kv_parts, q_parts, log_scale):
    slots, size, width = kv_parts[0].shape
    heads, rows, _ = q_parts[0].shape
    nkv, nq, per = len(kv_parts), len(q_parts), rows // size
    wide = heads * size
    longest = meta[1].shape[0] // (nq * per)
    smem = pl.BlockSpec(memory_space=pltpu.SMEM)
    anywhere = pl.BlockSpec(memory_space=pl.ANY)
    parts = jax.ShapeDtypeStruct((per, wide + 16, width), jnp.bfloat16)
    moved = jax.ShapeDtypeStruct((2 * per, size, width), jnp.bfloat16)
    return pl.pallas_call(
        functools.partial(attend_kernel, log_scale, nkv, nq),
        out_shape=(parts,) * nq + (moved,) * nq,
        in_specs=[smem] * len(meta) + [anywhere] * (nkv + nq),
        out_specs=(anywhere,) * (2 * nq),
        scratch_shapes=[
            pltpu.VMEM((nkv * slots, size, width), jnp.bfloat16),
            pltpu.VMEM((nq, heads, rows, width), jnp.bfloat16),
            pltpu.VMEM((longest // 2, wide, 2 * size), jnp.float32),
            pltpu.VMEM((wide, size), jnp.float32),
            pltpu.VMEM((wide, 2 * width), jnp.float32),
            pltpu.VMEM((nq * per, wide + 16, width), jnp.bfloat16),
            pltpu.SemaphoreType.DMA((nkv + nq,)),
            pltpu.SemaphoreType.DMA((nq,)),
            pltpu.SemaphoreType.DMA((2 * nq * per,)),
        ],
        compiler_params=pltpu.CompilerParams(vmem_limit_bytes=56 << 20),
        cost_estimate=pl.CostEstimate(
            flops=5_000_000_000, bytes_accessed=8_000_000, transcendentals=8_000_000
        ),
        name="attend",
    )(*meta, *kv_parts, *q_parts)


def finish_kernel(heads, nparts, nw, pieces, *refs):
    part_in = refs[:nparts]
    w_in = refs[nparts : nparts + nw]
    first_out = refs[nparts + nw : nparts + nw + NX]
    second_out = refs[nparts + nw + NX : nparts + nw + NX + NL]
    parts, weight, mixed_rows, first, second, part_sem, w_sem, a_sem, b_sem = refs[
        nparts + nw + NX + NL :
    ]
    group = w_in[0].shape[0]
    per, lines, width = part_in[0].shape
    size = (lines - 16) // heads
    part_loads = [
        pltpu.make_async_copy(part_in[r], parts.at[r], part_sem.at[r]) for r in range(nparts)
    ]
    w_loads = [
        pltpu.make_async_copy(w_in[a], weight.at[pl.ds(a * group, group)], w_sem.at[a])
        for a in range(nw)
    ]
    for load in part_loads + w_loads:
        load.start()
    for load in part_loads:
        load.wait()
    row_ids = lax.broadcasted_iota(jnp.int32, (size, width), 0)
    col_ids = lax.broadcasted_iota(jnp.int32, (size, width), 1)
    for s in range(per):
        levels = []
        for r in range(nparts):
            stats = parts[r, s, heads * size :, :].astype(jnp.float32)
            levels.append(
                stats[0:heads] + stats[heads : 2 * heads] + stats[2 * heads : 3 * heads]
            )
        top = functools.reduce(jnp.maximum, levels)
        shares = [jnp.exp2(level - top) for level in levels]
        whole = functools.reduce(jnp.add, shares)
        shares = [share / whole for share in shares]
        for h in range(heads):
            mixed = jnp.zeros((size, width), jnp.float32)
            for r in range(nparts):
                spread = jnp.where(row_ids == col_ids, shares[r][h : h + 1, :], 0.0)
                column = jnp.sum(spread, axis=1, keepdims=True)
                mixed += column * parts[r, s, h * size : (h + 1) * size, :].astype(jnp.float32)
            mixed_rows[s * size : (s + 1) * size, h * width : (h + 1) * width] = mixed.astype(
                jnp.bfloat16
            )
    for load in w_loads:
        load.wait()
    sends = []
    for r in reversed(range(NX)):
        for z in range(NL):
            at = (r * NL + z) * group
            rows = jnp.concatenate([weight[pieces[at + q]] for q in range(group)], axis=0)
            product = lax.dot_general(
                mixed_rows[...], rows, (((1,), (1,)), ((), ())), preferred_element_type=jnp.float32
            ).astype(jnp.bfloat16)
            first[r, z] = product[:size]
            second[z, r] = product[size:]
        sends.append(pltpu.make_async_copy(first.at[r], first_out[r], a_sem.at[r]))
        sends[-1].start()
    for z in range(NL):
        sends.append(pltpu.make_async_copy(second.at[z], second_out[z], b_sem.at[z]))
        sends[-1].start()
    for send in sends:
        send.wait()


def finish(pieces, parts, w_parts, heads):
    per, lines, width = parts[0].shape
    size = (lines - 16) // heads
    group, rows, depth = w_parts[0].shape
    columns = group * rows
    nparts, nw = len(parts), len(w_parts)
    anywhere = pl.BlockSpec(memory_space=pl.ANY)
    first = jax.ShapeDtypeStruct((NL, size, columns), jnp.bfloat16)
    second = jax.ShapeDtypeStruct((NX, size, columns), jnp.bfloat16)
    return pl.pallas_call(
        functools.partial(finish_kernel, heads, nparts, nw),
        out_shape=(first,) * NX + (second,) * NL,
        in_specs=[pl.BlockSpec(memory_space=pltpu.SMEM)] + [anywhere] * (nparts + nw),
        out_specs=(anywhere,) * (NX + NL),
        scratch_shapes=[
            pltpu.VMEM((nparts, per, lines, width), jnp.bfloat16),
            pltpu.VMEM((nw * group, rows, depth), jnp.bfloat16),
            pltpu.VMEM((per * size, heads * width), jnp.bfloat16),
            pltpu.VMEM((NX, NL, size, columns), jnp.bfloat16),
            pltpu.VMEM((NL, NX, size, columns), jnp.bfloat16),
            pltpu.SemaphoreType.DMA((nparts,)),
            pltpu.SemaphoreType.DMA((nw,)),
            pltpu.SemaphoreType.DMA((NX,)),
            pltpu.SemaphoreType.DMA((NL,)),
        ],
        compiler_params=pltpu.CompilerParams(vmem_limit_bytes=24 << 20),
        cost_estimate=pl.CostEstimate(
            flops=2_000_000_000, bytes_accessed=12_000_000, transcendentals=10_000
        ),
        name="finish",
    )(pieces, *parts, *w_parts)


def piece_table(device, head, group):
    c = device % NC
    z = device // NC % NZ
    y = device // (NC * NZ)
    steps = jnp.array(SHIFTS, jnp.int32)
    target = (head // NL + steps[:, None]) % NX * NL + (head + jnp.arange(NL)[None, :]) % NL
    owner = (target.reshape(-1)[:, None] * group + jnp.arange(group)[None, :]).reshape(-1)
    place = ring_place(y - owner // (NC * NZ)) * NC + (c + owner) % NC
    return (place * NZ + ring_place(z - owner // NC % NZ)).astype(jnp.int32)


def refill_kernel(nq, source, ck, cv, *refs):
    moved_in = refs[:nq]
    new_ck, new_cv, moved, sem = refs[nq:]
    per = moved_in[0].shape[0] // 2
    old = ck.shape[0] - per
    loads = [pltpu.make_async_copy(moved_in[r], moved.at[r], sem.at[r]) for r in range(nq)]
    for load in loads:
        load.start()
    new_ck[0:old] = ck[0:old]
    new_cv[0:old] = cv[0:old]
    for load in loads:
        load.wait()
    for s in range(per):
        new_ck[old + s] = moved[source[s], 2 * s]
        new_cv[old + s] = moved[source[s], 2 * s + 1]


def refill(source, ck, cv, moved):
    shape = jax.ShapeDtypeStruct(ck.shape, ck.dtype)
    whole = pl.BlockSpec(memory_space=pltpu.VMEM)
    anywhere = pl.BlockSpec(memory_space=pl.ANY)
    nq = len(moved)
    return pl.pallas_call(
        functools.partial(refill_kernel, nq),
        out_shape=(shape, shape),
        in_specs=[pl.BlockSpec(memory_space=pltpu.SMEM)] + [whole] * 2 + [anywhere] * nq,
        out_specs=(whole, whole),
        scratch_shapes=[
            pltpu.VMEM((nq,) + moved[0].shape, moved[0].dtype),
            pltpu.SemaphoreType.DMA((nq,)),
        ],
        name="refill",
    )(source, ck, cv, *moved)


def plan(device, per, slots, size, cache_len, span_len, block_table, window):
    old = slots - per
    c = device % NC
    z = device // NC % NZ
    y = device // (NC * NZ)
    ring = jnp.array([-k for k in SHIFTS], jnp.int32)
    q_dev = ((y + ring) % NY * NZ + z) * NC + c
    pair = jnp.arange(NC, dtype=jnp.int32)
    k_dev = ((y * NZ + (z + ring[:, None]) % NZ) * NC + (c + pair[None, :]) % NC).reshape(-1)
    slot = jnp.arange(slots, dtype=jnp.int32)
    step = jnp.arange(per, dtype=jnp.int32)
    q_ids = (q_dev[:, None] * per + step[None, :]).reshape(-1)
    q_request, q_first = block_start(q_ids, span_len, cache_len, size)
    q_window = lookup(window, q_request)
    within = jnp.tile(slot, k_dev.shape[0])
    owner = jnp.repeat(k_dev, slots)
    is_old = within < old
    o_request, o_logical, o_live = slot_owner(block_table, cache_len // size, owner * slots + within)
    n_request, n_first = block_start(
        owner * per + jnp.maximum(within - old, 0), span_len, cache_len, size
    )
    k_request = jnp.where(is_old, o_request, n_request)
    k_first = jnp.where(is_old, o_logical * size, n_first)
    live = jnp.where(is_old, o_live, True)
    last = q_first + size - 1
    seen = (
        live[None, :]
        & (q_request[:, None] == k_request[None, :])
        & (k_first[None, :] <= last[:, None])
        & (
            (k_first[None, :] < SINK)
            | (q_first[:, None] - (k_first[None, :] + size - 1) < q_window[:, None])
        )
    )
    inside = (k_first[None, :] + size - 1 <= q_first[:, None]) & (
        last[:, None] - k_first[None, :] < q_window[:, None]
    )
    total = k_first.shape[0]
    ids = jnp.arange(total, dtype=jnp.int32)
    hits = seen.astype(jnp.int32)
    rim = (seen & ~inside).astype(jnp.int32)
    count = jnp.sum(hits, axis=1)
    rims = jnp.sum(rim, axis=1)
    odd = count % 2
    before = ids[None, None, :] < ids[None, :, None]
    rim_rank = jnp.sum(jnp.where(before, rim[:, None, :], 0), axis=2)
    rank = jnp.sum(jnp.where(before, hits[:, None, :], 0), axis=2)
    rank = odd[:, None] + jnp.where(rim > 0, rim_rank, rims[:, None] + rank - rim_rank)
    at = seen[:, None, :] & (rank[:, None, :] == ids[None, :, None])
    packed = jnp.sum(jnp.where(at, (k_first * total + ids)[None, None, :] + 1, 0), axis=2)
    chosen = jnp.maximum(packed - 1, 0) % total
    first_key = jnp.where(packed > 0, jnp.maximum(packed - 1, 0) // total, FAR)
    edges = (odd + rims + 1) // 2
    targets = table_entry(block_table, n_request, n_first // size)
    wanted = (q_dev[:, None] * slots + old + step[None, :]).reshape(-1)
    hit = (targets[None, :] == wanted[:, None]) & ~is_old[None, :]
    moves = jnp.sum(jnp.where(hit, ids[None, :], 0), axis=1)
    all_new = jnp.arange(NY * NZ * NC * per, dtype=jnp.int32)
    a_request, a_first = block_start(all_new, span_len, cache_len, size)
    a_target = table_entry(block_table, a_request, a_first // size)
    mine = a_target[None, :] == (device * slots + old + step)[:, None]
    from_y = jnp.sum(jnp.where(mine, (all_new // (per * NC * NZ))[None, :], 0), axis=1)
    source = ring_place(from_y - y)
    meta = (
        count,
        chosen.reshape(-1),
        edges,
        first_key.reshape(-1),
        q_first,
        q_window,
        moves,
    )
    return meta, source


def shards(
    queries,
    new_keys,
    new_values,
    cache_keys,
    cache_values,
    out_weight,
    cache_len,
    span_len,
    block_table,
    window,
):
    device = lax.axis_index("blk")
    head = lax.axis_index("head")
    tokens, heads, width = queries.shape
    slots, size = cache_keys.shape[:2]
    per = tokens // size
    log_scale = math.log2(math.e) / math.sqrt(width)
    ck = cache_keys.reshape(slots, size, width)
    cv = cache_values.reshape(slots, size, width)
    own_q = jnp.transpose(queries, (1, 0, 2))
    w_line = [out_weight] + [shift(out_weight, dz=k) for k in SHIFTS[1:]]
    own_kv = pack(
        ck, cv, new_keys.reshape(per, size, width), new_values.reshape(per, size, width)
    )
    lines = [own_kv] + [shift(own_kv, dz=k) for k in SHIFTS[1:]]
    q_parts = [own_q] + [shift(own_q, dy=k) for k in SHIFTS[1:]]
    kv_parts = []
    for part in lines:
        kv_parts += [part, shift(part, dc=1)]
    w_four = jnp.stack(w_line)
    w_far = [shift(w_four, dy=k) for k in SHIFTS[1:]]
    w_parts = [w_four, shift(w_four, dc=1)]
    meta, source = plan(device, per, slots, size, cache_len, span_len, block_table, window)
    outs = attend(meta, kv_parts, q_parts, log_scale)
    parts, moved = outs[: len(SHIFTS)], outs[len(SHIFTS) :]
    for part in lax.optimization_barrier((*w_far, parts[0]))[:-1]:
        w_parts += [part, shift(part, dc=1)]
    parts = [parts[0]] + [shift(p, dy=-k) for p, k in zip(parts[1:], SHIFTS[1:])]
    moved = [moved[0]] + [shift(p, dy=-k) for p, k in zip(moved[1:], SHIFTS[1:])]
    pieces = piece_table(device, head, heads * width // out_weight.shape[0])
    shares = finish(pieces, parts, w_parts, heads)
    first, second = shares[:NX], shares[NX:]
    first = [first[0]] + [head_shift(p, dx=k) for p, k in zip(first[1:], SHIFTS[1:])]
    second_sum = second[0].astype(jnp.float32) + head_shift(second[1], dz=1).astype(jnp.float32)
    first_sum = functools.reduce(jnp.add, [p.astype(jnp.float32) for p in first])
    second_out = second_sum[0]
    for r in range(1, NX):
        second_out += head_shift(second_sum[r].astype(jnp.bfloat16), dx=SHIFTS[r]).astype(
            jnp.float32
        )
    first_out = first_sum[0] + head_shift(first_sum[1].astype(jnp.bfloat16), dz=1).astype(
        jnp.float32
    )
    attn_output = jnp.concatenate([first_out, second_out], axis=0).astype(jnp.bfloat16)
    new_ck, new_cv = refill(source, ck, cv, moved)
    return (
        attn_output,
        new_ck.reshape(cache_keys.shape),
        new_cv.reshape(cache_values.shape),
    )


def solution(mesh):
    placed = (
        P("blk", "head", None),
        P("blk", "head", None),
        P("blk", "head", None),
        P("blk", None, "head", None),
        P("blk", None, "head", None),
        P("blk", "head"),
        P(),
        P(),
        P(),
        P(),
    )
    return jax.shard_map(
        shards,
        mesh=mesh,
        in_specs=placed,
        out_specs=(P("blk", "head"), P("blk", None, "head", None), P("blk", None, "head", None)),
        check_vma=False,
    )
```

```python
import functools
import math

import jax
import jax.numpy as jnp
from jax import lax
from jax.experimental import pallas as pl
from jax.experimental.pallas import tpu as pltpu
from jax.sharding import PartitionSpec as P

NY, NZ, NC = 4, 4, 2
NX, NL = 4, 2
SINK = 4
LOWEST = -1e30
FLOOR = -1e25
FAR = 1 << 29
SHIFTS = (0, 1, -1, 2)


def blk_perm(dy, dz, dc):
    pairs = []
    for y in range(NY):
        for z in range(NZ):
            for c in range(NC):
                src = (y * NZ + z) * NC + c
                dst = ((y + dy) % NY * NZ + (z + dz) % NZ) * NC + (c + dc) % NC
                pairs.append((src, dst))
    return pairs


def shift(value, dy=0, dz=0, dc=0):
    return lax.ppermute(value, "blk", blk_perm(dy, dz, dc))


def after(value, *earlier):
    return lax.optimization_barrier((value, *earlier))[0]


def in_hbm(value):
    return pltpu.with_memory_space_constraint(value, pltpu.HBM)


def head_shift(value, dx=0, dz=0):
    pairs = []
    for x in range(NX):
        for z in range(NL):
            pairs.append((x * NL + z, (x + dx) % NX * NL + (z + dz) % NL))
    return lax.ppermute(value, "head", pairs)


def ring_place(distance):
    distance = distance % len(SHIFTS)
    return jnp.where(distance == 3, 2, jnp.where(distance == 2, 3, distance))


def lookup(table_row, wanted):
    places = jnp.arange(table_row.shape[0], dtype=jnp.int32)
    return jnp.sum(jnp.where(places[None, :] == wanted[:, None], table_row[None, :], 0), axis=1)


def block_start(global_block, span_len, cache_len, block_size):
    lower = jnp.arange(span_len.shape[0], dtype=jnp.int32)
    span_end = jnp.sum(jnp.where(lower[:, None] >= lower[None, :], span_len[None, :], 0), axis=1)
    first_token = global_block * block_size
    request = jnp.sum((first_token[:, None] >= span_end[None, :]).astype(jnp.int32), axis=1)
    return (request, lookup(cache_len - span_end + span_len, request) + first_token)


def table_entry(block_table, request, logical):
    row_ids = jnp.arange(block_table.shape[0], dtype=jnp.int32)
    col_ids = jnp.arange(block_table.shape[1], dtype=jnp.int32)
    match = (row_ids[None, :, None] == request[:, None, None]) & (
        col_ids[None, None, :] == logical[:, None, None]
    )
    return jnp.sum(jnp.where(match, block_table[None], 0), axis=(1, 2))


def slot_owner(block_table, limit, slot_ids):
    row_ids = jnp.arange(block_table.shape[0], dtype=jnp.int32)
    col_ids = jnp.arange(block_table.shape[1], dtype=jnp.int32)
    match = (block_table[None] == slot_ids[:, None, None]) & (
        col_ids[None, None, :] < limit[None, :, None]
    )
    packed = row_ids[:, None] * 4096 + col_ids[None, :] + 1
    found = jnp.sum(jnp.where(match, packed[None], 0), axis=(1, 2))
    place = jnp.maximum(found - 1, 0)
    return (place // 4096, place % 4096, found > 0)


def pack_kernel(ck, cv, nk, nv, out):
    new = nk.shape[0]
    old = ck.shape[0] - new
    out[0:old] = ck[0:old]
    out[old : old + new] = nk[...]
    out[old + new : 2 * old + new] = cv[0:old]
    out[2 * old + new :] = nv[...]


def pack(ck, cv, nk, nv):
    return pl.pallas_call(
        pack_kernel,
        out_shape=jax.ShapeDtypeStruct((2 * ck.shape[0],) + ck.shape[1:], ck.dtype),
        name="pack",
    )(ck, cv, nk, nv)


def attend_kernel(
    log_scale,
    nkv,
    nq,
    count,
    chosen,
    edges,
    first_key,
    first_query,
    reach,
    moves,
    *refs,
):
    kv_in = refs[:nkv]
    q_in = refs[nkv : nkv + nq]
    out_refs = refs[nkv + nq : nkv + 2 * nq]
    move_refs = refs[nkv + 2 * nq : nkv + 3 * nq]
    kv, queries, scores, high, total, result, in_sem, out_sem, move_sem = refs[nkv + 3 * nq :]
    slots = kv_in[0].shape[0]
    half = slots // 2
    begins = [sum(ref.shape[0] for ref in kv_in[:a]) for a in range(nkv)]
    heads, rows, width = q_in[0].shape
    size = kv_in[0].shape[1]
    per = rows // size
    wide = heads * size
    longest = chosen.shape[0] // (nq * per)
    loads = []
    for a in range(nkv):
        loads.append(
            pltpu.make_async_copy(
                kv_in[a], kv.at[pl.ds(begins[a], kv_in[a].shape[0])], in_sem.at[a]
            )
        )
    for r in range(nq):
        loads.append(pltpu.make_async_copy(q_in[r], queries.at[r], in_sem.at[nkv + r]))
    for load in loads:
        load.start()
    for load in loads:
        load.wait()

    def place(j):
        return j // half * slots + j % half

    sends = []
    for r in range(nq):
        for s in range(per):
            at = place(moves[r * per + s])
            for side in range(2):
                sends.append(
                    pltpu.make_async_copy(
                        kv.at[at + side * half],
                        move_refs[r].at[2 * s + side],
                        move_sem.at[(r * per + s) * 2 + side],
                    )
                )
    for send in sends:
        send.start()

    row_ids = lax.broadcasted_iota(jnp.int32, (size, width), 0)
    col_ids = lax.broadcasted_iota(jnp.int32, (size, width), 1)
    ones = jnp.ones((2 * size, width), jnp.bfloat16)

    def one_block(i, unused):
        r = i // per
        s = i % per
        begin = pl.multiple_of(s * size, size)
        query = jnp.concatenate(
            [queries[r, h, pl.ds(begin, size), :] for h in range(heads)], axis=0
        )
        pairs = (count[i] + 1) // 2
        high[...] = jnp.full_like(high, LOWEST)

        def raw_scores(t):
            at = i * longest + 2 * t
            keys = jnp.concatenate([kv[place(chosen[at])], kv[place(chosen[at + 1])]], axis=0)
            return lax.dot_general(
                query, keys, (((1,), (1,)), ((), ())), preferred_element_type=jnp.float32
            )

        def score_edge(t, unused):
            raw = raw_scores(t)
            for side in range(2):
                key_pos = first_key[i * longest + 2 * t + side] + col_ids
                distance = first_query[i] + row_ids - key_pos
                allowed = (distance >= 0) & ((distance < reach[i]) | (key_pos < SINK))
                hidden = jnp.where(allowed, 0.0, LOWEST)
                for h in range(heads):
                    lines = slice(h * size, (h + 1) * size)
                    part = raw[lines, side * size : (side + 1) * size]
                    part = jnp.where(hidden < 0.0, LOWEST, part)
                    scores[t, lines, side * size : (side + 1) * size] = part
                    high[lines, :] = jnp.maximum(high[lines, :], part)
            return unused

        def score_full(t, unused):
            raw = raw_scores(t)
            scores[t] = raw
            high[...] = jnp.maximum(high[...], jnp.maximum(raw[:, :size], raw[:, size:]))
            return unused

        lax.fori_loop(0, edges[i], score_edge, 0)
        lax.fori_loop(edges[i], pairs, score_full, 0)
        top = jnp.maximum(jnp.max(high[...], axis=1, keepdims=True), FLOOR)
        high[...] = jnp.broadcast_to(top, high.shape)
        total[...] = jnp.zeros_like(total)

        def blend(t, unused):
            at = i * longest + 2 * t
            values = jnp.concatenate(
                [kv[place(chosen[at]) + half], kv[place(chosen[at + 1]) + half]], axis=0
            )
            values = jnp.concatenate([values, ones], axis=1)
            level = high[...]
            level = jnp.concatenate([level, level], axis=1)
            weights = jnp.exp2((scores[t] - level) * log_scale).astype(jnp.bfloat16)
            total[...] += jnp.dot(weights, values, preferred_element_type=jnp.float32)
            return unused

        lax.fori_loop(0, pairs, blend, 0)
        summed = total[:, width:]
        safe = jnp.where(summed > 0.0, summed, 1.0)
        result[i, 0:wide, :] = (total[:, :width] / safe).astype(jnp.bfloat16)
        line_ids = lax.broadcasted_iota(jnp.int32, (16, width), 0)
        tops = jnp.zeros((16, width), jnp.float32)
        sums = jnp.zeros((16, width), jnp.float32)
        for h in range(heads):
            lines = slice(h * size, (h + 1) * size)
            row = jnp.sum(jnp.where(row_ids == col_ids, high[lines, :], 0.0), axis=0, keepdims=True)
            tops = jnp.where(line_ids % heads == h, row, tops)
            row = jnp.sum(
                jnp.where(row_ids == col_ids, total[lines, width:], 0.0), axis=0, keepdims=True
            )
            sums = jnp.where(line_ids % heads == h, row, sums)
        live = sums > 0.0
        level = tops * log_scale + jnp.log2(jnp.where(live, sums, 1.0))
        level = jnp.where(live, level, LOWEST)
        first = level.astype(jnp.bfloat16).astype(jnp.float32)
        second = (level - first).astype(jnp.bfloat16).astype(jnp.float32)
        third = level - first - second
        stats = jnp.where(line_ids < heads, first, jnp.where(line_ids < 2 * heads, second, third))
        result[i, wide : wide + 16, :] = stats.astype(jnp.bfloat16)
        return unused

    lax.fori_loop(0, nq * per, one_block, 0)
    backs = []
    for r in range(nq):
        backs.append(
            pltpu.make_async_copy(result.at[pl.ds(r * per, per)], out_refs[r], out_sem.at[r])
        )
    for back in backs:
        back.start()
    for send in sends:
        send.wait()
    for back in backs:
        back.wait()


def attend(meta, kv_parts, q_parts, log_scale):
    _, size, width = kv_parts[0].shape
    heads, rows, _ = q_parts[0].shape
    nkv, nq, per = len(kv_parts), len(q_parts), rows // size
    wide = heads * size
    longest = meta[1].shape[0] // (nq * per)
    smem = pl.BlockSpec(memory_space=pltpu.SMEM)
    anywhere = pl.BlockSpec(memory_space=pl.ANY)
    parts = jax.ShapeDtypeStruct((per, wide + 16, width), jnp.bfloat16)
    moved = jax.ShapeDtypeStruct((2 * per, size, width), jnp.bfloat16)
    return pl.pallas_call(
        functools.partial(attend_kernel, log_scale, nkv, nq),
        out_shape=(parts,) * nq + (moved,) * nq,
        in_specs=[smem] * len(meta) + [anywhere] * (nkv + nq),
        out_specs=(anywhere,) * (2 * nq),
        scratch_shapes=[
            pltpu.VMEM((sum(p.shape[0] for p in kv_parts), size, width), jnp.bfloat16),
            pltpu.VMEM((nq, heads, rows, width), jnp.bfloat16),
            pltpu.VMEM((longest // 2, wide, 2 * size), jnp.float32),
            pltpu.VMEM((wide, size), jnp.float32),
            pltpu.VMEM((wide, 2 * width), jnp.float32),
            pltpu.VMEM((nq * per, wide + 16, width), jnp.bfloat16),
            pltpu.SemaphoreType.DMA((nkv + nq,)),
            pltpu.SemaphoreType.DMA((nq,)),
            pltpu.SemaphoreType.DMA((2 * nq * per,)),
        ],
        compiler_params=pltpu.CompilerParams(vmem_limit_bytes=56 << 20),
        cost_estimate=pl.CostEstimate(
            flops=5_000_000_000, bytes_accessed=8_000_000, transcendentals=8_000_000
        ),
        name="attend",
    )(*meta, *kv_parts, *q_parts)


def finish_kernel(heads, nparts, nw, pieces, *refs):
    part_in = refs[:nparts]
    w_in = refs[nparts : nparts + nw]
    first_out = refs[nparts + nw : nparts + nw + NX]
    second_out = refs[nparts + nw + NX : nparts + nw + NX + NL]
    parts, weight, mixed_rows, first, second, part_sem, w_sem, a_sem, b_sem = refs[
        nparts + nw + NX + NL :
    ]
    group = w_in[0].shape[0]
    per, lines, width = part_in[0].shape
    size = (lines - 16) // heads
    part_loads = [
        pltpu.make_async_copy(part_in[r], parts.at[r], part_sem.at[r]) for r in range(nparts)
    ]
    w_loads = [
        pltpu.make_async_copy(w_in[a], weight.at[pl.ds(a * group, group)], w_sem.at[a])
        for a in range(nw)
    ]
    for load in part_loads + w_loads:
        load.start()
    for load in part_loads:
        load.wait()
    row_ids = lax.broadcasted_iota(jnp.int32, (size, width), 0)
    col_ids = lax.broadcasted_iota(jnp.int32, (size, width), 1)
    for s in range(per):
        levels = []
        for r in range(nparts):
            stats = parts[r, s, heads * size :, :].astype(jnp.float32)
            levels.append(
                stats[0:heads] + stats[heads : 2 * heads] + stats[2 * heads : 3 * heads]
            )
        top = functools.reduce(jnp.maximum, levels)
        shares = [jnp.exp2(level - top) for level in levels]
        whole = functools.reduce(jnp.add, shares)
        shares = [share / whole for share in shares]
        for h in range(heads):
            mixed = jnp.zeros((size, width), jnp.float32)
            for r in range(nparts):
                spread = jnp.where(row_ids == col_ids, shares[r][h : h + 1, :], 0.0)
                column = jnp.sum(spread, axis=1, keepdims=True)
                mixed += column * parts[r, s, h * size : (h + 1) * size, :].astype(jnp.float32)
            mixed_rows[s * size : (s + 1) * size, h * width : (h + 1) * width] = mixed.astype(
                jnp.bfloat16
            )
    for load in w_loads:
        load.wait()
    sends = []
    for r in reversed(range(NX)):
        for z in range(NL):
            at = (r * NL + z) * group
            rows = jnp.concatenate([weight[pieces[at + q]] for q in range(group)], axis=0)
            product = lax.dot_general(
                mixed_rows[...], rows, (((1,), (1,)), ((), ())), preferred_element_type=jnp.float32
            ).astype(jnp.bfloat16)
            first[r, z] = product[:size]
            second[z, r] = product[size:]
        sends.append(pltpu.make_async_copy(first.at[r], first_out[r], a_sem.at[r]))
        sends[-1].start()
    for z in range(NL):
        sends.append(pltpu.make_async_copy(second.at[z], second_out[z], b_sem.at[z]))
        sends[-1].start()
    for send in sends:
        send.wait()


def finish(pieces, parts, w_parts, heads):
    per, lines, width = parts[0].shape
    size = (lines - 16) // heads
    group, rows, depth = w_parts[0].shape
    columns = group * rows
    nparts, nw = len(parts), len(w_parts)
    anywhere = pl.BlockSpec(memory_space=pl.ANY)
    first = jax.ShapeDtypeStruct((NL, size, columns), jnp.bfloat16)
    second = jax.ShapeDtypeStruct((NX, size, columns), jnp.bfloat16)
    return pl.pallas_call(
        functools.partial(finish_kernel, heads, nparts, nw),
        out_shape=(first,) * NX + (second,) * NL,
        in_specs=[pl.BlockSpec(memory_space=pltpu.SMEM)] + [anywhere] * (nparts + nw),
        out_specs=(anywhere,) * (NX + NL),
        scratch_shapes=[
            pltpu.VMEM((nparts, per, lines, width), jnp.bfloat16),
            pltpu.VMEM((nw * group, rows, depth), jnp.bfloat16),
            pltpu.VMEM((per * size, heads * width), jnp.bfloat16),
            pltpu.VMEM((NX, NL, size, columns), jnp.bfloat16),
            pltpu.VMEM((NL, NX, size, columns), jnp.bfloat16),
            pltpu.SemaphoreType.DMA((nparts,)),
            pltpu.SemaphoreType.DMA((nw,)),
            pltpu.SemaphoreType.DMA((NX,)),
            pltpu.SemaphoreType.DMA((NL,)),
        ],
        compiler_params=pltpu.CompilerParams(vmem_limit_bytes=24 << 20),
        cost_estimate=pl.CostEstimate(
            flops=2_000_000_000, bytes_accessed=12_000_000, transcendentals=10_000
        ),
        name="finish",
    )(pieces, *parts, *w_parts)


def piece_table(device, head, group):
    c = device % NC
    z = device // NC % NZ
    y = device // (NC * NZ)
    steps = jnp.array(SHIFTS, jnp.int32)
    target = (head // NL + steps[:, None]) % NX * NL + (head + jnp.arange(NL)[None, :]) % NL
    owner = (target.reshape(-1)[:, None] * group + jnp.arange(group)[None, :]).reshape(-1)
    place = ring_place(y - owner // (NC * NZ)) * NC + (c + owner) % NC
    return (place * NZ + ring_place(z - owner // NC % NZ)).astype(jnp.int32)


def refill_kernel(nq, source, ck, cv, *refs):
    moved_in = refs[:nq]
    new_ck, new_cv, moved, sem = refs[nq:]
    per = moved_in[0].shape[0] // 2
    old = ck.shape[0] - per
    loads = [pltpu.make_async_copy(moved_in[r], moved.at[r], sem.at[r]) for r in range(nq)]
    for load in loads:
        load.start()
    new_ck[0:old] = ck[0:old]
    new_cv[0:old] = cv[0:old]
    for load in loads:
        load.wait()
    for s in range(per):
        new_ck[old + s] = moved[source[s], 2 * s]
        new_cv[old + s] = moved[source[s], 2 * s + 1]


def refill(source, ck, cv, moved):
    shape = jax.ShapeDtypeStruct(ck.shape, ck.dtype)
    whole = pl.BlockSpec(memory_space=pltpu.VMEM)
    anywhere = pl.BlockSpec(memory_space=pl.ANY)
    nq = len(moved)
    return pl.pallas_call(
        functools.partial(refill_kernel, nq),
        out_shape=(shape, shape),
        in_specs=[pl.BlockSpec(memory_space=pltpu.SMEM)] + [whole] * 2 + [anywhere] * nq,
        out_specs=(whole, whole),
        scratch_shapes=[
            pltpu.VMEM((nq,) + moved[0].shape, moved[0].dtype),
            pltpu.SemaphoreType.DMA((nq,)),
        ],
        name="refill",
    )(source, ck, cv, *moved)


def plan(device, per, slots, size, cache_len, span_len, block_table, window):
    old = slots - per
    c = device % NC
    z = device // NC % NZ
    y = device // (NC * NZ)
    ring = jnp.array([-k for k in SHIFTS], jnp.int32)
    q_dev = ((y + ring) % NY * NZ + z) * NC + c
    pair = jnp.arange(NC, dtype=jnp.int32)
    k_dev = ((y * NZ + (z + ring[:, None]) % NZ) * NC + (c + pair[None, :]) % NC).reshape(-1)
    slot = jnp.arange(slots, dtype=jnp.int32)
    step = jnp.arange(per, dtype=jnp.int32)
    q_ids = (q_dev[:, None] * per + step[None, :]).reshape(-1)
    q_request, q_first = block_start(q_ids, span_len, cache_len, size)
    q_window = lookup(window, q_request)
    within = jnp.tile(slot, k_dev.shape[0])
    owner = jnp.repeat(k_dev, slots)
    is_old = within < old
    o_request, o_logical, o_live = slot_owner(block_table, cache_len // size, owner * slots + within)
    n_request, n_first = block_start(
        owner * per + jnp.maximum(within - old, 0), span_len, cache_len, size
    )
    k_request = jnp.where(is_old, o_request, n_request)
    k_first = jnp.where(is_old, o_logical * size, n_first)
    live = jnp.where(is_old, o_live, True)
    last = q_first + size - 1
    seen = (
        live[None, :]
        & (q_request[:, None] == k_request[None, :])
        & (k_first[None, :] <= last[:, None])
        & (
            (k_first[None, :] < SINK)
            | (q_first[:, None] - (k_first[None, :] + size - 1) < q_window[:, None])
        )
    )
    inside = (k_first[None, :] + size - 1 <= q_first[:, None]) & (
        last[:, None] - k_first[None, :] < q_window[:, None]
    )
    total = k_first.shape[0]
    ids = jnp.arange(total, dtype=jnp.int32)
    hits = seen.astype(jnp.int32)
    rim = (seen & ~inside).astype(jnp.int32)
    count = jnp.sum(hits, axis=1)
    rims = jnp.sum(rim, axis=1)
    odd = count % 2
    before = ids[None, None, :] < ids[None, :, None]
    rim_rank = jnp.sum(jnp.where(before, rim[:, None, :], 0), axis=2)
    rank = jnp.sum(jnp.where(before, hits[:, None, :], 0), axis=2)
    rank = odd[:, None] + jnp.where(rim > 0, rim_rank, rims[:, None] + rank - rim_rank)
    at = seen[:, None, :] & (rank[:, None, :] == ids[None, :, None])
    packed = jnp.sum(jnp.where(at, (k_first * total + ids)[None, None, :] + 1, 0), axis=2)
    chosen = jnp.maximum(packed - 1, 0) % total
    first_key = jnp.where(packed > 0, jnp.maximum(packed - 1, 0) // total, FAR)
    edges = (odd + rims + 1) // 2
    targets = table_entry(block_table, n_request, n_first // size)
    wanted = (q_dev[:, None] * slots + old + step[None, :]).reshape(-1)
    hit = (targets[None, :] == wanted[:, None]) & ~is_old[None, :]
    moves = jnp.sum(jnp.where(hit, ids[None, :], 0), axis=1)
    all_new = jnp.arange(NY * NZ * NC * per, dtype=jnp.int32)
    a_request, a_first = block_start(all_new, span_len, cache_len, size)
    a_target = table_entry(block_table, a_request, a_first // size)
    mine = a_target[None, :] == (device * slots + old + step)[:, None]
    from_y = jnp.sum(jnp.where(mine, (all_new // (per * NC * NZ))[None, :], 0), axis=1)
    source = ring_place(from_y - y)
    meta = (
        count,
        chosen.reshape(-1),
        edges,
        first_key.reshape(-1),
        q_first,
        q_window,
        moves,
    )
    return meta, source


def shards(
    queries,
    new_keys,
    new_values,
    cache_keys,
    cache_values,
    out_weight,
    cache_len,
    span_len,
    block_table,
    window,
):
    device = lax.axis_index("blk")
    head = lax.axis_index("head")
    tokens, heads, width = queries.shape
    slots, size = cache_keys.shape[:2]
    per = tokens // size
    log_scale = math.log2(math.e) / math.sqrt(width)
    ck = cache_keys.reshape(slots, size, width)
    cv = cache_values.reshape(slots, size, width)
    own_q = jnp.transpose(queries, (1, 0, 2))
    w_line = [out_weight] + [shift(out_weight, dz=k) for k in SHIFTS[1:]]
    q_near = [shift(own_q, dy=k) for k in SHIFTS[1:3]]
    own_kv = pack(
        ck, cv, new_keys.reshape(per, size, width), new_values.reshape(per, size, width)
    )
    own_kv = after(own_kv, *w_line[1:], *q_near)
    kv_near = [shift(own_kv, dz=k) for k in SHIFTS[1:3]]
    q_parts = [own_q, *q_near, shift(after(own_q, *q_near), dy=SHIFTS[3])]
    w_four = jnp.stack(w_line)
    w_near = [shift(w_four, dy=k) for k in SHIFTS[1:3]]
    far = [
        shift(kv_near[0][:slots], dz=SHIFTS[1]),
        shift(kv_near[1][slots:], dz=SHIFTS[2]),
    ]
    w_far = [*w_near, shift(after(w_four, *w_near), dy=SHIFTS[3])]
    kv_parts = []
    for part in (own_kv, *kv_near):
        kv_parts += [part, shift(part, dc=1)]
    kv_parts += far + [shift(part, dc=1) for part in far]
    w_parts = []
    for part in (w_four, *w_near):
        w_parts += [part, shift(part, dc=1)]
    meta, source = plan(device, per, slots, size, cache_len, span_len, block_table, window)
    outs = attend(meta, kv_parts, q_parts, log_scale)
    parts, moved = outs[: len(SHIFTS)], outs[len(SHIFTS) :]
    parts = [parts[0]] + [shift(p, dy=-k) for p, k in zip(parts[1:], SHIFTS[1:])]
    w_far[2] = after(w_far[2], *parts[1:])
    w_parts += [w_far[2], shift(w_far[2], dc=1)]
    pieces = piece_table(device, head, heads * width // out_weight.shape[0])
    shares = finish(pieces, [in_hbm(p) for p in parts], w_parts, heads)
    first, second = shares[:NX], shares[NX:]
    first = [first[0]] + [head_shift(p, dx=k) for p, k in zip(first[1:], SHIFTS[1:])]
    moved = [moved[0]] + [
        shift(after(p, first[1]), dy=-k) for p, k in zip(moved[1:], SHIFTS[1:])
    ]
    second_sum = second[0].astype(jnp.float32) + head_shift(second[1], dz=1).astype(jnp.float32)
    first_sum = functools.reduce(jnp.add, [p.astype(jnp.float32) for p in first])
    second_out = second_sum[0]
    for r in range(1, NX):
        second_out += head_shift(second_sum[r].astype(jnp.bfloat16), dx=SHIFTS[r]).astype(
            jnp.float32
        )
    first_out = first_sum[0] + head_shift(first_sum[1].astype(jnp.bfloat16), dz=1).astype(
        jnp.float32
    )
    attn_output = jnp.concatenate([first_out, second_out], axis=0).astype(jnp.bfloat16)
    new_ck, new_cv = refill(source, ck, cv, moved)
    return (
        attn_output,
        new_ck.reshape(cache_keys.shape),
        new_cv.reshape(cache_values.shape),
    )


def solution(mesh):
    placed = (
        P("blk", "head", None),
        P("blk", "head", None),
        P("blk", "head", None),
        P("blk", None, "head", None),
        P("blk", None, "head", None),
        P("blk", "head"),
        P(),
        P(),
        P(),
        P(),
    )
    return jax.shard_map(
        shards,
        mesh=mesh,
        in_specs=placed,
        out_specs=(P("blk", "head"), P("blk", None, "head", None), P("blk", None, "head", None)),
        check_vma=False,
    )
```

```python
import functools
import math

import jax
import jax.numpy as jnp
from jax import lax
from jax.experimental import pallas as pl
from jax.experimental.pallas import tpu as pltpu
from jax.sharding import PartitionSpec as P

NY, NZ, NC = 4, 4, 2
NX, NL = 4, 2
SINK = 4
LOWEST = -1e30
FLOOR = -1e25
FAR = 1 << 29
SHIFTS = (0, 1, -1, 2)


def blk_perm(dy, dz, dc):
    pairs = []
    for y in range(NY):
        for z in range(NZ):
            for c in range(NC):
                src = (y * NZ + z) * NC + c
                dst = ((y + dy) % NY * NZ + (z + dz) % NZ) * NC + (c + dc) % NC
                pairs.append((src, dst))
    return pairs


def shift(value, dy=0, dz=0, dc=0):
    return lax.ppermute(value, "blk", blk_perm(dy, dz, dc))


def after(value, *earlier):
    return lax.optimization_barrier((value, *earlier))[0]


def in_hbm(value):
    return pltpu.with_memory_space_constraint(value, pltpu.HBM)


def head_shift(value, dx=0, dz=0):
    pairs = []
    for x in range(NX):
        for z in range(NL):
            pairs.append((x * NL + z, (x + dx) % NX * NL + (z + dz) % NL))
    return lax.ppermute(value, "head", pairs)


def ring_place(distance):
    distance = distance % len(SHIFTS)
    return jnp.where(distance == 3, 2, jnp.where(distance == 2, 3, distance))


def lookup(table_row, wanted):
    places = jnp.arange(table_row.shape[0], dtype=jnp.int32)
    return jnp.sum(jnp.where(places[None, :] == wanted[:, None], table_row[None, :], 0), axis=1)


def block_start(global_block, span_len, cache_len, block_size):
    lower = jnp.arange(span_len.shape[0], dtype=jnp.int32)
    span_end = jnp.sum(jnp.where(lower[:, None] >= lower[None, :], span_len[None, :], 0), axis=1)
    first_token = global_block * block_size
    request = jnp.sum((first_token[:, None] >= span_end[None, :]).astype(jnp.int32), axis=1)
    return (request, lookup(cache_len - span_end + span_len, request) + first_token)


def table_entry(block_table, request, logical):
    row_ids = jnp.arange(block_table.shape[0], dtype=jnp.int32)
    col_ids = jnp.arange(block_table.shape[1], dtype=jnp.int32)
    match = (row_ids[None, :, None] == request[:, None, None]) & (
        col_ids[None, None, :] == logical[:, None, None]
    )
    return jnp.sum(jnp.where(match, block_table[None], 0), axis=(1, 2))


def slot_owner(block_table, limit, slot_ids):
    row_ids = jnp.arange(block_table.shape[0], dtype=jnp.int32)
    col_ids = jnp.arange(block_table.shape[1], dtype=jnp.int32)
    match = (block_table[None] == slot_ids[:, None, None]) & (
        col_ids[None, None, :] < limit[None, :, None]
    )
    packed = row_ids[:, None] * 4096 + col_ids[None, :] + 1
    found = jnp.sum(jnp.where(match, packed[None], 0), axis=(1, 2))
    place = jnp.maximum(found - 1, 0)
    return (place // 4096, place % 4096, found > 0)


def pack_kernel(ck, cv, nk, nv, out):
    new = nk.shape[0]
    old = ck.shape[0] - new
    out[0:old] = ck[0:old]
    out[old : old + new] = nk[...]
    out[old + new : 2 * old + new] = cv[0:old]
    out[2 * old + new :] = nv[...]


def pack(ck, cv, nk, nv):
    return pl.pallas_call(
        pack_kernel,
        out_shape=jax.ShapeDtypeStruct((2 * ck.shape[0],) + ck.shape[1:], ck.dtype),
        name="pack",
    )(ck, cv, nk, nv)


def attend_kernel(
    log_scale,
    nkv,
    nq,
    count,
    chosen,
    edges,
    first_key,
    first_query,
    reach,
    moves,
    *refs,
):
    kv_in = refs[:nkv]
    q_in = refs[nkv : nkv + nq]
    out_refs = refs[nkv + nq : nkv + 2 * nq]
    move_refs = refs[nkv + 2 * nq : nkv + 3 * nq]
    kv, queries, scores, high, total, result, in_sem, out_sem, move_sem = refs[nkv + 3 * nq :]
    slots = kv_in[0].shape[0]
    half = slots // 2
    begins = [sum(ref.shape[0] for ref in kv_in[:a]) for a in range(nkv)]
    heads, rows, width = q_in[0].shape
    size = kv_in[0].shape[1]
    per = rows // size
    wide = heads * size
    longest = chosen.shape[0] // (nq * per)
    loads = []
    for a in range(nkv):
        loads.append(
            pltpu.make_async_copy(
                kv_in[a], kv.at[pl.ds(begins[a], kv_in[a].shape[0])], in_sem.at[a]
            )
        )
    for r in range(nq):
        loads.append(pltpu.make_async_copy(q_in[r], queries.at[r], in_sem.at[nkv + r]))
    for load in loads:
        load.start()
    for load in loads:
        load.wait()

    def place(j):
        return j // half * slots + j % half

    sends = []
    for r in range(nq):
        for s in range(per):
            at = place(moves[r * per + s])
            for side in range(2):
                sends.append(
                    pltpu.make_async_copy(
                        kv.at[at + side * half],
                        move_refs[r].at[2 * s + side],
                        move_sem.at[(r * per + s) * 2 + side],
                    )
                )
    for send in sends:
        send.start()

    row_ids = lax.broadcasted_iota(jnp.int32, (size, width), 0)
    col_ids = lax.broadcasted_iota(jnp.int32, (size, width), 1)
    ones = jnp.ones((2 * size, width), jnp.bfloat16)

    def one_block(i, unused):
        r = i // per
        s = i % per
        begin = pl.multiple_of(s * size, size)
        query = jnp.concatenate(
            [queries[r, h, pl.ds(begin, size), :] for h in range(heads)], axis=0
        )
        pairs = (count[i] + 1) // 2
        high[...] = jnp.full_like(high, LOWEST)

        def raw_scores(t):
            at = i * longest + 2 * t
            keys = jnp.concatenate([kv[place(chosen[at])], kv[place(chosen[at + 1])]], axis=0)
            return lax.dot_general(
                query, keys, (((1,), (1,)), ((), ())), preferred_element_type=jnp.float32
            )

        def score_edge(t, unused):
            raw = raw_scores(t)
            for side in range(2):
                key_pos = first_key[i * longest + 2 * t + side] + col_ids
                distance = first_query[i] + row_ids - key_pos
                allowed = (distance >= 0) & ((distance < reach[i]) | (key_pos < SINK))
                hidden = jnp.where(allowed, 0.0, LOWEST)
                for h in range(heads):
                    lines = slice(h * size, (h + 1) * size)
                    part = raw[lines, side * size : (side + 1) * size]
                    part = jnp.where(hidden < 0.0, LOWEST, part)
                    scores[t, lines, side * size : (side + 1) * size] = part
                    high[lines, :] = jnp.maximum(high[lines, :], part)
            return unused

        def score_full(t, unused):
            raw = raw_scores(t)
            scores[t] = raw
            high[...] = jnp.maximum(high[...], jnp.maximum(raw[:, :size], raw[:, size:]))
            return unused

        lax.fori_loop(0, edges[i], score_edge, 0)
        lax.fori_loop(edges[i], pairs, score_full, 0)
        top = jnp.maximum(jnp.max(high[...], axis=1, keepdims=True), FLOOR)
        high[...] = jnp.broadcast_to(top, high.shape)
        total[...] = jnp.zeros_like(total)

        def blend(t, unused):
            at = i * longest + 2 * t
            values = jnp.concatenate(
                [kv[place(chosen[at]) + half], kv[place(chosen[at + 1]) + half]], axis=0
            )
            values = jnp.concatenate([values, ones], axis=1)
            level = high[...]
            level = jnp.concatenate([level, level], axis=1)
            weights = jnp.exp2((scores[t] - level) * log_scale).astype(jnp.bfloat16)
            total[...] += jnp.dot(weights, values, preferred_element_type=jnp.float32)
            return unused

        lax.fori_loop(0, pairs, blend, 0)
        summed = total[:, width:]
        safe = jnp.where(summed > 0.0, summed, 1.0)
        result[i, 0:wide, :] = (total[:, :width] / safe).astype(jnp.bfloat16)
        line_ids = lax.broadcasted_iota(jnp.int32, (16, width), 0)
        tops = jnp.zeros((16, width), jnp.float32)
        sums = jnp.zeros((16, width), jnp.float32)
        for h in range(heads):
            lines = slice(h * size, (h + 1) * size)
            row = jnp.sum(jnp.where(row_ids == col_ids, high[lines, :], 0.0), axis=0, keepdims=True)
            tops = jnp.where(line_ids % heads == h, row, tops)
            row = jnp.sum(
                jnp.where(row_ids == col_ids, total[lines, width:], 0.0), axis=0, keepdims=True
            )
            sums = jnp.where(line_ids % heads == h, row, sums)
        live = sums > 0.0
        level = tops * log_scale + jnp.log2(jnp.where(live, sums, 1.0))
        level = jnp.where(live, level, LOWEST)
        first = level.astype(jnp.bfloat16).astype(jnp.float32)
        second = (level - first).astype(jnp.bfloat16).astype(jnp.float32)
        third = level - first - second
        stats = jnp.where(line_ids < heads, first, jnp.where(line_ids < 2 * heads, second, third))
        result[i, wide : wide + 16, :] = stats.astype(jnp.bfloat16)
        return unused

    backs = []
    for r in reversed(range(nq)):
        lax.fori_loop(r * per, (r + 1) * per, one_block, 0)
        backs.append(
            pltpu.make_async_copy(result.at[pl.ds(r * per, per)], out_refs[r], out_sem.at[r])
        )
        backs[-1].start()
    for send in sends:
        send.wait()
    for back in backs:
        back.wait()


def attend(meta, kv_parts, q_parts, log_scale):
    _, size, width = kv_parts[0].shape
    heads, rows, _ = q_parts[0].shape
    nkv, nq, per = len(kv_parts), len(q_parts), rows // size
    wide = heads * size
    longest = meta[1].shape[0] // (nq * per)
    smem = pl.BlockSpec(memory_space=pltpu.SMEM)
    anywhere = pl.BlockSpec(memory_space=pl.ANY)
    parts = jax.ShapeDtypeStruct((per, wide + 16, width), jnp.bfloat16)
    moved = jax.ShapeDtypeStruct((2 * per, size, width), jnp.bfloat16)
    return pl.pallas_call(
        functools.partial(attend_kernel, log_scale, nkv, nq),
        out_shape=(parts,) * nq + (moved,) * nq,
        in_specs=[smem] * len(meta) + [anywhere] * (nkv + nq),
        out_specs=(anywhere,) * (2 * nq),
        scratch_shapes=[
            pltpu.VMEM((sum(p.shape[0] for p in kv_parts), size, width), jnp.bfloat16),
            pltpu.VMEM((nq, heads, rows, width), jnp.bfloat16),
            pltpu.VMEM((longest // 2, wide, 2 * size), jnp.float32),
            pltpu.VMEM((wide, size), jnp.float32),
            pltpu.VMEM((wide, 2 * width), jnp.float32),
            pltpu.VMEM((nq * per, wide + 16, width), jnp.bfloat16),
            pltpu.SemaphoreType.DMA((nkv + nq,)),
            pltpu.SemaphoreType.DMA((nq,)),
            pltpu.SemaphoreType.DMA((2 * nq * per,)),
        ],
        compiler_params=pltpu.CompilerParams(vmem_limit_bytes=56 << 20),
        cost_estimate=pl.CostEstimate(
            flops=5_000_000_000, bytes_accessed=8_000_000, transcendentals=8_000_000
        ),
        name="attend",
    )(*meta, *kv_parts, *q_parts)


def finish_kernel(heads, nparts, nw, pieces, *refs):
    part_in = refs[:nparts]
    w_in = refs[nparts : nparts + nw]
    first_out = refs[nparts + nw : nparts + nw + NX]
    second_out = refs[nparts + nw + NX : nparts + nw + NX + NL]
    parts, weight, mixed_rows, first, second, part_sem, w_sem, a_sem, b_sem = refs[
        nparts + nw + NX + NL :
    ]
    group = w_in[0].shape[0]
    per, lines, width = part_in[0].shape
    size = (lines - 16) // heads
    part_loads = [
        pltpu.make_async_copy(part_in[r], parts.at[r], part_sem.at[r]) for r in range(nparts)
    ]
    w_loads = [
        pltpu.make_async_copy(w_in[a], weight.at[pl.ds(a * group, group)], w_sem.at[a])
        for a in range(nw)
    ]
    for load in part_loads + w_loads:
        load.start()
    for load in part_loads:
        load.wait()
    row_ids = lax.broadcasted_iota(jnp.int32, (size, width), 0)
    col_ids = lax.broadcasted_iota(jnp.int32, (size, width), 1)
    for s in range(per):
        levels = []
        for r in range(nparts):
            stats = parts[r, s, heads * size :, :].astype(jnp.float32)
            levels.append(
                stats[0:heads] + stats[heads : 2 * heads] + stats[2 * heads : 3 * heads]
            )
        top = functools.reduce(jnp.maximum, levels)
        shares = [jnp.exp2(level - top) for level in levels]
        whole = functools.reduce(jnp.add, shares)
        shares = [share / whole for share in shares]
        for h in range(heads):
            mixed = jnp.zeros((size, width), jnp.float32)
            for r in range(nparts):
                spread = jnp.where(row_ids == col_ids, shares[r][h : h + 1, :], 0.0)
                column = jnp.sum(spread, axis=1, keepdims=True)
                mixed += column * parts[r, s, h * size : (h + 1) * size, :].astype(jnp.float32)
            mixed_rows[s * size : (s + 1) * size, h * width : (h + 1) * width] = mixed.astype(
                jnp.bfloat16
            )
    for load in w_loads:
        load.wait()
    sends = []
    for r in reversed(range(NX)):
        for z in range(NL):
            at = (r * NL + z) * group
            rows = jnp.concatenate([weight[pieces[at + q]] for q in range(group)], axis=0)
            product = lax.dot_general(
                mixed_rows[...], rows, (((1,), (1,)), ((), ())), preferred_element_type=jnp.float32
            ).astype(jnp.bfloat16)
            first[r, z] = product[:size]
            second[z, r] = product[size:]
        sends.append(pltpu.make_async_copy(first.at[r], first_out[r], a_sem.at[r]))
        sends[-1].start()
    for z in range(NL):
        sends.append(pltpu.make_async_copy(second.at[z], second_out[z], b_sem.at[z]))
        sends[-1].start()
    for send in sends:
        send.wait()


def finish(pieces, parts, w_parts, heads):
    per, lines, width = parts[0].shape
    size = (lines - 16) // heads
    group, rows, depth = w_parts[0].shape
    columns = group * rows
    nparts, nw = len(parts), len(w_parts)
    anywhere = pl.BlockSpec(memory_space=pl.ANY)
    first = jax.ShapeDtypeStruct((NL, size, columns), jnp.bfloat16)
    second = jax.ShapeDtypeStruct((NX, size, columns), jnp.bfloat16)
    return pl.pallas_call(
        functools.partial(finish_kernel, heads, nparts, nw),
        out_shape=(first,) * NX + (second,) * NL,
        in_specs=[pl.BlockSpec(memory_space=pltpu.SMEM)] + [anywhere] * (nparts + nw),
        out_specs=(anywhere,) * (NX + NL),
        scratch_shapes=[
            pltpu.VMEM((nparts, per, lines, width), jnp.bfloat16),
            pltpu.VMEM((nw * group, rows, depth), jnp.bfloat16),
            pltpu.VMEM((per * size, heads * width), jnp.bfloat16),
            pltpu.VMEM((NX, NL, size, columns), jnp.bfloat16),
            pltpu.VMEM((NL, NX, size, columns), jnp.bfloat16),
            pltpu.SemaphoreType.DMA((nparts,)),
            pltpu.SemaphoreType.DMA((nw,)),
            pltpu.SemaphoreType.DMA((NX,)),
            pltpu.SemaphoreType.DMA((NL,)),
        ],
        compiler_params=pltpu.CompilerParams(vmem_limit_bytes=24 << 20),
        cost_estimate=pl.CostEstimate(
            flops=2_000_000_000, bytes_accessed=12_000_000, transcendentals=10_000
        ),
        name="finish",
    )(pieces, *parts, *w_parts)


def piece_table(device, head, group):
    c = device % NC
    z = device // NC % NZ
    y = device // (NC * NZ)
    steps = jnp.array(SHIFTS, jnp.int32)
    target = (head // NL + steps[:, None]) % NX * NL + (head + jnp.arange(NL)[None, :]) % NL
    owner = (target.reshape(-1)[:, None] * group + jnp.arange(group)[None, :]).reshape(-1)
    place = ring_place(y - owner // (NC * NZ)) * NC + (c + owner) % NC
    return (place * NZ + ring_place(z - owner // NC % NZ)).astype(jnp.int32)


def refill_kernel(nq, source, ck, cv, *refs):
    moved_in = refs[:nq]
    new_ck, new_cv, moved, sem = refs[nq:]
    per = moved_in[0].shape[0] // 2
    old = ck.shape[0] - per
    loads = [pltpu.make_async_copy(moved_in[r], moved.at[r], sem.at[r]) for r in range(nq)]
    for load in loads:
        load.start()
    new_ck[0:old] = ck[0:old]
    new_cv[0:old] = cv[0:old]
    for load in loads:
        load.wait()
    for s in range(per):
        new_ck[old + s] = moved[source[s], 2 * s]
        new_cv[old + s] = moved[source[s], 2 * s + 1]


def refill(source, ck, cv, moved):
    shape = jax.ShapeDtypeStruct(ck.shape, ck.dtype)
    whole = pl.BlockSpec(memory_space=pltpu.VMEM)
    anywhere = pl.BlockSpec(memory_space=pl.ANY)
    nq = len(moved)
    return pl.pallas_call(
        functools.partial(refill_kernel, nq),
        out_shape=(shape, shape),
        in_specs=[pl.BlockSpec(memory_space=pltpu.SMEM)] + [whole] * 2 + [anywhere] * nq,
        out_specs=(whole, whole),
        scratch_shapes=[
            pltpu.VMEM((nq,) + moved[0].shape, moved[0].dtype),
            pltpu.SemaphoreType.DMA((nq,)),
        ],
        name="refill",
    )(source, ck, cv, *moved)


def plan(device, per, slots, size, cache_len, span_len, block_table, window):
    old = slots - per
    c = device % NC
    z = device // NC % NZ
    y = device // (NC * NZ)
    ring = jnp.array([-k for k in SHIFTS], jnp.int32)
    q_dev = ((y + ring) % NY * NZ + z) * NC + c
    pair = jnp.arange(NC, dtype=jnp.int32)
    k_dev = ((y * NZ + (z + ring[:, None]) % NZ) * NC + (c + pair[None, :]) % NC).reshape(-1)
    slot = jnp.arange(slots, dtype=jnp.int32)
    step = jnp.arange(per, dtype=jnp.int32)
    q_ids = (q_dev[:, None] * per + step[None, :]).reshape(-1)
    q_request, q_first = block_start(q_ids, span_len, cache_len, size)
    q_window = lookup(window, q_request)
    within = jnp.tile(slot, k_dev.shape[0])
    owner = jnp.repeat(k_dev, slots)
    is_old = within < old
    o_request, o_logical, o_live = slot_owner(block_table, cache_len // size, owner * slots + within)
    n_request, n_first = block_start(
        owner * per + jnp.maximum(within - old, 0), span_len, cache_len, size
    )
    k_request = jnp.where(is_old, o_request, n_request)
    k_first = jnp.where(is_old, o_logical * size, n_first)
    live = jnp.where(is_old, o_live, True)
    last = q_first + size - 1
    seen = (
        live[None, :]
        & (q_request[:, None] == k_request[None, :])
        & (k_first[None, :] <= last[:, None])
        & (
            (k_first[None, :] < SINK)
            | (q_first[:, None] - (k_first[None, :] + size - 1) < q_window[:, None])
        )
    )
    inside = (k_first[None, :] + size - 1 <= q_first[:, None]) & (
        last[:, None] - k_first[None, :] < q_window[:, None]
    )
    total = k_first.shape[0]
    ids = jnp.arange(total, dtype=jnp.int32)
    hits = seen.astype(jnp.int32)
    rim = (seen & ~inside).astype(jnp.int32)
    count = jnp.sum(hits, axis=1)
    rims = jnp.sum(rim, axis=1)
    odd = count % 2
    before = ids[None, None, :] < ids[None, :, None]
    rim_rank = jnp.sum(jnp.where(before, rim[:, None, :], 0), axis=2)
    rank = jnp.sum(jnp.where(before, hits[:, None, :], 0), axis=2)
    rank = odd[:, None] + jnp.where(rim > 0, rim_rank, rims[:, None] + rank - rim_rank)
    at = seen[:, None, :] & (rank[:, None, :] == ids[None, :, None])
    packed = jnp.sum(jnp.where(at, (k_first * total + ids)[None, None, :] + 1, 0), axis=2)
    chosen = jnp.maximum(packed - 1, 0) % total
    first_key = jnp.where(packed > 0, jnp.maximum(packed - 1, 0) // total, FAR)
    edges = (odd + rims + 1) // 2
    targets = table_entry(block_table, n_request, n_first // size)
    wanted = (q_dev[:, None] * slots + old + step[None, :]).reshape(-1)
    hit = (targets[None, :] == wanted[:, None]) & ~is_old[None, :]
    moves = jnp.sum(jnp.where(hit, ids[None, :], 0), axis=1)
    all_new = jnp.arange(NY * NZ * NC * per, dtype=jnp.int32)
    a_request, a_first = block_start(all_new, span_len, cache_len, size)
    a_target = table_entry(block_table, a_request, a_first // size)
    mine = a_target[None, :] == (device * slots + old + step)[:, None]
    from_y = jnp.sum(jnp.where(mine, (all_new // (per * NC * NZ))[None, :], 0), axis=1)
    source = ring_place(from_y - y)
    meta = (
        count,
        chosen.reshape(-1),
        edges,
        first_key.reshape(-1),
        q_first,
        q_window,
        moves,
    )
    return meta, source


def shards(
    queries,
    new_keys,
    new_values,
    cache_keys,
    cache_values,
    out_weight,
    cache_len,
    span_len,
    block_table,
    window,
):
    device = lax.axis_index("blk")
    head = lax.axis_index("head")
    tokens, heads, width = queries.shape
    slots, size = cache_keys.shape[:2]
    per = tokens // size
    log_scale = math.log2(math.e) / math.sqrt(width)
    ck = cache_keys.reshape(slots, size, width)
    cv = cache_values.reshape(slots, size, width)
    own_q = jnp.transpose(queries, (1, 0, 2))
    w_line = [out_weight] + [shift(out_weight, dz=k) for k in SHIFTS[1:]]
    q_near = [shift(own_q, dy=k) for k in SHIFTS[1:3]]
    own_kv = pack(
        ck, cv, new_keys.reshape(per, size, width), new_values.reshape(per, size, width)
    )
    own_kv = after(own_kv, *w_line[1:], *q_near)
    kv_near = [shift(own_kv, dz=k) for k in SHIFTS[1:3]]
    q_parts = [own_q, *q_near, shift(after(own_q, *q_near), dy=SHIFTS[3])]
    w_four = jnp.stack(w_line)
    w_four = after(w_four, q_parts[3])
    w_near = [shift(w_four, dy=k) for k in SHIFTS[1:3]]
    far = [
        shift(kv_near[0][:slots], dz=SHIFTS[1]),
        shift(kv_near[1][slots:], dz=SHIFTS[2]),
    ]
    w_far = [*w_near, shift(after(w_four, *w_near), dy=SHIFTS[3])]
    kv_parts = []
    for part in (own_kv, *kv_near):
        kv_parts += [part, shift(part, dc=1)]
    kv_parts += far + [shift(part, dc=1) for part in far]
    w_parts = []
    for part in (w_four, *w_near):
        w_parts += [part, shift(part, dc=1)]
    meta, source = plan(device, per, slots, size, cache_len, span_len, block_table, window)
    outs = attend(meta, kv_parts, q_parts, log_scale)
    parts, moved = outs[: len(SHIFTS)], outs[len(SHIFTS) :]
    parts = [parts[0]] + [shift(p, dy=-k) for p, k in zip(parts[1:], SHIFTS[1:])]
    w_far[2] = after(w_far[2], *parts[1:])
    w_parts += [w_far[2], shift(w_far[2], dc=1)]
    pieces = piece_table(device, head, heads * width // out_weight.shape[0])
    shares = finish(pieces, [in_hbm(p) for p in parts], w_parts, heads)
    first, second = shares[:NX], shares[NX:]
    first = [first[0]] + [head_shift(p, dx=k) for p, k in zip(first[1:], SHIFTS[1:])]
    moved = list(moved)
    for r in (1, 2):
        moved[r] = shift(after(moved[r], first[1]), dy=-SHIFTS[r])
    moved[3] = shift(after(moved[3], moved[1]), dy=-SHIFTS[3])
    second_sum = second[0].astype(jnp.float32) + head_shift(second[1], dz=1).astype(jnp.float32)
    first_sum = functools.reduce(jnp.add, [p.astype(jnp.float32) for p in first])
    second_sum = after(second_sum, moved[1], moved[2])
    second_far = [
        head_shift(second_sum[r].astype(jnp.bfloat16), dx=SHIFTS[r]) for r in range(1, NX)
    ]
    second_out = functools.reduce(
        jnp.add, [p.astype(jnp.float32) for p in second_far], second_sum[0]
    )
    first_out = first_sum[0] + head_shift(first_sum[1].astype(jnp.bfloat16), dz=1).astype(
        jnp.float32
    )
    attn_output = jnp.concatenate([first_out, second_out], axis=0).astype(jnp.bfloat16)
    moved[1] = after(moved[1], second_far[0])
    new_ck, new_cv = refill(source, ck, cv, moved)
    return (
        attn_output,
        new_ck.reshape(cache_keys.shape),
        new_cv.reshape(cache_values.shape),
    )


def solution(mesh):
    placed = (
        P("blk", "head", None),
        P("blk", "head", None),
        P("blk", "head", None),
        P("blk", None, "head", None),
        P("blk", None, "head", None),
        P("blk", "head"),
        P(),
        P(),
        P(),
        P(),
    )
    return jax.shard_map(
        shards,
        mesh=mesh,
        in_specs=placed,
        out_specs=(P("blk", "head"), P("blk", None, "head", None), P("blk", None, "head", None)),
        check_vma=False,
    )
```

```python
import functools
import math

import jax
import jax.numpy as jnp
from jax import lax
from jax.experimental import pallas as pl
from jax.experimental.pallas import tpu as pltpu
from jax.sharding import PartitionSpec as P

NY, NZ, NC = 4, 4, 2
NX, NL = 4, 2
SINK = 4
LOWEST = -1e30
FLOOR = -1e25
FAR = 1 << 29
SHIFTS = (0, 1, -1, 2)


def blk_perm(dy, dz, dc):
    pairs = []
    for y in range(NY):
        for z in range(NZ):
            for c in range(NC):
                src = (y * NZ + z) * NC + c
                dst = ((y + dy) % NY * NZ + (z + dz) % NZ) * NC + (c + dc) % NC
                pairs.append((src, dst))
    return pairs


def shift(value, dy=0, dz=0, dc=0):
    return lax.ppermute(value, "blk", blk_perm(dy, dz, dc))


def after(value, *earlier):
    return lax.optimization_barrier((value, *earlier))[0]


def in_hbm(value):
    return pltpu.with_memory_space_constraint(value, pltpu.HBM)


def head_shift(value, dx=0, dz=0):
    pairs = []
    for x in range(NX):
        for z in range(NL):
            pairs.append((x * NL + z, (x + dx) % NX * NL + (z + dz) % NL))
    return lax.ppermute(value, "head", pairs)


def ring_place(distance):
    distance = distance % len(SHIFTS)
    return jnp.where(distance == 3, 2, jnp.where(distance == 2, 3, distance))


def lookup(table_row, wanted):
    places = jnp.arange(table_row.shape[0], dtype=jnp.int32)
    return jnp.sum(jnp.where(places[None, :] == wanted[:, None], table_row[None, :], 0), axis=1)


def block_start(global_block, span_len, cache_len, block_size):
    lower = jnp.arange(span_len.shape[0], dtype=jnp.int32)
    span_end = jnp.sum(jnp.where(lower[:, None] >= lower[None, :], span_len[None, :], 0), axis=1)
    first_token = global_block * block_size
    request = jnp.sum((first_token[:, None] >= span_end[None, :]).astype(jnp.int32), axis=1)
    return (request, lookup(cache_len - span_end + span_len, request) + first_token)


def table_entry(block_table, request, logical):
    row_ids = jnp.arange(block_table.shape[0], dtype=jnp.int32)
    col_ids = jnp.arange(block_table.shape[1], dtype=jnp.int32)
    match = (row_ids[None, :, None] == request[:, None, None]) & (
        col_ids[None, None, :] == logical[:, None, None]
    )
    return jnp.sum(jnp.where(match, block_table[None], 0), axis=(1, 2))


def slot_owner(block_table, limit, slot_ids):
    row_ids = jnp.arange(block_table.shape[0], dtype=jnp.int32)
    col_ids = jnp.arange(block_table.shape[1], dtype=jnp.int32)
    match = (block_table[None] == slot_ids[:, None, None]) & (
        col_ids[None, None, :] < limit[None, :, None]
    )
    packed = row_ids[:, None] * 4096 + col_ids[None, :] + 1
    found = jnp.sum(jnp.where(match, packed[None], 0), axis=(1, 2))
    place = jnp.maximum(found - 1, 0)
    return (place // 4096, place % 4096, found > 0)


def pack_kernel(ck, cv, nk, nv, out):
    new = nk.shape[0]
    old = ck.shape[0] - new
    out[0:old] = ck[0:old]
    out[old : old + new] = nk[...]
    out[old + new : 2 * old + new] = cv[0:old]
    out[2 * old + new :] = nv[...]


def pack(ck, cv, nk, nv):
    return pl.pallas_call(
        pack_kernel,
        out_shape=jax.ShapeDtypeStruct((2 * ck.shape[0],) + ck.shape[1:], ck.dtype),
        name="pack",
    )(ck, cv, nk, nv)


def attend_kernel(
    log_scale,
    nkv,
    nq,
    count,
    chosen,
    edges,
    first_key,
    first_query,
    reach,
    moves,
    *refs,
):
    kv_in = refs[:nkv]
    q_in = refs[nkv : nkv + nq]
    out_refs = refs[nkv + nq : nkv + 2 * nq]
    move_refs = refs[nkv + 2 * nq : nkv + 3 * nq]
    kv, queries, scores, high, total, result, in_sem, out_sem, move_sem = refs[nkv + 3 * nq :]
    slots = kv_in[0].shape[0]
    half = slots // 2
    begins = [sum(ref.shape[0] for ref in kv_in[:a]) for a in range(nkv)]
    heads, rows, width = q_in[0].shape
    size = kv_in[0].shape[1]
    per = rows // size
    wide = heads * size
    longest = chosen.shape[0] // (nq * per)
    loads = []
    for a in range(nkv):
        loads.append(
            pltpu.make_async_copy(
                kv_in[a], kv.at[pl.ds(begins[a], kv_in[a].shape[0])], in_sem.at[a]
            )
        )
    for r in range(nq):
        loads.append(pltpu.make_async_copy(q_in[r], queries.at[r], in_sem.at[nkv + r]))
    for load in loads:
        load.start()
    for load in loads:
        load.wait()

    def place(j):
        return j // half * slots + j % half

    sends = []
    for r in range(nq):
        for s in range(per):
            at = place(moves[r * per + s])
            for side in range(2):
                sends.append(
                    pltpu.make_async_copy(
                        kv.at[at + side * half],
                        move_refs[r].at[2 * s + side],
                        move_sem.at[(r * per + s) * 2 + side],
                    )
                )
    for send in sends:
        send.start()

    row_ids = lax.broadcasted_iota(jnp.int32, (size, width), 0)
    col_ids = lax.broadcasted_iota(jnp.int32, (size, width), 1)
    ones = jnp.ones((2 * size, width), jnp.bfloat16)

    def one_block(i, unused):
        r = i // per
        s = i % per
        begin = pl.multiple_of(s * size, size)
        query = jnp.concatenate(
            [queries[r, h, pl.ds(begin, size), :] for h in range(heads)], axis=0
        )
        pairs = (count[i] + 1) // 2
        high[...] = jnp.full_like(high, LOWEST)

        def raw_scores(t):
            at = i * longest + 2 * t
            keys = jnp.concatenate([kv[place(chosen[at])], kv[place(chosen[at + 1])]], axis=0)
            return lax.dot_general(
                query, keys, (((1,), (1,)), ((), ())), preferred_element_type=jnp.float32
            )

        def score_edge(t, unused):
            raw = raw_scores(t)
            for side in range(2):
                key_pos = first_key[i * longest + 2 * t + side] + col_ids
                distance = first_query[i] + row_ids - key_pos
                allowed = (distance >= 0) & ((distance < reach[i]) | (key_pos < SINK))
                hidden = jnp.where(allowed, 0.0, LOWEST)
                for h in range(heads):
                    lines = slice(h * size, (h + 1) * size)
                    part = raw[lines, side * size : (side + 1) * size]
                    part = jnp.where(hidden < 0.0, LOWEST, part)
                    scores[t, lines, side * size : (side + 1) * size] = part
                    high[lines, :] = jnp.maximum(high[lines, :], part)
            return unused

        def score_full(t, unused):
            raw = raw_scores(t)
            scores[t] = raw
            high[...] = jnp.maximum(high[...], jnp.maximum(raw[:, :size], raw[:, size:]))
            return unused

        lax.fori_loop(0, edges[i], score_edge, 0)
        lax.fori_loop(edges[i], pairs, score_full, 0)
        top = jnp.maximum(jnp.max(high[...], axis=1, keepdims=True), FLOOR)
        high[...] = jnp.broadcast_to(top, high.shape)
        total[...] = jnp.zeros_like(total)

        def blend(t, unused):
            at = i * longest + 2 * t
            values = jnp.concatenate(
                [kv[place(chosen[at]) + half], kv[place(chosen[at + 1]) + half]], axis=0
            )
            values = jnp.concatenate([values, ones], axis=1)
            level = high[...]
            level = jnp.concatenate([level, level], axis=1)
            weights = jnp.exp2((scores[t] - level) * log_scale).astype(jnp.bfloat16)
            total[...] += jnp.dot(weights, values, preferred_element_type=jnp.float32)
            return unused

        lax.fori_loop(0, pairs, blend, 0)
        summed = total[:, width:]
        safe = jnp.where(summed > 0.0, summed, 1.0)
        result[i, 0:wide, :] = (total[:, :width] / safe).astype(jnp.bfloat16)
        line_ids = lax.broadcasted_iota(jnp.int32, (16, width), 0)
        tops = jnp.zeros((16, width), jnp.float32)
        sums = jnp.zeros((16, width), jnp.float32)
        for h in range(heads):
            lines = slice(h * size, (h + 1) * size)
            row = jnp.sum(jnp.where(row_ids == col_ids, high[lines, :], 0.0), axis=0, keepdims=True)
            tops = jnp.where(line_ids % heads == h, row, tops)
            row = jnp.sum(
                jnp.where(row_ids == col_ids, total[lines, width:], 0.0), axis=0, keepdims=True
            )
            sums = jnp.where(line_ids % heads == h, row, sums)
        live = sums > 0.0
        level = tops * log_scale + jnp.log2(jnp.where(live, sums, 1.0))
        level = jnp.where(live, level, LOWEST)
        first = level.astype(jnp.bfloat16).astype(jnp.float32)
        second = (level - first).astype(jnp.bfloat16).astype(jnp.float32)
        third = level - first - second
        stats = jnp.where(line_ids < heads, first, jnp.where(line_ids < 2 * heads, second, third))
        result[i, wide : wide + 16, :] = stats.astype(jnp.bfloat16)
        return unused

    backs = []
    for r in reversed(range(nq)):
        lax.fori_loop(r * per, (r + 1) * per, one_block, 0)
        backs.append(
            pltpu.make_async_copy(result.at[pl.ds(r * per, per)], out_refs[r], out_sem.at[r])
        )
        backs[-1].start()
    for send in sends:
        send.wait()
    for back in backs:
        back.wait()


def attend(meta, kv_parts, q_parts, log_scale):
    _, size, width = kv_parts[0].shape
    heads, rows, _ = q_parts[0].shape
    nkv, nq, per = len(kv_parts), len(q_parts), rows // size
    wide = heads * size
    longest = meta[1].shape[0] // (nq * per)
    smem = pl.BlockSpec(memory_space=pltpu.SMEM)
    anywhere = pl.BlockSpec(memory_space=pl.ANY)
    parts = jax.ShapeDtypeStruct((per, wide + 16, width), jnp.bfloat16)
    moved = jax.ShapeDtypeStruct((2 * per, size, width), jnp.bfloat16)
    return pl.pallas_call(
        functools.partial(attend_kernel, log_scale, nkv, nq),
        out_shape=(parts,) * nq + (moved,) * nq,
        in_specs=[smem] * len(meta) + [anywhere] * (nkv + nq),
        out_specs=(anywhere,) * (2 * nq),
        scratch_shapes=[
            pltpu.VMEM((sum(p.shape[0] for p in kv_parts), size, width), jnp.bfloat16),
            pltpu.VMEM((nq, heads, rows, width), jnp.bfloat16),
            pltpu.VMEM((longest // 2, wide, 2 * size), jnp.float32),
            pltpu.VMEM((wide, size), jnp.float32),
            pltpu.VMEM((wide, 2 * width), jnp.float32),
            pltpu.VMEM((nq * per, wide + 16, width), jnp.bfloat16),
            pltpu.SemaphoreType.DMA((nkv + nq,)),
            pltpu.SemaphoreType.DMA((nq,)),
            pltpu.SemaphoreType.DMA((2 * nq * per,)),
        ],
        compiler_params=pltpu.CompilerParams(vmem_limit_bytes=56 << 20),
        cost_estimate=pl.CostEstimate(
            flops=5_000_000_000, bytes_accessed=8_000_000, transcendentals=8_000_000
        ),
        name="attend",
    )(*meta, *kv_parts, *q_parts)


def finish_kernel(heads, nparts, nw, pieces, *refs):
    part_in = refs[:nparts]
    w_in = refs[nparts : nparts + nw]
    first_out = refs[nparts + nw : nparts + nw + NX]
    second_out = refs[nparts + nw + NX : nparts + nw + NX + NL]
    parts, weight, mixed_rows, first, second, part_sem, w_sem, a_sem, b_sem = refs[
        nparts + nw + NX + NL :
    ]
    group = w_in[0].shape[0]
    per, lines, width = part_in[0].shape
    size = (lines - 16) // heads
    part_loads = [
        pltpu.make_async_copy(part_in[r], parts.at[r], part_sem.at[r]) for r in range(nparts)
    ]
    w_loads = [
        pltpu.make_async_copy(w_in[a], weight.at[pl.ds(a * group, group)], w_sem.at[a])
        for a in range(nw)
    ]
    for load in part_loads + w_loads:
        load.start()
    for load in part_loads:
        load.wait()
    row_ids = lax.broadcasted_iota(jnp.int32, (size, width), 0)
    col_ids = lax.broadcasted_iota(jnp.int32, (size, width), 1)
    for s in range(per):
        levels = []
        for r in range(nparts):
            stats = parts[r, s, heads * size :, :].astype(jnp.float32)
            levels.append(
                stats[0:heads] + stats[heads : 2 * heads] + stats[2 * heads : 3 * heads]
            )
        top = functools.reduce(jnp.maximum, levels)
        shares = [jnp.exp2(level - top) for level in levels]
        whole = functools.reduce(jnp.add, shares)
        shares = [share / whole for share in shares]
        for h in range(heads):
            mixed = jnp.zeros((size, width), jnp.float32)
            for r in range(nparts):
                spread = jnp.where(row_ids == col_ids, shares[r][h : h + 1, :], 0.0)
                column = jnp.sum(spread, axis=1, keepdims=True)
                mixed += column * parts[r, s, h * size : (h + 1) * size, :].astype(jnp.float32)
            mixed_rows[s * size : (s + 1) * size, h * width : (h + 1) * width] = mixed.astype(
                jnp.bfloat16
            )
    for load in w_loads:
        load.wait()
    sends = []
    for r in reversed(range(NX)):
        for z in range(NL):
            at = (r * NL + z) * group
            rows = jnp.concatenate([weight[pieces[at + q]] for q in range(group)], axis=0)
            product = lax.dot_general(
                mixed_rows[...], rows, (((1,), (1,)), ((), ())), preferred_element_type=jnp.float32
            ).astype(jnp.bfloat16)
            first[r, z] = product[:size]
            second[z, r] = product[size:]
        sends.append(pltpu.make_async_copy(first.at[r], first_out[r], a_sem.at[r]))
        sends[-1].start()
    for z in range(NL):
        sends.append(pltpu.make_async_copy(second.at[z], second_out[z], b_sem.at[z]))
        sends[-1].start()
    for send in sends:
        send.wait()


def finish(pieces, parts, w_parts, heads):
    per, lines, width = parts[0].shape
    size = (lines - 16) // heads
    group, rows, depth = w_parts[0].shape
    columns = group * rows
    nparts, nw = len(parts), len(w_parts)
    anywhere = pl.BlockSpec(memory_space=pl.ANY)
    first = jax.ShapeDtypeStruct((NL, size, columns), jnp.bfloat16)
    second = jax.ShapeDtypeStruct((NX, size, columns), jnp.bfloat16)
    return pl.pallas_call(
        functools.partial(finish_kernel, heads, nparts, nw),
        out_shape=(first,) * NX + (second,) * NL,
        in_specs=[pl.BlockSpec(memory_space=pltpu.SMEM)] + [anywhere] * (nparts + nw),
        out_specs=(anywhere,) * (NX + NL),
        scratch_shapes=[
            pltpu.VMEM((nparts, per, lines, width), jnp.bfloat16),
            pltpu.VMEM((nw * group, rows, depth), jnp.bfloat16),
            pltpu.VMEM((per * size, heads * width), jnp.bfloat16),
            pltpu.VMEM((NX, NL, size, columns), jnp.bfloat16),
            pltpu.VMEM((NL, NX, size, columns), jnp.bfloat16),
            pltpu.SemaphoreType.DMA((nparts,)),
            pltpu.SemaphoreType.DMA((nw,)),
            pltpu.SemaphoreType.DMA((NX,)),
            pltpu.SemaphoreType.DMA((NL,)),
        ],
        compiler_params=pltpu.CompilerParams(vmem_limit_bytes=24 << 20),
        cost_estimate=pl.CostEstimate(
            flops=2_000_000_000, bytes_accessed=12_000_000, transcendentals=10_000
        ),
        name="finish",
    )(pieces, *parts, *w_parts)


def piece_table(device, head, group):
    c = device % NC
    z = device // NC % NZ
    y = device // (NC * NZ)
    steps = jnp.array(SHIFTS, jnp.int32)
    target = (head // NL + steps[:, None]) % NX * NL + (head + jnp.arange(NL)[None, :]) % NL
    owner = (target.reshape(-1)[:, None] * group + jnp.arange(group)[None, :]).reshape(-1)
    place = ring_place(y - owner // (NC * NZ)) * NC + (c + owner) % NC
    return (place * NZ + ring_place(z - owner // NC % NZ)).astype(jnp.int32)


def refill_kernel(nq, source, ck, cv, *refs):
    moved_in = refs[:nq]
    new_ck, new_cv, moved, sem = refs[nq:]
    per = moved_in[0].shape[0] // 2
    old = ck.shape[0] - per
    loads = [pltpu.make_async_copy(moved_in[r], moved.at[r], sem.at[r]) for r in range(nq)]
    for load in loads:
        load.start()
    new_ck[0:old] = ck[0:old]
    new_cv[0:old] = cv[0:old]
    for load in loads:
        load.wait()
    for s in range(per):
        new_ck[old + s] = moved[source[s], 2 * s]
        new_cv[old + s] = moved[source[s], 2 * s + 1]


def refill(source, ck, cv, moved):
    shape = jax.ShapeDtypeStruct(ck.shape, ck.dtype)
    whole = pl.BlockSpec(memory_space=pltpu.VMEM)
    anywhere = pl.BlockSpec(memory_space=pl.ANY)
    nq = len(moved)
    return pl.pallas_call(
        functools.partial(refill_kernel, nq),
        out_shape=(shape, shape),
        in_specs=[pl.BlockSpec(memory_space=pltpu.SMEM)] + [whole] * 2 + [anywhere] * nq,
        out_specs=(whole, whole),
        scratch_shapes=[
            pltpu.VMEM((nq,) + moved[0].shape, moved[0].dtype),
            pltpu.SemaphoreType.DMA((nq,)),
        ],
        name="refill",
    )(source, ck, cv, *moved)


def plan(device, per, slots, size, cache_len, span_len, block_table, window):
    old = slots - per
    c = device % NC
    z = device // NC % NZ
    y = device // (NC * NZ)
    ring = jnp.array([-k for k in SHIFTS], jnp.int32)
    q_dev = ((y + ring) % NY * NZ + z) * NC + c
    pair = jnp.arange(NC, dtype=jnp.int32)
    k_dev = ((y * NZ + (z + ring[:, None]) % NZ) * NC + (c + pair[None, :]) % NC).reshape(-1)
    slot = jnp.arange(slots, dtype=jnp.int32)
    step = jnp.arange(per, dtype=jnp.int32)
    q_ids = (q_dev[:, None] * per + step[None, :]).reshape(-1)
    q_request, q_first = block_start(q_ids, span_len, cache_len, size)
    q_window = lookup(window, q_request)
    within = jnp.tile(slot, k_dev.shape[0])
    owner = jnp.repeat(k_dev, slots)
    is_old = within < old
    o_request, o_logical, o_live = slot_owner(block_table, cache_len // size, owner * slots + within)
    n_request, n_first = block_start(
        owner * per + jnp.maximum(within - old, 0), span_len, cache_len, size
    )
    k_request = jnp.where(is_old, o_request, n_request)
    k_first = jnp.where(is_old, o_logical * size, n_first)
    live = jnp.where(is_old, o_live, True)
    last = q_first + size - 1
    seen = (
        live[None, :]
        & (q_request[:, None] == k_request[None, :])
        & (k_first[None, :] <= last[:, None])
        & (
            (k_first[None, :] < SINK)
            | (q_first[:, None] - (k_first[None, :] + size - 1) < q_window[:, None])
        )
    )
    inside = (k_first[None, :] + size - 1 <= q_first[:, None]) & (
        last[:, None] - k_first[None, :] < q_window[:, None]
    )
    total = k_first.shape[0]
    ids = jnp.arange(total, dtype=jnp.int32)
    hits = seen.astype(jnp.int32)
    rim = (seen & ~inside).astype(jnp.int32)
    count = jnp.sum(hits, axis=1)
    rims = jnp.sum(rim, axis=1)
    odd = count % 2
    before = ids[None, None, :] < ids[None, :, None]
    rim_rank = jnp.sum(jnp.where(before, rim[:, None, :], 0), axis=2)
    rank = jnp.sum(jnp.where(before, hits[:, None, :], 0), axis=2)
    rank = odd[:, None] + jnp.where(rim > 0, rim_rank, rims[:, None] + rank - rim_rank)
    at = seen[:, None, :] & (rank[:, None, :] == ids[None, :, None])
    packed = jnp.sum(jnp.where(at, (k_first * total + ids)[None, None, :] + 1, 0), axis=2)
    chosen = jnp.maximum(packed - 1, 0) % total
    first_key = jnp.where(packed > 0, jnp.maximum(packed - 1, 0) // total, FAR)
    edges = (odd + rims + 1) // 2
    targets = table_entry(block_table, n_request, n_first // size)
    wanted = (q_dev[:, None] * slots + old + step[None, :]).reshape(-1)
    hit = (targets[None, :] == wanted[:, None]) & ~is_old[None, :]
    moves = jnp.sum(jnp.where(hit, ids[None, :], 0), axis=1)
    all_new = jnp.arange(NY * NZ * NC * per, dtype=jnp.int32)
    a_request, a_first = block_start(all_new, span_len, cache_len, size)
    a_target = table_entry(block_table, a_request, a_first // size)
    mine = a_target[None, :] == (device * slots + old + step)[:, None]
    from_y = jnp.sum(jnp.where(mine, (all_new // (per * NC * NZ))[None, :], 0), axis=1)
    source = ring_place(from_y - y)
    meta = (
        count,
        chosen.reshape(-1),
        edges,
        first_key.reshape(-1),
        q_first,
        q_window,
        moves,
    )
    return meta, source


def shards(
    queries,
    new_keys,
    new_values,
    cache_keys,
    cache_values,
    out_weight,
    cache_len,
    span_len,
    block_table,
    window,
):
    device = lax.axis_index("blk")
    head = lax.axis_index("head")
    tokens, heads, width = queries.shape
    slots, size = cache_keys.shape[:2]
    per = tokens // size
    log_scale = math.log2(math.e) / math.sqrt(width)
    ck = cache_keys.reshape(slots, size, width)
    cv = cache_values.reshape(slots, size, width)
    own_q = jnp.transpose(queries, (1, 0, 2))
    w_line = [out_weight] + [shift(out_weight, dz=k) for k in SHIFTS[1:]]
    q_near = [shift(own_q, dy=k) for k in SHIFTS[1:3]]
    own_kv = pack(
        ck, cv, new_keys.reshape(per, size, width), new_values.reshape(per, size, width)
    )
    own_kv = after(own_kv, *w_line[1:], *q_near)
    kv_near = [shift(own_kv, dz=k) for k in SHIFTS[1:3]]
    q_parts = [own_q, *q_near, shift(after(own_q, *q_near), dy=SHIFTS[3])]
    w_four = jnp.stack(w_line)
    w_four = after(w_four, q_parts[3])
    w_near = [shift(w_four, dy=k) for k in SHIFTS[1:3]]
    far = [
        shift(kv_near[0][:slots], dz=SHIFTS[1]),
        shift(kv_near[1][slots:], dz=SHIFTS[2]),
    ]
    w_far = [*w_near, shift(after(w_four, *w_near), dy=SHIFTS[3])]
    kv_parts = []
    for part in (own_kv, *kv_near):
        kv_parts += [part, shift(part, dc=1)]
    kv_parts += far + [shift(part, dc=1) for part in far]
    meta, source = plan(device, per, slots, size, cache_len, span_len, block_table, window)
    half = len(SHIFTS) // 2
    late, early = [
        [x[a * x.shape[0] // 2 : (a + 1) * x.shape[0] // 2] for x in meta] for a in range(2)
    ]
    far_outs = attend(early, kv_parts, q_parts[half:], log_scale)
    far_parts = [shift(p, dy=-k) for p, k in zip(far_outs[:half], SHIFTS[half:])]
    late[0] = after(late[0], far_outs[0])
    near_outs = attend(late, kv_parts, q_parts[:half], log_scale)
    parts = [near_outs[0], shift(near_outs[1], dy=-SHIFTS[1])] + far_parts
    moved = near_outs[half:] + far_outs[half:]
    w_parts = []
    for i, part in enumerate((w_four, *w_far)):
        part = after(part, near_outs[0]) if i < 3 else after(part, *parts[1:])
        w_parts += [part, shift(part, dc=1)]
    pieces = piece_table(device, head, heads * width // out_weight.shape[0])
    shares = finish(pieces, [in_hbm(p) for p in parts], w_parts, heads)
    first, second = shares[:NX], shares[NX:]
    first = [first[0]] + [head_shift(p, dx=k) for p, k in zip(first[1:], SHIFTS[1:])]
    moved = list(moved)
    for r in (1, 2):
        moved[r] = shift(after(moved[r], first[1]), dy=-SHIFTS[r])
    moved[3] = shift(after(moved[3], moved[1]), dy=-SHIFTS[3])
    second_sum = second[0].astype(jnp.float32) + head_shift(second[1], dz=1).astype(jnp.float32)
    first_sum = functools.reduce(jnp.add, [p.astype(jnp.float32) for p in first])
    second_sum = after(second_sum, moved[1], moved[2])
    second_far = [
        head_shift(second_sum[r].astype(jnp.bfloat16), dx=SHIFTS[r]) for r in range(1, NX)
    ]
    first_far = head_shift(first_sum[1].astype(jnp.bfloat16), dz=1)
    moved[1] = after(moved[1], first_far)
    new_ck, new_cv = refill(source, ck, cv, moved)
    second_far = lax.optimization_barrier((*second_far, new_ck, new_cv))[: NX - 1]
    second_out = functools.reduce(
        jnp.add, [p.astype(jnp.float32) for p in second_far], second_sum[0]
    )
    first_out = first_sum[0] + first_far.astype(jnp.float32)
    attn_output = jnp.concatenate([first_out, second_out], axis=0).astype(jnp.bfloat16)
    return (
        attn_output,
        new_ck.reshape(cache_keys.shape),
        new_cv.reshape(cache_values.shape),
    )


def solution(mesh):
    placed = (
        P("blk", "head", None),
        P("blk", "head", None),
        P("blk", "head", None),
        P("blk", None, "head", None),
        P("blk", None, "head", None),
        P("blk", "head"),
        P(),
        P(),
        P(),
        P(),
    )
    return jax.shard_map(
        shards,
        mesh=mesh,
        in_specs=placed,
        out_specs=(P("blk", "head"), P("blk", None, "head", None), P("blk", None, "head", None)),
        check_vma=False,
    )
```

```python
import functools
import math

import jax
import jax.numpy as jnp
from jax import lax
from jax.experimental import pallas as pl
from jax.experimental.pallas import tpu as pltpu
from jax.sharding import PartitionSpec as P

NY, NZ, NC = 4, 4, 2
NX, NL = 4, 2
SINK = 4
LOWEST = -1e30
FLOOR = -1e25
FAR = 1 << 29
SHIFTS = (0, 1, -1, 2)


def blk_perm(dy, dz, dc):
    pairs = []
    for y in range(NY):
        for z in range(NZ):
            for c in range(NC):
                src = (y * NZ + z) * NC + c
                dst = ((y + dy) % NY * NZ + (z + dz) % NZ) * NC + (c + dc) % NC
                pairs.append((src, dst))
    return pairs


def shift(value, dy=0, dz=0, dc=0):
    return lax.ppermute(value, "blk", blk_perm(dy, dz, dc))


def after(value, *earlier):
    return lax.optimization_barrier((value, *earlier))[0]


def in_hbm(value):
    return pltpu.with_memory_space_constraint(value, pltpu.HBM)


def head_shift(value, dx=0, dz=0):
    pairs = []
    for x in range(NX):
        for z in range(NL):
            pairs.append((x * NL + z, (x + dx) % NX * NL + (z + dz) % NL))
    return lax.ppermute(value, "head", pairs)


def ring_place(distance):
    distance = distance % len(SHIFTS)
    return jnp.where(distance == 3, 2, jnp.where(distance == 2, 3, distance))


def lookup(table_row, wanted):
    places = jnp.arange(table_row.shape[0], dtype=jnp.int32)
    return jnp.sum(jnp.where(places[None, :] == wanted[:, None], table_row[None, :], 0), axis=1)


def block_start(global_block, span_len, cache_len, block_size):
    lower = jnp.arange(span_len.shape[0], dtype=jnp.int32)
    span_end = jnp.sum(jnp.where(lower[:, None] >= lower[None, :], span_len[None, :], 0), axis=1)
    first_token = global_block * block_size
    request = jnp.sum((first_token[:, None] >= span_end[None, :]).astype(jnp.int32), axis=1)
    return (request, lookup(cache_len - span_end + span_len, request) + first_token)


def table_entry(block_table, request, logical):
    row_ids = jnp.arange(block_table.shape[0], dtype=jnp.int32)
    col_ids = jnp.arange(block_table.shape[1], dtype=jnp.int32)
    match = (row_ids[None, :, None] == request[:, None, None]) & (
        col_ids[None, None, :] == logical[:, None, None]
    )
    return jnp.sum(jnp.where(match, block_table[None], 0), axis=(1, 2))


def slot_owner(block_table, limit, slot_ids):
    row_ids = jnp.arange(block_table.shape[0], dtype=jnp.int32)
    col_ids = jnp.arange(block_table.shape[1], dtype=jnp.int32)
    match = (block_table[None] == slot_ids[:, None, None]) & (
        col_ids[None, None, :] < limit[None, :, None]
    )
    packed = row_ids[:, None] * 4096 + col_ids[None, :] + 1
    found = jnp.sum(jnp.where(match, packed[None], 0), axis=(1, 2))
    place = jnp.maximum(found - 1, 0)
    return (place // 4096, place % 4096, found > 0)


def pack_kernel(ck, cv, nk, nv, out):
    new = nk.shape[0]
    old = ck.shape[0] - new
    out[0:old] = ck[0:old]
    out[old : old + new] = nk[...]
    out[old + new : 2 * old + new] = cv[0:old]
    out[2 * old + new :] = nv[...]


def pack(ck, cv, nk, nv):
    return pl.pallas_call(
        pack_kernel,
        out_shape=jax.ShapeDtypeStruct((2 * ck.shape[0],) + ck.shape[1:], ck.dtype),
        name="pack",
    )(ck, cv, nk, nv)


def attend_kernel(
    log_scale,
    base,
    nkv,
    nq,
    count,
    chosen,
    edges,
    first_key,
    first_query,
    reach,
    moves,
    *refs,
):
    kv_in = refs[:nkv]
    q_in = refs[nkv : nkv + nq]
    out_refs = refs[nkv + nq : nkv + 2 * nq]
    move_refs = refs[nkv + 2 * nq : nkv + 3 * nq]
    kv, queries, scores, high, total, result, in_sem, out_sem, move_sem = refs[nkv + 3 * nq :]
    slots = kv_in[0].shape[0]
    half = slots // 2
    begins = [sum(ref.shape[0] for ref in kv_in[:a]) for a in range(nkv)]
    heads, rows, width = q_in[0].shape
    size = kv_in[0].shape[1]
    per = rows // size
    wide = heads * size
    longest = chosen.shape[0] // count.shape[0]
    loads = []
    for a in range(nkv):
        loads.append(
            pltpu.make_async_copy(
                kv_in[a], kv.at[pl.ds(begins[a], kv_in[a].shape[0])], in_sem.at[a]
            )
        )
    for r in range(nq):
        loads.append(pltpu.make_async_copy(q_in[r], queries.at[r], in_sem.at[nkv + r]))
    for load in loads:
        load.start()
    for load in loads:
        load.wait()

    def place(j):
        return j // half * slots + j % half

    sends = []
    for r in range(nq):
        for s in range(per):
            at = place(moves[(base + r) * per + s])
            for side in range(2):
                sends.append(
                    pltpu.make_async_copy(
                        kv.at[at + side * half],
                        move_refs[r].at[2 * s + side],
                        move_sem.at[(r * per + s) * 2 + side],
                    )
                )
    for send in sends:
        send.start()

    row_ids = lax.broadcasted_iota(jnp.int32, (size, width), 0)
    col_ids = lax.broadcasted_iota(jnp.int32, (size, width), 1)
    ones = jnp.ones((2 * size, width), jnp.bfloat16)

    def one_block(i, unused):
        r = i // per - base
        s = i % per
        begin = pl.multiple_of(s * size, size)
        query = jnp.concatenate(
            [queries[r, h, pl.ds(begin, size), :] for h in range(heads)], axis=0
        )
        pairs = (count[i] + 1) // 2
        high[...] = jnp.full_like(high, LOWEST)

        def raw_scores(t):
            at = i * longest + 2 * t
            keys = jnp.concatenate([kv[place(chosen[at])], kv[place(chosen[at + 1])]], axis=0)
            return lax.dot_general(
                query, keys, (((1,), (1,)), ((), ())), preferred_element_type=jnp.float32
            )

        def score_edge(t, unused):
            raw = raw_scores(t)
            for side in range(2):
                key_pos = first_key[i * longest + 2 * t + side] + col_ids
                distance = first_query[i] + row_ids - key_pos
                allowed = (distance >= 0) & ((distance < reach[i]) | (key_pos < SINK))
                hidden = jnp.where(allowed, 0.0, LOWEST)
                for h in range(heads):
                    lines = slice(h * size, (h + 1) * size)
                    part = raw[lines, side * size : (side + 1) * size]
                    part = jnp.where(hidden < 0.0, LOWEST, part)
                    scores[t, lines, side * size : (side + 1) * size] = part
                    high[lines, :] = jnp.maximum(high[lines, :], part)
            return unused

        def score_full(t, unused):
            raw = raw_scores(t)
            scores[t] = raw
            high[...] = jnp.maximum(high[...], jnp.maximum(raw[:, :size], raw[:, size:]))
            return unused

        lax.fori_loop(0, edges[i], score_edge, 0)
        lax.fori_loop(edges[i], pairs, score_full, 0)
        top = jnp.maximum(jnp.max(high[...], axis=1, keepdims=True), FLOOR)
        high[...] = jnp.broadcast_to(top, high.shape)
        total[...] = jnp.zeros_like(total)

        def blend(t, unused):
            at = i * longest + 2 * t
            values = jnp.concatenate(
                [kv[place(chosen[at]) + half], kv[place(chosen[at + 1]) + half]], axis=0
            )
            values = jnp.concatenate([values, ones], axis=1)
            level = high[...]
            level = jnp.concatenate([level, level], axis=1)
            weights = jnp.exp2((scores[t] - level) * log_scale).astype(jnp.bfloat16)
            total[...] += jnp.dot(weights, values, preferred_element_type=jnp.float32)
            return unused

        lax.fori_loop(0, pairs, blend, 0)
        summed = total[:, width:]
        safe = jnp.where(summed > 0.0, summed, 1.0)
        result[i - base * per, 0:wide, :] = (total[:, :width] / safe).astype(jnp.bfloat16)
        line_ids = lax.broadcasted_iota(jnp.int32, (16, width), 0)
        tops = jnp.zeros((16, width), jnp.float32)
        sums = jnp.zeros((16, width), jnp.float32)
        for h in range(heads):
            lines = slice(h * size, (h + 1) * size)
            row = jnp.sum(jnp.where(row_ids == col_ids, high[lines, :], 0.0), axis=0, keepdims=True)
            tops = jnp.where(line_ids % heads == h, row, tops)
            row = jnp.sum(
                jnp.where(row_ids == col_ids, total[lines, width:], 0.0), axis=0, keepdims=True
            )
            sums = jnp.where(line_ids % heads == h, row, sums)
        live = sums > 0.0
        level = tops * log_scale + jnp.log2(jnp.where(live, sums, 1.0))
        level = jnp.where(live, level, LOWEST)
        first = level.astype(jnp.bfloat16).astype(jnp.float32)
        second = (level - first).astype(jnp.bfloat16).astype(jnp.float32)
        third = level - first - second
        stats = jnp.where(line_ids < heads, first, jnp.where(line_ids < 2 * heads, second, third))
        result[i - base * per, wide : wide + 16, :] = stats.astype(jnp.bfloat16)
        return unused

    backs = []
    for r in reversed(range(nq)):
        lax.fori_loop((base + r) * per, (base + r + 1) * per, one_block, 0)
        backs.append(
            pltpu.make_async_copy(result.at[pl.ds(r * per, per)], out_refs[r], out_sem.at[r])
        )
        backs[-1].start()
    for send in sends:
        send.wait()
    for back in backs:
        back.wait()


def attend(meta, kv_parts, q_parts, log_scale, base):
    _, size, width = kv_parts[0].shape
    heads, rows, _ = q_parts[0].shape
    nkv, nq, per = len(kv_parts), len(q_parts), rows // size
    wide = heads * size
    longest = meta[1].shape[0] // meta[0].shape[0]
    smem = pl.BlockSpec(memory_space=pltpu.SMEM)
    anywhere = pl.BlockSpec(memory_space=pl.ANY)
    parts = jax.ShapeDtypeStruct((per, wide + 16, width), jnp.bfloat16)
    moved = jax.ShapeDtypeStruct((2 * per, size, width), jnp.bfloat16)
    return pl.pallas_call(
        functools.partial(attend_kernel, log_scale, base, nkv, nq),
        out_shape=(parts,) * nq + (moved,) * nq,
        in_specs=[smem] * len(meta) + [anywhere] * (nkv + nq),
        out_specs=(anywhere,) * (2 * nq),
        scratch_shapes=[
            pltpu.VMEM((sum(p.shape[0] for p in kv_parts), size, width), jnp.bfloat16),
            pltpu.VMEM((nq, heads, rows, width), jnp.bfloat16),
            pltpu.VMEM((longest // 2, wide, 2 * size), jnp.float32),
            pltpu.VMEM((wide, size), jnp.float32),
            pltpu.VMEM((wide, 2 * width), jnp.float32),
            pltpu.VMEM((nq * per, wide + 16, width), jnp.bfloat16),
            pltpu.SemaphoreType.DMA((nkv + nq,)),
            pltpu.SemaphoreType.DMA((nq,)),
            pltpu.SemaphoreType.DMA((2 * nq * per,)),
        ],
        compiler_params=pltpu.CompilerParams(vmem_limit_bytes=56 << 20),
        cost_estimate=pl.CostEstimate(
            flops=3_000_000_000 * nq, bytes_accessed=8_000_000, transcendentals=8_000_000
        ),
        name="attend",
    )(*meta, *kv_parts, *q_parts)


def finish_kernel(heads, nparts, nw, pieces, *refs):
    part_in = refs[:nparts]
    w_in = refs[nparts : nparts + nw]
    first_out = refs[nparts + nw : nparts + nw + NX]
    second_out = refs[nparts + nw + NX : nparts + nw + NX + NL]
    parts, weight, mixed_rows, first, second, part_sem, w_sem, a_sem, b_sem = refs[
        nparts + nw + NX + NL :
    ]
    group = w_in[0].shape[0]
    per, lines, width = part_in[0].shape
    size = (lines - 16) // heads
    part_loads = [
        pltpu.make_async_copy(part_in[r], parts.at[r], part_sem.at[r]) for r in range(nparts)
    ]
    w_loads = [
        pltpu.make_async_copy(w_in[a], weight.at[pl.ds(a * group, group)], w_sem.at[a])
        for a in range(nw)
    ]
    for load in part_loads + w_loads:
        load.start()
    for load in part_loads:
        load.wait()
    row_ids = lax.broadcasted_iota(jnp.int32, (size, width), 0)
    col_ids = lax.broadcasted_iota(jnp.int32, (size, width), 1)
    for s in range(per):
        levels = []
        for r in range(nparts):
            stats = parts[r, s, heads * size :, :].astype(jnp.float32)
            levels.append(
                stats[0:heads] + stats[heads : 2 * heads] + stats[2 * heads : 3 * heads]
            )
        top = functools.reduce(jnp.maximum, levels)
        shares = [jnp.exp2(level - top) for level in levels]
        whole = functools.reduce(jnp.add, shares)
        shares = [share / whole for share in shares]
        for h in range(heads):
            mixed = jnp.zeros((size, width), jnp.float32)
            for r in range(nparts):
                spread = jnp.where(row_ids == col_ids, shares[r][h : h + 1, :], 0.0)
                column = jnp.sum(spread, axis=1, keepdims=True)
                mixed += column * parts[r, s, h * size : (h + 1) * size, :].astype(jnp.float32)
            mixed_rows[s * size : (s + 1) * size, h * width : (h + 1) * width] = mixed.astype(
                jnp.bfloat16
            )
    for load in w_loads:
        load.wait()
    sends = []
    for r in reversed(range(NX)):
        for z in range(NL):
            at = (r * NL + z) * group
            rows = jnp.concatenate([weight[pieces[at + q]] for q in range(group)], axis=0)
            product = lax.dot_general(
                mixed_rows[...], rows, (((1,), (1,)), ((), ())), preferred_element_type=jnp.float32
            ).astype(jnp.bfloat16)
            first[r, z] = product[:size]
            second[z, r] = product[size:]
        sends.append(pltpu.make_async_copy(first.at[r], first_out[r], a_sem.at[r]))
        sends[-1].start()
    for z in range(NL):
        sends.append(pltpu.make_async_copy(second.at[z], second_out[z], b_sem.at[z]))
        sends[-1].start()
    for send in sends:
        send.wait()


def finish(pieces, parts, w_parts, heads):
    per, lines, width = parts[0].shape
    size = (lines - 16) // heads
    group, rows, depth = w_parts[0].shape
    columns = group * rows
    nparts, nw = len(parts), len(w_parts)
    anywhere = pl.BlockSpec(memory_space=pl.ANY)
    first = jax.ShapeDtypeStruct((NL, size, columns), jnp.bfloat16)
    second = jax.ShapeDtypeStruct((NX, size, columns), jnp.bfloat16)
    return pl.pallas_call(
        functools.partial(finish_kernel, heads, nparts, nw),
        out_shape=(first,) * NX + (second,) * NL,
        in_specs=[pl.BlockSpec(memory_space=pltpu.SMEM)] + [anywhere] * (nparts + nw),
        out_specs=(anywhere,) * (NX + NL),
        scratch_shapes=[
            pltpu.VMEM((nparts, per, lines, width), jnp.bfloat16),
            pltpu.VMEM((nw * group, rows, depth), jnp.bfloat16),
            pltpu.VMEM((per * size, heads * width), jnp.bfloat16),
            pltpu.VMEM((NX, NL, size, columns), jnp.bfloat16),
            pltpu.VMEM((NL, NX, size, columns), jnp.bfloat16),
            pltpu.SemaphoreType.DMA((nparts,)),
            pltpu.SemaphoreType.DMA((nw,)),
            pltpu.SemaphoreType.DMA((NX,)),
            pltpu.SemaphoreType.DMA((NL,)),
        ],
        compiler_params=pltpu.CompilerParams(vmem_limit_bytes=24 << 20),
        cost_estimate=pl.CostEstimate(
            flops=2_000_000_000, bytes_accessed=12_000_000, transcendentals=10_000
        ),
        name="finish",
    )(pieces, *parts, *w_parts)


def piece_table(device, head, group):
    c = device % NC
    z = device // NC % NZ
    y = device // (NC * NZ)
    steps = jnp.array(SHIFTS, jnp.int32)
    target = (head // NL + steps[:, None]) % NX * NL + (head + jnp.arange(NL)[None, :]) % NL
    owner = (target.reshape(-1)[:, None] * group + jnp.arange(group)[None, :]).reshape(-1)
    place = ring_place(y - owner // (NC * NZ)) * NC + (c + owner) % NC
    return (place * NZ + ring_place(z - owner // NC % NZ)).astype(jnp.int32)


def refill_kernel(nq, source, ck, cv, *refs):
    moved_in = refs[:nq]
    new_ck, new_cv, moved, sem = refs[nq:]
    per = moved_in[0].shape[0] // 2
    old = ck.shape[0] - per
    loads = [pltpu.make_async_copy(moved_in[r], moved.at[r], sem.at[r]) for r in range(nq)]
    for load in loads:
        load.start()
    new_ck[0:old] = ck[0:old]
    new_cv[0:old] = cv[0:old]
    for load in loads:
        load.wait()
    for s in range(per):
        new_ck[old + s] = moved[source[s], 2 * s]
        new_cv[old + s] = moved[source[s], 2 * s + 1]


def refill(source, ck, cv, moved):
    shape = jax.ShapeDtypeStruct(ck.shape, ck.dtype)
    whole = pl.BlockSpec(memory_space=pltpu.VMEM)
    anywhere = pl.BlockSpec(memory_space=pl.ANY)
    nq = len(moved)
    return pl.pallas_call(
        functools.partial(refill_kernel, nq),
        out_shape=(shape, shape),
        in_specs=[pl.BlockSpec(memory_space=pltpu.SMEM)] + [whole] * 2 + [anywhere] * nq,
        out_specs=(whole, whole),
        scratch_shapes=[
            pltpu.VMEM((nq,) + moved[0].shape, moved[0].dtype),
            pltpu.SemaphoreType.DMA((nq,)),
        ],
        name="refill",
    )(source, ck, cv, *moved)


def plan(device, per, slots, size, cache_len, span_len, block_table, window):
    old = slots - per
    c = device % NC
    z = device // NC % NZ
    y = device // (NC * NZ)
    ring = jnp.array([-k for k in SHIFTS], jnp.int32)
    q_dev = ((y + ring) % NY * NZ + z) * NC + c
    pair = jnp.arange(NC, dtype=jnp.int32)
    k_dev = ((y * NZ + (z + ring[:, None]) % NZ) * NC + (c + pair[None, :]) % NC).reshape(-1)
    slot = jnp.arange(slots, dtype=jnp.int32)
    step = jnp.arange(per, dtype=jnp.int32)
    q_ids = (q_dev[:, None] * per + step[None, :]).reshape(-1)
    q_request, q_first = block_start(q_ids, span_len, cache_len, size)
    q_window = lookup(window, q_request)
    within = jnp.tile(slot, k_dev.shape[0])
    owner = jnp.repeat(k_dev, slots)
    is_old = within < old
    o_request, o_logical, o_live = slot_owner(block_table, cache_len // size, owner * slots + within)
    n_request, n_first = block_start(
        owner * per + jnp.maximum(within - old, 0), span_len, cache_len, size
    )
    k_request = jnp.where(is_old, o_request, n_request)
    k_first = jnp.where(is_old, o_logical * size, n_first)
    live = jnp.where(is_old, o_live, True)
    last = q_first + size - 1
    seen = (
        live[None, :]
        & (q_request[:, None] == k_request[None, :])
        & (k_first[None, :] <= last[:, None])
        & (
            (k_first[None, :] < SINK)
            | (q_first[:, None] - (k_first[None, :] + size - 1) < q_window[:, None])
        )
    )
    inside = (k_first[None, :] + size - 1 <= q_first[:, None]) & (
        last[:, None] - k_first[None, :] < q_window[:, None]
    )
    total = k_first.shape[0]
    ids = jnp.arange(total, dtype=jnp.int32)
    hits = seen.astype(jnp.int32)
    rim = (seen & ~inside).astype(jnp.int32)
    count = jnp.sum(hits, axis=1)
    rims = jnp.sum(rim, axis=1)
    odd = count % 2
    before = ids[None, None, :] < ids[None, :, None]
    rim_rank = jnp.sum(jnp.where(before, rim[:, None, :], 0), axis=2)
    rank = jnp.sum(jnp.where(before, hits[:, None, :], 0), axis=2)
    rank = odd[:, None] + jnp.where(rim > 0, rim_rank, rims[:, None] + rank - rim_rank)
    at = seen[:, None, :] & (rank[:, None, :] == ids[None, :, None])
    packed = jnp.sum(jnp.where(at, (k_first * total + ids)[None, None, :] + 1, 0), axis=2)
    chosen = jnp.maximum(packed - 1, 0) % total
    first_key = jnp.where(packed > 0, jnp.maximum(packed - 1, 0) // total, FAR)
    edges = (odd + rims + 1) // 2
    targets = table_entry(block_table, n_request, n_first // size)
    wanted = (q_dev[:, None] * slots + old + step[None, :]).reshape(-1)
    hit = (targets[None, :] == wanted[:, None]) & ~is_old[None, :]
    moves = jnp.sum(jnp.where(hit, ids[None, :], 0), axis=1)
    all_new = jnp.arange(NY * NZ * NC * per, dtype=jnp.int32)
    a_request, a_first = block_start(all_new, span_len, cache_len, size)
    a_target = table_entry(block_table, a_request, a_first // size)
    mine = a_target[None, :] == (device * slots + old + step)[:, None]
    from_y = jnp.sum(jnp.where(mine, (all_new // (per * NC * NZ))[None, :], 0), axis=1)
    source = ring_place(from_y - y)
    meta = (
        count,
        chosen.reshape(-1),
        edges,
        first_key.reshape(-1),
        q_first,
        q_window,
        moves,
    )
    return meta, source


def shards(
    queries,
    new_keys,
    new_values,
    cache_keys,
    cache_values,
    out_weight,
    cache_len,
    span_len,
    block_table,
    window,
):
    device = lax.axis_index("blk")
    head = lax.axis_index("head")
    tokens, heads, width = queries.shape
    slots, size = cache_keys.shape[:2]
    per = tokens // size
    log_scale = math.log2(math.e) / math.sqrt(width)
    ck = cache_keys.reshape(slots, size, width)
    cv = cache_values.reshape(slots, size, width)
    own_q = jnp.transpose(queries, (1, 0, 2))
    w_line = [out_weight] + [shift(out_weight, dz=k) for k in SHIFTS[1:]]
    q_near = [shift(own_q, dy=k) for k in SHIFTS[1:3]]
    own_kv = pack(
        ck, cv, new_keys.reshape(per, size, width), new_values.reshape(per, size, width)
    )
    own_kv = after(own_kv, *w_line[1:], *q_near)
    kv_near = [shift(own_kv, dz=k) for k in SHIFTS[1:3]]
    q_parts = [own_q, *q_near, shift(after(own_q, *q_near), dy=SHIFTS[3])]
    w_four = jnp.stack(w_line)
    w_near = [shift(w_four, dy=k) for k in SHIFTS[1:3]]
    far = [
        shift(kv_near[0][:slots], dz=SHIFTS[1]),
        shift(kv_near[1][slots:], dz=SHIFTS[2]),
    ]
    w_far = [*w_near, shift(after(w_four, *w_near), dy=SHIFTS[3])]
    kv_parts = []
    for part in (own_kv, *kv_near):
        kv_parts += [part, shift(part, dc=1)]
    kv_parts += far + [shift(part, dc=1) for part in far]
    meta, source = plan(device, per, slots, size, cache_len, span_len, block_table, window)
    near = len(SHIFTS) - 1
    early = (after(meta[0], *w_near), *meta[1:])
    far_outs = attend(early, kv_parts, q_parts[near:], log_scale, near)
    far_parts = [shift(far_outs[0], dy=-SHIFTS[near])]
    late = (after(meta[0], far_outs[0]), *meta[1:])
    near_outs = attend(late, kv_parts, q_parts[:near], log_scale, 0)
    parts = [near_outs[0]]
    parts += [shift(p, dy=-k) for p, k in zip(near_outs[1:near], SHIFTS[1:near])] + far_parts
    moved = near_outs[near:] + far_outs[1:]
    w_parts = []
    for i, part in enumerate((w_four, *w_far)):
        part = after(part, near_outs[0]) if i < 3 else after(part, *parts[1:])
        w_parts += [part, shift(part, dc=1)]
    pieces = piece_table(device, head, heads * width // out_weight.shape[0])
    shares = finish(pieces, [in_hbm(p) for p in parts], w_parts, heads)
    first, second = shares[:NX], shares[NX:]
    first = [first[0]] + [head_shift(p, dx=k) for p, k in zip(first[1:], SHIFTS[1:])]
    moved = list(moved)
    for r in (1, 2):
        moved[r] = shift(after(moved[r], first[1]), dy=-SHIFTS[r])
    moved[3] = shift(after(moved[3], moved[1]), dy=-SHIFTS[3])
    second_sum = second[0].astype(jnp.float32) + head_shift(second[1], dz=1).astype(jnp.float32)
    first_sum = functools.reduce(jnp.add, [p.astype(jnp.float32) for p in first])
    second_sum = after(second_sum, moved[1], moved[2])
    second_far = [
        head_shift(second_sum[r].astype(jnp.bfloat16), dx=SHIFTS[r]) for r in range(1, NX)
    ]
    first_far = head_shift(first_sum[1].astype(jnp.bfloat16), dz=1)
    moved[1] = after(moved[1], first_far)
    new_ck, new_cv = refill(source, ck, cv, moved)
    second_far = lax.optimization_barrier((*second_far, new_ck, new_cv))[: NX - 1]
    second_out = functools.reduce(
        jnp.add, [p.astype(jnp.float32) for p in second_far], second_sum[0]
    )
    first_out = first_sum[0] + first_far.astype(jnp.float32)
    attn_output = jnp.concatenate([first_out, second_out], axis=0).astype(jnp.bfloat16)
    return (
        attn_output,
        new_ck.reshape(cache_keys.shape),
        new_cv.reshape(cache_values.shape),
    )


def solution(mesh):
    placed = (
        P("blk", "head", None),
        P("blk", "head", None),
        P("blk", "head", None),
        P("blk", None, "head", None),
        P("blk", None, "head", None),
        P("blk", "head"),
        P(),
        P(),
        P(),
        P(),
    )
    return jax.shard_map(
        shards,
        mesh=mesh,
        in_specs=placed,
        out_specs=(P("blk", "head"), P("blk", None, "head", None), P("blk", None, "head", None)),
        check_vma=False,
    )
```

```python
import functools
import math

import jax
import jax.numpy as jnp
from jax import lax
from jax.experimental import pallas as pl
from jax.experimental.pallas import tpu as pltpu
from jax.sharding import PartitionSpec as P

NY, NZ, NC = 4, 4, 2
NX, NL = 4, 2
SINK = 4
LOWEST = -1e30
FLOOR = -1e25
FAR = 1 << 29
SHIFTS = (0, 1, -1, 2)


def blk_perm(dy, dz, dc):
    pairs = []
    for y in range(NY):
        for z in range(NZ):
            for c in range(NC):
                src = (y * NZ + z) * NC + c
                dst = ((y + dy) % NY * NZ + (z + dz) % NZ) * NC + (c + dc) % NC
                pairs.append((src, dst))
    return pairs


def shift(value, dy=0, dz=0, dc=0):
    return lax.ppermute(value, "blk", blk_perm(dy, dz, dc))


def after(value, *earlier):
    return lax.optimization_barrier((value, *earlier))[0]


def in_hbm(value):
    return pltpu.with_memory_space_constraint(value, pltpu.HBM)


def head_shift(value, dx=0, dz=0):
    pairs = []
    for x in range(NX):
        for z in range(NL):
            pairs.append((x * NL + z, (x + dx) % NX * NL + (z + dz) % NL))
    return lax.ppermute(value, "head", pairs)


def ring_place(distance):
    distance = distance % len(SHIFTS)
    return jnp.where(distance == 3, 2, jnp.where(distance == 2, 3, distance))


def lookup(table_row, wanted):
    places = jnp.arange(table_row.shape[0], dtype=jnp.int32)
    return jnp.sum(jnp.where(places[None, :] == wanted[:, None], table_row[None, :], 0), axis=1)


def block_start(global_block, span_len, cache_len, block_size):
    lower = jnp.arange(span_len.shape[0], dtype=jnp.int32)
    span_end = jnp.sum(jnp.where(lower[:, None] >= lower[None, :], span_len[None, :], 0), axis=1)
    first_token = global_block * block_size
    request = jnp.sum((first_token[:, None] >= span_end[None, :]).astype(jnp.int32), axis=1)
    return (request, lookup(cache_len - span_end + span_len, request) + first_token)


def table_entry(block_table, request, logical):
    row_ids = jnp.arange(block_table.shape[0], dtype=jnp.int32)
    col_ids = jnp.arange(block_table.shape[1], dtype=jnp.int32)
    match = (row_ids[None, :, None] == request[:, None, None]) & (
        col_ids[None, None, :] == logical[:, None, None]
    )
    return jnp.sum(jnp.where(match, block_table[None], 0), axis=(1, 2))


def slot_owner(block_table, limit, slot_ids):
    row_ids = jnp.arange(block_table.shape[0], dtype=jnp.int32)
    col_ids = jnp.arange(block_table.shape[1], dtype=jnp.int32)
    match = (block_table[None] == slot_ids[:, None, None]) & (
        col_ids[None, None, :] < limit[None, :, None]
    )
    packed = row_ids[:, None] * 4096 + col_ids[None, :] + 1
    found = jnp.sum(jnp.where(match, packed[None], 0), axis=(1, 2))
    place = jnp.maximum(found - 1, 0)
    return (place // 4096, place % 4096, found > 0)


def pack_kernel(ck, cv, nk, nv, out):
    new = nk.shape[0]
    old = ck.shape[0] - new
    out[0:old] = ck[0:old]
    out[old : old + new] = nk[...]
    out[old + new : 2 * old + new] = cv[0:old]
    out[2 * old + new :] = nv[...]


def pack(ck, cv, nk, nv):
    return pl.pallas_call(
        pack_kernel,
        out_shape=jax.ShapeDtypeStruct((2 * ck.shape[0],) + ck.shape[1:], ck.dtype),
        name="pack",
    )(ck, cv, nk, nv)


def attend_kernel(
    log_scale,
    nkv,
    nq,
    count,
    chosen,
    edges,
    first_key,
    first_query,
    reach,
    moves,
    *refs,
):
    kv_in = refs[:nkv]
    q_in = refs[nkv : nkv + nq]
    out_refs = refs[nkv + nq : nkv + 2 * nq]
    move_refs = refs[nkv + 2 * nq : nkv + 3 * nq]
    kv, queries, scores, high, total, result, in_sem, out_sem, move_sem = refs[nkv + 3 * nq :]
    slots = kv_in[0].shape[0]
    half = slots // 2
    begins = [sum(ref.shape[0] for ref in kv_in[:a]) for a in range(nkv)]
    heads, rows, width = q_in[0].shape
    size = kv_in[0].shape[1]
    per = rows // size
    wide = heads * size
    longest = chosen.shape[0] // (nq * per)
    loads = []
    for a in range(nkv):
        loads.append(
            pltpu.make_async_copy(
                kv_in[a], kv.at[pl.ds(begins[a], kv_in[a].shape[0])], in_sem.at[a]
            )
        )
    for r in range(nq):
        loads.append(pltpu.make_async_copy(q_in[r], queries.at[r], in_sem.at[nkv + r]))
    for load in loads:
        load.start()
    for load in loads:
        load.wait()

    def place(j):
        return j // half * slots + j % half

    sends = []
    for r in range(nq):
        for s in range(per):
            at = place(moves[r * per + s])
            for side in range(2):
                sends.append(
                    pltpu.make_async_copy(
                        kv.at[at + side * half],
                        move_refs[r].at[2 * s + side],
                        move_sem.at[(r * per + s) * 2 + side],
                    )
                )
    for send in sends:
        send.start()

    row_ids = lax.broadcasted_iota(jnp.int32, (size, width), 0)
    col_ids = lax.broadcasted_iota(jnp.int32, (size, width), 1)
    ones = jnp.ones((2 * size, width), jnp.bfloat16)

    def one_block(i, unused):
        r = i // per
        s = i % per
        begin = pl.multiple_of(s * size, size)
        query = jnp.concatenate(
            [queries[r, h, pl.ds(begin, size), :] for h in range(heads)], axis=0
        )
        pairs = (count[i] + 1) // 2
        high[...] = jnp.full_like(high, LOWEST)

        def raw_scores(t):
            at = i * longest + 2 * t
            keys = jnp.concatenate([kv[place(chosen[at])], kv[place(chosen[at + 1])]], axis=0)
            return lax.dot_general(
                query, keys, (((1,), (1,)), ((), ())), preferred_element_type=jnp.float32
            )

        def score_edge(t, unused):
            raw = raw_scores(t)
            for side in range(2):
                key_pos = first_key[i * longest + 2 * t + side] + col_ids
                distance = first_query[i] + row_ids - key_pos
                allowed = (distance >= 0) & ((distance < reach[i]) | (key_pos < SINK))
                hidden = jnp.where(allowed, 0.0, LOWEST)
                for h in range(heads):
                    lines = slice(h * size, (h + 1) * size)
                    part = raw[lines, side * size : (side + 1) * size]
                    part = jnp.where(hidden < 0.0, LOWEST, part)
                    scores[t, lines, side * size : (side + 1) * size] = part
                    high[lines, :] = jnp.maximum(high[lines, :], part)
            return unused

        def score_full(t, unused):
            raw = raw_scores(t)
            scores[t] = raw
            high[...] = jnp.maximum(high[...], jnp.maximum(raw[:, :size], raw[:, size:]))
            return unused

        def score_two(u, unused):
            t = edges[i] + 2 * u
            one = raw_scores(t)
            two = raw_scores(t + 1)
            scores[t] = one
            scores[t + 1] = two
            best = jnp.maximum(
                jnp.maximum(one[:, :size], one[:, size:]),
                jnp.maximum(two[:, :size], two[:, size:]),
            )
            high[...] = jnp.maximum(high[...], best)
            return unused

        lax.fori_loop(0, edges[i], score_edge, 0)
        lax.fori_loop(0, (pairs - edges[i]) // 2, score_two, 0)
        lax.fori_loop(pairs - (pairs - edges[i]) % 2, pairs, score_full, 0)
        top = jnp.maximum(jnp.max(high[...], axis=1, keepdims=True), FLOOR)
        high[...] = jnp.broadcast_to(top, high.shape)
        total[...] = jnp.zeros_like(total)

        def product(t):
            at = i * longest + 2 * t
            values = jnp.concatenate(
                [kv[place(chosen[at]) + half], kv[place(chosen[at + 1]) + half]], axis=0
            )
            values = jnp.concatenate([values, ones], axis=1)
            level = high[...]
            level = jnp.concatenate([level, level], axis=1)
            weights = jnp.exp2((scores[t] - level) * log_scale).astype(jnp.bfloat16)
            return jnp.dot(weights, values, preferred_element_type=jnp.float32)

        def blend(t, unused):
            total[...] += product(t)
            return unused

        def blend_two(u, unused):
            total[...] += product(2 * u) + product(2 * u + 1)
            return unused

        lax.fori_loop(0, pairs // 2, blend_two, 0)
        lax.fori_loop(pairs - pairs % 2, pairs, blend, 0)
        summed = total[:, width:]
        safe = jnp.where(summed > 0.0, summed, 1.0)
        result[i, 0:wide, :] = (total[:, :width] / safe).astype(jnp.bfloat16)
        line_ids = lax.broadcasted_iota(jnp.int32, (16, width), 0)
        tops = jnp.zeros((16, width), jnp.float32)
        sums = jnp.zeros((16, width), jnp.float32)
        for h in range(heads):
            lines = slice(h * size, (h + 1) * size)
            row = jnp.sum(jnp.where(row_ids == col_ids, high[lines, :], 0.0), axis=0, keepdims=True)
            tops = jnp.where(line_ids % heads == h, row, tops)
            row = jnp.sum(
                jnp.where(row_ids == col_ids, total[lines, width:], 0.0), axis=0, keepdims=True
            )
            sums = jnp.where(line_ids % heads == h, row, sums)
        live = sums > 0.0
        level = tops * log_scale + jnp.log2(jnp.where(live, sums, 1.0))
        level = jnp.where(live, level, LOWEST)
        first = level.astype(jnp.bfloat16).astype(jnp.float32)
        second = (level - first).astype(jnp.bfloat16).astype(jnp.float32)
        third = level - first - second
        stats = jnp.where(line_ids < heads, first, jnp.where(line_ids < 2 * heads, second, third))
        result[i, wide : wide + 16, :] = stats.astype(jnp.bfloat16)
        return unused

    backs = []
    for r in reversed(range(nq)):
        lax.fori_loop(r * per, (r + 1) * per, one_block, 0)
        backs.append(
            pltpu.make_async_copy(result.at[pl.ds(r * per, per)], out_refs[r], out_sem.at[r])
        )
        backs[-1].start()
    for send in sends:
        send.wait()
    for back in backs:
        back.wait()


def attend(meta, kv_parts, q_parts, log_scale):
    _, size, width = kv_parts[0].shape
    heads, rows, _ = q_parts[0].shape
    nkv, nq, per = len(kv_parts), len(q_parts), rows // size
    wide = heads * size
    longest = meta[1].shape[0] // (nq * per)
    smem = pl.BlockSpec(memory_space=pltpu.SMEM)
    anywhere = pl.BlockSpec(memory_space=pl.ANY)
    parts = jax.ShapeDtypeStruct((per, wide + 16, width), jnp.bfloat16)
    moved = jax.ShapeDtypeStruct((2 * per, size, width), jnp.bfloat16)
    return pl.pallas_call(
        functools.partial(attend_kernel, log_scale, nkv, nq),
        out_shape=(parts,) * nq + (moved,) * nq,
        in_specs=[smem] * len(meta) + [anywhere] * (nkv + nq),
        out_specs=(anywhere,) * (2 * nq),
        scratch_shapes=[
            pltpu.VMEM((sum(p.shape[0] for p in kv_parts), size, width), jnp.bfloat16),
            pltpu.VMEM((nq, heads, rows, width), jnp.bfloat16),
            pltpu.VMEM((longest // 2, wide, 2 * size), jnp.float32),
            pltpu.VMEM((wide, size), jnp.float32),
            pltpu.VMEM((wide, 2 * width), jnp.float32),
            pltpu.VMEM((nq * per, wide + 16, width), jnp.bfloat16),
            pltpu.SemaphoreType.DMA((nkv + nq,)),
            pltpu.SemaphoreType.DMA((nq,)),
            pltpu.SemaphoreType.DMA((2 * nq * per,)),
        ],
        compiler_params=pltpu.CompilerParams(vmem_limit_bytes=56 << 20),
        cost_estimate=pl.CostEstimate(
            flops=5_000_000_000, bytes_accessed=8_000_000, transcendentals=8_000_000
        ),
        name="attend",
    )(*meta, *kv_parts, *q_parts)


def finish_kernel(heads, nparts, nw, pieces, *refs):
    part_in = refs[:nparts]
    w_in = refs[nparts : nparts + nw]
    first_out = refs[nparts + nw : nparts + nw + NX]
    second_out = refs[nparts + nw + NX : nparts + nw + NX + NL]
    parts, weight, mixed_rows, first, second, part_sem, w_sem, a_sem, b_sem = refs[
        nparts + nw + NX + NL :
    ]
    group = w_in[0].shape[0]
    per, lines, width = part_in[0].shape
    size = (lines - 16) // heads
    part_loads = [
        pltpu.make_async_copy(part_in[r], parts.at[r], part_sem.at[r]) for r in range(nparts)
    ]
    w_loads = [
        pltpu.make_async_copy(w_in[a], weight.at[pl.ds(a * group, group)], w_sem.at[a])
        for a in range(nw)
    ]
    for load in part_loads + w_loads:
        load.start()
    for load in part_loads:
        load.wait()
    row_ids = lax.broadcasted_iota(jnp.int32, (size, width), 0)
    col_ids = lax.broadcasted_iota(jnp.int32, (size, width), 1)
    for s in range(per):
        levels = []
        for r in range(nparts):
            stats = parts[r, s, heads * size :, :].astype(jnp.float32)
            levels.append(
                stats[0:heads] + stats[heads : 2 * heads] + stats[2 * heads : 3 * heads]
            )
        top = functools.reduce(jnp.maximum, levels)
        shares = [jnp.exp2(level - top) for level in levels]
        whole = functools.reduce(jnp.add, shares)
        shares = [share / whole for share in shares]
        for h in range(heads):
            mixed = jnp.zeros((size, width), jnp.float32)
            for r in range(nparts):
                spread = jnp.where(row_ids == col_ids, shares[r][h : h + 1, :], 0.0)
                column = jnp.sum(spread, axis=1, keepdims=True)
                mixed += column * parts[r, s, h * size : (h + 1) * size, :].astype(jnp.float32)
            mixed_rows[s * size : (s + 1) * size, h * width : (h + 1) * width] = mixed.astype(
                jnp.bfloat16
            )
    for load in w_loads:
        load.wait()
    sends = []
    for r in reversed(range(NX)):
        for z in range(NL):
            at = (r * NL + z) * group
            rows = jnp.concatenate([weight[pieces[at + q]] for q in range(group)], axis=0)
            product = lax.dot_general(
                mixed_rows[...], rows, (((1,), (1,)), ((), ())), preferred_element_type=jnp.float32
            ).astype(jnp.bfloat16)
            first[r, z] = product[:size]
            second[z, r] = product[size:]
        sends.append(pltpu.make_async_copy(first.at[r], first_out[r], a_sem.at[r]))
        sends[-1].start()
    for z in range(NL):
        sends.append(pltpu.make_async_copy(second.at[z], second_out[z], b_sem.at[z]))
        sends[-1].start()
    for send in sends:
        send.wait()


def finish(pieces, parts, w_parts, heads):
    per, lines, width = parts[0].shape
    size = (lines - 16) // heads
    group, rows, depth = w_parts[0].shape
    columns = group * rows
    nparts, nw = len(parts), len(w_parts)
    anywhere = pl.BlockSpec(memory_space=pl.ANY)
    first = jax.ShapeDtypeStruct((NL, size, columns), jnp.bfloat16)
    second = jax.ShapeDtypeStruct((NX, size, columns), jnp.bfloat16)
    return pl.pallas_call(
        functools.partial(finish_kernel, heads, nparts, nw),
        out_shape=(first,) * NX + (second,) * NL,
        in_specs=[pl.BlockSpec(memory_space=pltpu.SMEM)] + [anywhere] * (nparts + nw),
        out_specs=(anywhere,) * (NX + NL),
        scratch_shapes=[
            pltpu.VMEM((nparts, per, lines, width), jnp.bfloat16),
            pltpu.VMEM((nw * group, rows, depth), jnp.bfloat16),
            pltpu.VMEM((per * size, heads * width), jnp.bfloat16),
            pltpu.VMEM((NX, NL, size, columns), jnp.bfloat16),
            pltpu.VMEM((NL, NX, size, columns), jnp.bfloat16),
            pltpu.SemaphoreType.DMA((nparts,)),
            pltpu.SemaphoreType.DMA((nw,)),
            pltpu.SemaphoreType.DMA((NX,)),
            pltpu.SemaphoreType.DMA((NL,)),
        ],
        compiler_params=pltpu.CompilerParams(vmem_limit_bytes=24 << 20),
        cost_estimate=pl.CostEstimate(
            flops=2_000_000_000, bytes_accessed=12_000_000, transcendentals=10_000
        ),
        name="finish",
    )(pieces, *parts, *w_parts)


def piece_table(device, head, group):
    c = device % NC
    z = device // NC % NZ
    y = device // (NC * NZ)
    steps = jnp.array(SHIFTS, jnp.int32)
    target = (head // NL + steps[:, None]) % NX * NL + (head + jnp.arange(NL)[None, :]) % NL
    owner = (target.reshape(-1)[:, None] * group + jnp.arange(group)[None, :]).reshape(-1)
    place = ring_place(y - owner // (NC * NZ)) * NC + (c + owner) % NC
    return (place * NZ + ring_place(z - owner // NC % NZ)).astype(jnp.int32)


def refill_kernel(nq, source, ck, cv, *refs):
    moved_in = refs[:nq]
    new_ck, new_cv, moved, sem = refs[nq:]
    per = moved_in[0].shape[0] // 2
    old = ck.shape[0] - per
    loads = [pltpu.make_async_copy(moved_in[r], moved.at[r], sem.at[r]) for r in range(nq)]
    for load in loads:
        load.start()
    new_ck[0:old] = ck[0:old]
    new_cv[0:old] = cv[0:old]
    for load in loads:
        load.wait()
    for s in range(per):
        new_ck[old + s] = moved[source[s], 2 * s]
        new_cv[old + s] = moved[source[s], 2 * s + 1]


def refill(source, ck, cv, moved):
    shape = jax.ShapeDtypeStruct(ck.shape, ck.dtype)
    whole = pl.BlockSpec(memory_space=pltpu.VMEM)
    anywhere = pl.BlockSpec(memory_space=pl.ANY)
    nq = len(moved)
    return pl.pallas_call(
        functools.partial(refill_kernel, nq),
        out_shape=(shape, shape),
        in_specs=[pl.BlockSpec(memory_space=pltpu.SMEM)] + [whole] * 2 + [anywhere] * nq,
        out_specs=(whole, whole),
        scratch_shapes=[
            pltpu.VMEM((nq,) + moved[0].shape, moved[0].dtype),
            pltpu.SemaphoreType.DMA((nq,)),
        ],
        name="refill",
    )(source, ck, cv, *moved)


def plan(device, per, slots, size, cache_len, span_len, block_table, window):
    old = slots - per
    c = device % NC
    z = device // NC % NZ
    y = device // (NC * NZ)
    ring = jnp.array([-k for k in SHIFTS], jnp.int32)
    q_dev = ((y + ring) % NY * NZ + z) * NC + c
    pair = jnp.arange(NC, dtype=jnp.int32)
    k_dev = ((y * NZ + (z + ring[:, None]) % NZ) * NC + (c + pair[None, :]) % NC).reshape(-1)
    slot = jnp.arange(slots, dtype=jnp.int32)
    step = jnp.arange(per, dtype=jnp.int32)
    q_ids = (q_dev[:, None] * per + step[None, :]).reshape(-1)
    q_request, q_first = block_start(q_ids, span_len, cache_len, size)
    q_window = lookup(window, q_request)
    within = jnp.tile(slot, k_dev.shape[0])
    owner = jnp.repeat(k_dev, slots)
    is_old = within < old
    o_request, o_logical, o_live = slot_owner(block_table, cache_len // size, owner * slots + within)
    n_request, n_first = block_start(
        owner * per + jnp.maximum(within - old, 0), span_len, cache_len, size
    )
    k_request = jnp.where(is_old, o_request, n_request)
    k_first = jnp.where(is_old, o_logical * size, n_first)
    live = jnp.where(is_old, o_live, True)
    last = q_first + size - 1
    seen = (
        live[None, :]
        & (q_request[:, None] == k_request[None, :])
        & (k_first[None, :] <= last[:, None])
        & (
            (k_first[None, :] < SINK)
            | (q_first[:, None] - (k_first[None, :] + size - 1) < q_window[:, None])
        )
    )
    inside = (k_first[None, :] + size - 1 <= q_first[:, None]) & (
        last[:, None] - k_first[None, :] < q_window[:, None]
    )
    total = k_first.shape[0]
    ids = jnp.arange(total, dtype=jnp.int32)
    hits = seen.astype(jnp.int32)
    rim = (seen & ~inside).astype(jnp.int32)
    count = jnp.sum(hits, axis=1)
    rims = jnp.sum(rim, axis=1)
    odd = count % 2
    before = ids[None, None, :] < ids[None, :, None]
    rim_rank = jnp.sum(jnp.where(before, rim[:, None, :], 0), axis=2)
    rank = jnp.sum(jnp.where(before, hits[:, None, :], 0), axis=2)
    rank = odd[:, None] + jnp.where(rim > 0, rim_rank, rims[:, None] + rank - rim_rank)
    at = seen[:, None, :] & (rank[:, None, :] == ids[None, :, None])
    packed = jnp.sum(jnp.where(at, (k_first * total + ids)[None, None, :] + 1, 0), axis=2)
    chosen = jnp.maximum(packed - 1, 0) % total
    first_key = jnp.where(packed > 0, jnp.maximum(packed - 1, 0) // total, FAR)
    edges = (odd + rims + 1) // 2
    targets = table_entry(block_table, n_request, n_first // size)
    wanted = (q_dev[:, None] * slots + old + step[None, :]).reshape(-1)
    hit = (targets[None, :] == wanted[:, None]) & ~is_old[None, :]
    moves = jnp.sum(jnp.where(hit, ids[None, :], 0), axis=1)
    all_new = jnp.arange(NY * NZ * NC * per, dtype=jnp.int32)
    a_request, a_first = block_start(all_new, span_len, cache_len, size)
    a_target = table_entry(block_table, a_request, a_first // size)
    mine = a_target[None, :] == (device * slots + old + step)[:, None]
    from_y = jnp.sum(jnp.where(mine, (all_new // (per * NC * NZ))[None, :], 0), axis=1)
    source = ring_place(from_y - y)
    meta = (
        count,
        chosen.reshape(-1),
        edges,
        first_key.reshape(-1),
        q_first,
        q_window,
        moves,
    )
    return meta, source


def shards(
    queries,
    new_keys,
    new_values,
    cache_keys,
    cache_values,
    out_weight,
    cache_len,
    span_len,
    block_table,
    window,
):
    device = lax.axis_index("blk")
    head = lax.axis_index("head")
    tokens, heads, width = queries.shape
    slots, size = cache_keys.shape[:2]
    per = tokens // size
    log_scale = math.log2(math.e) / math.sqrt(width)
    ck = cache_keys.reshape(slots, size, width)
    cv = cache_values.reshape(slots, size, width)
    own_q = jnp.transpose(queries, (1, 0, 2))
    w_line = [out_weight] + [shift(out_weight, dz=k) for k in SHIFTS[1:]]
    q_near = [shift(own_q, dy=k) for k in SHIFTS[1:3]]
    own_kv = pack(
        ck, cv, new_keys.reshape(per, size, width), new_values.reshape(per, size, width)
    )
    own_kv = after(own_kv, *w_line[1:], *q_near)
    kv_near = [shift(own_kv, dz=k) for k in SHIFTS[1:3]]
    q_parts = [own_q, *q_near, shift(after(own_q, *q_near), dy=SHIFTS[3])]
    w_four = jnp.stack(w_line)
    w_four = after(w_four, q_parts[3])
    w_near = [shift(w_four, dy=k) for k in SHIFTS[1:3]]
    far = [
        shift(kv_near[0][:slots], dz=SHIFTS[1]),
        shift(kv_near[1][slots:], dz=SHIFTS[2]),
    ]
    w_far = [*w_near, shift(after(w_four, *w_near), dy=SHIFTS[3])]
    kv_parts = []
    for part in (own_kv, *kv_near):
        kv_parts += [part, shift(part, dc=1)]
    kv_parts += far + [shift(part, dc=1) for part in far]
    w_parts = []
    for part in (w_four, *w_near):
        w_parts += [part, shift(part, dc=1)]
    meta, source = plan(device, per, slots, size, cache_len, span_len, block_table, window)
    outs = attend(meta, kv_parts, q_parts, log_scale)
    parts, moved = outs[: len(SHIFTS)], outs[len(SHIFTS) :]
    parts = [parts[0]] + [shift(p, dy=-k) for p, k in zip(parts[1:], SHIFTS[1:])]
    w_far[2] = after(w_far[2], *parts[1:])
    w_parts += [w_far[2], shift(w_far[2], dc=1)]
    pieces = piece_table(device, head, heads * width // out_weight.shape[0])
    shares = finish(pieces, [in_hbm(p) for p in parts], w_parts, heads)
    first, second = shares[:NX], shares[NX:]
    first = [first[0]] + [head_shift(p, dx=k) for p, k in zip(first[1:], SHIFTS[1:])]
    moved = list(moved)
    for r in (1, 2):
        moved[r] = shift(after(moved[r], first[1]), dy=-SHIFTS[r])
    moved[3] = shift(after(moved[3], moved[1]), dy=-SHIFTS[3])
    second_sum = second[0].astype(jnp.float32) + head_shift(second[1], dz=1).astype(jnp.float32)
    first_sum = functools.reduce(jnp.add, [p.astype(jnp.float32) for p in first])
    second_sum = after(second_sum, moved[1], moved[2])
    second_far = [
        head_shift(second_sum[r].astype(jnp.bfloat16), dx=SHIFTS[r]) for r in range(1, NX)
    ]
    second_out = functools.reduce(
        jnp.add, [p.astype(jnp.float32) for p in second_far], second_sum[0]
    )
    first_out = first_sum[0] + head_shift(first_sum[1].astype(jnp.bfloat16), dz=1).astype(
        jnp.float32
    )
    attn_output = jnp.concatenate([first_out, second_out], axis=0).astype(jnp.bfloat16)
    moved[1] = after(moved[1], second_far[0])
    new_ck, new_cv = refill(source, ck, cv, moved)
    return (
        attn_output,
        new_ck.reshape(cache_keys.shape),
        new_cv.reshape(cache_values.shape),
    )


def solution(mesh):
    placed = (
        P("blk", "head", None),
        P("blk", "head", None),
        P("blk", "head", None),
        P("blk", None, "head", None),
        P("blk", None, "head", None),
        P("blk", "head"),
        P(),
        P(),
        P(),
        P(),
    )
    return jax.shard_map(
        shards,
        mesh=mesh,
        in_specs=placed,
        out_specs=(P("blk", "head"), P("blk", None, "head", None), P("blk", None, "head", None)),
        check_vma=False,
    )
```

```python
import functools
import math

import jax
import jax.numpy as jnp
from jax import lax
from jax.experimental import pallas as pl
from jax.experimental.pallas import tpu as pltpu
from jax.sharding import PartitionSpec as P

NY, NZ, NC = 4, 4, 2
NX, NL = 4, 2
SINK = 4
LOWEST = -1e30
FLOOR = -1e25
FAR = 1 << 29
SHIFTS = (0, 1, -1, 2)


def blk_perm(dy, dz, dc):
    pairs = []
    for y in range(NY):
        for z in range(NZ):
            for c in range(NC):
                src = (y * NZ + z) * NC + c
                dst = ((y + dy) % NY * NZ + (z + dz) % NZ) * NC + (c + dc) % NC
                pairs.append((src, dst))
    return pairs


def shift(value, dy=0, dz=0, dc=0):
    return lax.ppermute(value, "blk", blk_perm(dy, dz, dc))


def after(value, *earlier):
    return lax.optimization_barrier((value, *earlier))[0]


def in_hbm(value):
    return pltpu.with_memory_space_constraint(value, pltpu.HBM)


def head_shift(value, dx=0, dz=0):
    pairs = []
    for x in range(NX):
        for z in range(NL):
            pairs.append((x * NL + z, (x + dx) % NX * NL + (z + dz) % NL))
    return lax.ppermute(value, "head", pairs)


def ring_place(distance):
    distance = distance % len(SHIFTS)
    return jnp.where(distance == 3, 2, jnp.where(distance == 2, 3, distance))


def lookup(table_row, wanted):
    places = jnp.arange(table_row.shape[0], dtype=jnp.int32)
    return jnp.sum(jnp.where(places[None, :] == wanted[:, None], table_row[None, :], 0), axis=1)


def block_start(global_block, span_len, cache_len, block_size):
    lower = jnp.arange(span_len.shape[0], dtype=jnp.int32)
    span_end = jnp.sum(jnp.where(lower[:, None] >= lower[None, :], span_len[None, :], 0), axis=1)
    first_token = global_block * block_size
    request = jnp.sum((first_token[:, None] >= span_end[None, :]).astype(jnp.int32), axis=1)
    return (request, lookup(cache_len - span_end + span_len, request) + first_token)


def table_entry(block_table, request, logical):
    row_ids = jnp.arange(block_table.shape[0], dtype=jnp.int32)
    col_ids = jnp.arange(block_table.shape[1], dtype=jnp.int32)
    match = (row_ids[None, :, None] == request[:, None, None]) & (
        col_ids[None, None, :] == logical[:, None, None]
    )
    return jnp.sum(jnp.where(match, block_table[None], 0), axis=(1, 2))


def slot_owner(block_table, limit, slot_ids):
    row_ids = jnp.arange(block_table.shape[0], dtype=jnp.int32)
    col_ids = jnp.arange(block_table.shape[1], dtype=jnp.int32)
    match = (block_table[None] == slot_ids[:, None, None]) & (
        col_ids[None, None, :] < limit[None, :, None]
    )
    packed = row_ids[:, None] * 4096 + col_ids[None, :] + 1
    found = jnp.sum(jnp.where(match, packed[None], 0), axis=(1, 2))
    place = jnp.maximum(found - 1, 0)
    return (place // 4096, place % 4096, found > 0)


def pack_kernel(ck, cv, nk, nv, out):
    new = nk.shape[0]
    old = ck.shape[0] - new
    out[0:old] = ck[0:old]
    out[old : old + new] = nk[...]
    out[old + new : 2 * old + new] = cv[0:old]
    out[2 * old + new :] = nv[...]


def pack(ck, cv, nk, nv):
    return pl.pallas_call(
        pack_kernel,
        out_shape=jax.ShapeDtypeStruct((2 * ck.shape[0],) + ck.shape[1:], ck.dtype),
        name="pack",
    )(ck, cv, nk, nv)


def attend_kernel(
    log_scale,
    nkv,
    nq,
    count,
    chosen,
    edges,
    first_key,
    first_query,
    reach,
    moves,
    *refs,
):
    kv_in = refs[:nkv]
    q_in = refs[nkv : nkv + nq]
    out_refs = refs[nkv + nq : nkv + 2 * nq]
    move_refs = refs[nkv + 2 * nq : nkv + 3 * nq]
    kv, queries, scores, high, total, result, in_sem, out_sem, move_sem = refs[nkv + 3 * nq :]
    slots = kv_in[0].shape[0]
    half = slots // 2
    begins = [sum(ref.shape[0] for ref in kv_in[:a]) for a in range(nkv)]
    heads, rows, width = q_in[0].shape
    size = kv_in[0].shape[1]
    per = rows // size
    wide = heads * size
    longest = chosen.shape[0] // (nq * per)
    loads = []
    for a in range(nkv):
        loads.append(
            pltpu.make_async_copy(
                kv_in[a], kv.at[pl.ds(begins[a], kv_in[a].shape[0])], in_sem.at[a]
            )
        )
    for r in range(nq):
        loads.append(pltpu.make_async_copy(q_in[r], queries.at[r], in_sem.at[nkv + r]))
    for load in loads:
        load.start()
    for load in loads:
        load.wait()

    def place(j):
        return j // half * slots + j % half

    sends = []
    for r in range(nq):
        for s in range(per):
            at = place(moves[r * per + s])
            for side in range(2):
                sends.append(
                    pltpu.make_async_copy(
                        kv.at[at + side * half],
                        move_refs[r].at[2 * s + side],
                        move_sem.at[(r * per + s) * 2 + side],
                    )
                )
    for send in sends:
        send.start()

    row_ids = lax.broadcasted_iota(jnp.int32, (size, width), 0)
    col_ids = lax.broadcasted_iota(jnp.int32, (size, width), 1)
    ones = jnp.ones((2 * size, width), jnp.bfloat16)

    def one_block(i, unused):
        r = i // per
        s = i % per
        begin = pl.multiple_of(s * size, size)
        query = jnp.concatenate(
            [queries[r, h, pl.ds(begin, size), :] for h in range(heads)], axis=0
        )
        pairs = (count[i] + 1) // 2
        high[...] = jnp.full_like(high, LOWEST)

        def raw_scores(t):
            at = i * longest + 2 * t
            keys = jnp.concatenate([kv[place(chosen[at])], kv[place(chosen[at + 1])]], axis=0)
            return lax.dot_general(
                query, keys, (((1,), (1,)), ((), ())), preferred_element_type=jnp.float32
            )

        def score_edge(t, unused):
            raw = raw_scores(t)
            for side in range(2):
                key_pos = first_key[i * longest + 2 * t + side] + col_ids
                distance = first_query[i] + row_ids - key_pos
                allowed = (distance >= 0) & ((distance < reach[i]) | (key_pos < SINK))
                hidden = jnp.where(allowed, 0.0, LOWEST)
                for h in range(heads):
                    lines = slice(h * size, (h + 1) * size)
                    part = raw[lines, side * size : (side + 1) * size]
                    part = jnp.where(hidden < 0.0, LOWEST, part)
                    scores[t, lines, side * size : (side + 1) * size] = part
                    high[lines, :] = jnp.maximum(high[lines, :], part)
            return unused

        def score_full(t, unused):
            raw = raw_scores(t)
            scores[t] = raw
            high[...] = jnp.maximum(high[...], jnp.maximum(raw[:, :size], raw[:, size:]))
            return unused

        def score_two(u, unused):
            t = edges[i] + 2 * u
            one = raw_scores(t)
            two = raw_scores(t + 1)
            scores[t] = one
            scores[t + 1] = two
            best = jnp.maximum(
                jnp.maximum(one[:, :size], one[:, size:]),
                jnp.maximum(two[:, :size], two[:, size:]),
            )
            high[...] = jnp.maximum(high[...], best)
            return unused

        lax.fori_loop(0, edges[i], score_edge, 0)
        lax.fori_loop(0, (pairs - edges[i]) // 2, score_two, 0)
        lax.fori_loop(pairs - (pairs - edges[i]) % 2, pairs, score_full, 0)
        top = jnp.maximum(jnp.max(high[...], axis=1, keepdims=True), FLOOR)
        high[...] = jnp.broadcast_to(top, high.shape)
        total[...] = jnp.zeros_like(total)

        def product(t):
            at = i * longest + 2 * t
            values = jnp.concatenate(
                [kv[place(chosen[at]) + half], kv[place(chosen[at + 1]) + half]], axis=0
            )
            values = jnp.concatenate([values, ones], axis=1)
            level = high[...]
            level = jnp.concatenate([level, level], axis=1)
            weights = jnp.exp2((scores[t] - level) * log_scale).astype(jnp.bfloat16)
            return jnp.dot(weights, values, preferred_element_type=jnp.float32)

        def blend(t, unused):
            total[...] += product(t)
            return unused

        def blend_two(u, unused):
            total[...] += product(2 * u) + product(2 * u + 1)
            return unused

        lax.fori_loop(0, pairs // 2, blend_two, 0)
        lax.fori_loop(pairs - pairs % 2, pairs, blend, 0)
        summed = total[:, width:]
        safe = jnp.where(summed > 0.0, summed, 1.0)
        result[i, 0:wide, :] = (total[:, :width] / safe).astype(jnp.bfloat16)
        line_ids = lax.broadcasted_iota(jnp.int32, (16, width), 0)
        tops = jnp.zeros((16, width), jnp.float32)
        sums = jnp.zeros((16, width), jnp.float32)
        for h in range(heads):
            lines = slice(h * size, (h + 1) * size)
            row = jnp.sum(jnp.where(row_ids == col_ids, high[lines, :], 0.0), axis=0, keepdims=True)
            tops = jnp.where(line_ids % heads == h, row, tops)
            row = jnp.sum(
                jnp.where(row_ids == col_ids, total[lines, width:], 0.0), axis=0, keepdims=True
            )
            sums = jnp.where(line_ids % heads == h, row, sums)
        live = sums > 0.0
        level = tops * log_scale + jnp.log2(jnp.where(live, sums, 1.0))
        level = jnp.where(live, level, LOWEST)
        first = level.astype(jnp.bfloat16).astype(jnp.float32)
        second = (level - first).astype(jnp.bfloat16).astype(jnp.float32)
        third = level - first - second
        stats = jnp.where(line_ids < heads, first, jnp.where(line_ids < 2 * heads, second, third))
        result[i, wide : wide + 16, :] = stats.astype(jnp.bfloat16)
        return unused

    backs = []
    for r in reversed(range(nq)):
        lax.fori_loop(r * per, (r + 1) * per, one_block, 0)
        backs.append(
            pltpu.make_async_copy(result.at[pl.ds(r * per, per)], out_refs[r], out_sem.at[r])
        )
        backs[-1].start()
    for send in sends:
        send.wait()
    for back in backs:
        back.wait()


def attend(meta, kv_parts, q_parts, log_scale):
    _, size, width = kv_parts[0].shape
    heads, rows, _ = q_parts[0].shape
    nkv, nq, per = len(kv_parts), len(q_parts), rows // size
    wide = heads * size
    longest = meta[1].shape[0] // (nq * per)
    smem = pl.BlockSpec(memory_space=pltpu.SMEM)
    anywhere = pl.BlockSpec(memory_space=pl.ANY)
    parts = jax.ShapeDtypeStruct((per, wide + 16, width), jnp.bfloat16)
    moved = jax.ShapeDtypeStruct((2 * per, size, width), jnp.bfloat16)
    return pl.pallas_call(
        functools.partial(attend_kernel, log_scale, nkv, nq),
        out_shape=(parts,) * nq + (moved,) * nq,
        in_specs=[smem] * len(meta) + [anywhere] * (nkv + nq),
        out_specs=(anywhere,) * (2 * nq),
        scratch_shapes=[
            pltpu.VMEM((sum(p.shape[0] for p in kv_parts), size, width), jnp.bfloat16),
            pltpu.VMEM((nq, heads, rows, width), jnp.bfloat16),
            pltpu.VMEM((longest // 2, wide, 2 * size), jnp.float32),
            pltpu.VMEM((wide, size), jnp.float32),
            pltpu.VMEM((wide, 2 * width), jnp.float32),
            pltpu.VMEM((nq * per, wide + 16, width), jnp.bfloat16),
            pltpu.SemaphoreType.DMA((nkv + nq,)),
            pltpu.SemaphoreType.DMA((nq,)),
            pltpu.SemaphoreType.DMA((2 * nq * per,)),
        ],
        compiler_params=pltpu.CompilerParams(vmem_limit_bytes=56 << 20),
        cost_estimate=pl.CostEstimate(
            flops=5_000_000_000, bytes_accessed=8_000_000, transcendentals=8_000_000
        ),
        name="attend",
    )(*meta, *kv_parts, *q_parts)


def finish_kernel(heads, nparts, nw, pieces, *refs):
    part_in = refs[:nparts]
    w_in = refs[nparts : nparts + nw]
    first_out = refs[nparts + nw : nparts + nw + NX]
    second_out = refs[nparts + nw + NX : nparts + nw + NX + NL]
    parts, weight, mixed_rows, first, second, part_sem, w_sem, a_sem, b_sem = refs[
        nparts + nw + NX + NL :
    ]
    group = w_in[0].shape[0]
    per, lines, width = part_in[0].shape
    size = (lines - 16) // heads
    part_loads = [
        pltpu.make_async_copy(part_in[r], parts.at[r], part_sem.at[r]) for r in range(nparts)
    ]
    w_loads = [
        pltpu.make_async_copy(w_in[a], weight.at[pl.ds(a * group, group)], w_sem.at[a])
        for a in range(nw)
    ]
    for load in part_loads + w_loads:
        load.start()
    for load in part_loads:
        load.wait()
    row_ids = lax.broadcasted_iota(jnp.int32, (size, width), 0)
    col_ids = lax.broadcasted_iota(jnp.int32, (size, width), 1)
    for s in range(per):
        levels = []
        for r in range(nparts):
            stats = parts[r, s, heads * size :, :].astype(jnp.float32)
            levels.append(
                stats[0:heads] + stats[heads : 2 * heads] + stats[2 * heads : 3 * heads]
            )
        top = functools.reduce(jnp.maximum, levels)
        shares = [jnp.exp2(level - top) for level in levels]
        whole = functools.reduce(jnp.add, shares)
        shares = [share / whole for share in shares]
        for h in range(heads):
            mixed = jnp.zeros((size, width), jnp.float32)
            for r in range(nparts):
                spread = jnp.where(row_ids == col_ids, shares[r][h : h + 1, :], 0.0)
                column = jnp.sum(spread, axis=1, keepdims=True)
                mixed += column * parts[r, s, h * size : (h + 1) * size, :].astype(jnp.float32)
            mixed_rows[s * size : (s + 1) * size, h * width : (h + 1) * width] = mixed.astype(
                jnp.bfloat16
            )
    for load in w_loads:
        load.wait()
    sends = []
    for r in reversed(range(NX)):
        at = r * NL * group
        rows = jnp.concatenate([weight[pieces[at + q]] for q in range(NL * group)], axis=0)
        product = lax.dot_general(
            mixed_rows[...], rows, (((1,), (1,)), ((), ())), preferred_element_type=jnp.float32
        ).astype(jnp.bfloat16)
        columns = product.shape[1] // NL
        for z in range(NL):
            first[r, z] = product[:size, z * columns : (z + 1) * columns]
            second[z, r] = product[size:, z * columns : (z + 1) * columns]
        sends.append(pltpu.make_async_copy(first.at[r], first_out[r], a_sem.at[r]))
        sends[-1].start()
    for z in range(NL):
        sends.append(pltpu.make_async_copy(second.at[z], second_out[z], b_sem.at[z]))
        sends[-1].start()
    for send in sends:
        send.wait()


def finish(pieces, parts, w_parts, heads):
    per, lines, width = parts[0].shape
    size = (lines - 16) // heads
    group, rows, depth = w_parts[0].shape
    columns = group * rows
    nparts, nw = len(parts), len(w_parts)
    anywhere = pl.BlockSpec(memory_space=pl.ANY)
    first = jax.ShapeDtypeStruct((NL, size, columns), jnp.bfloat16)
    second = jax.ShapeDtypeStruct((NX, size, columns), jnp.bfloat16)
    return pl.pallas_call(
        functools.partial(finish_kernel, heads, nparts, nw),
        out_shape=(first,) * NX + (second,) * NL,
        in_specs=[pl.BlockSpec(memory_space=pltpu.SMEM)] + [anywhere] * (nparts + nw),
        out_specs=(anywhere,) * (NX + NL),
        scratch_shapes=[
            pltpu.VMEM((nparts, per, lines, width), jnp.bfloat16),
            pltpu.VMEM((nw * group, rows, depth), jnp.bfloat16),
            pltpu.VMEM((per * size, heads * width), jnp.bfloat16),
            pltpu.VMEM((NX, NL, size, columns), jnp.bfloat16),
            pltpu.VMEM((NL, NX, size, columns), jnp.bfloat16),
            pltpu.SemaphoreType.DMA((nparts,)),
            pltpu.SemaphoreType.DMA((nw,)),
            pltpu.SemaphoreType.DMA((NX,)),
            pltpu.SemaphoreType.DMA((NL,)),
        ],
        compiler_params=pltpu.CompilerParams(vmem_limit_bytes=24 << 20),
        cost_estimate=pl.CostEstimate(
            flops=2_000_000_000, bytes_accessed=12_000_000, transcendentals=10_000
        ),
        name="finish",
    )(pieces, *parts, *w_parts)


def piece_table(device, head, group):
    c = device % NC
    z = device // NC % NZ
    y = device // (NC * NZ)
    steps = jnp.array(SHIFTS, jnp.int32)
    target = (head // NL + steps[:, None]) % NX * NL + (head + jnp.arange(NL)[None, :]) % NL
    owner = (target.reshape(-1)[:, None] * group + jnp.arange(group)[None, :]).reshape(-1)
    place = ring_place(y - owner // (NC * NZ)) * NC + (c + owner) % NC
    return (place * NZ + ring_place(z - owner // NC % NZ)).astype(jnp.int32)


def refill_kernel(nq, source, ck, cv, *refs):
    moved = refs[:nq]
    new_ck, new_cv, blocks, in_sem, out_sem = refs[nq:]
    per = moved[0].shape[0] // 2
    old = ck.shape[0] - per

    def load(s, r):
        return pltpu.make_async_copy(
            moved[r].at[pl.ds(2 * s, 2)], blocks.at[pl.ds(2 * s, 2)], in_sem.at[s]
        )

    for step in ("start", "wait"):
        for s in range(per):
            for r in range(nq):

                @pl.when(source[s] == r)
                def _():
                    getattr(load(s, r), step)()

    stores = []
    for s in range(per):
        for side, new in enumerate((new_ck, new_cv)):
            stores.append(
                pltpu.make_async_copy(
                    blocks.at[2 * s + side], new.at[old + s], out_sem.at[2 * s + side]
                )
            )
    for store in stores:
        store.start()
    for store in stores:
        store.wait()


def keep_kernel(ck, cv, new_ck, new_cv):
    new_ck[...] = ck[...]
    new_cv[...] = cv[...]


def keep(ck, cv):
    shape = jax.ShapeDtypeStruct(ck.shape, ck.dtype)
    return pl.pallas_call(keep_kernel, out_shape=(shape, shape), name="keep")(ck, cv)


def refill(source, ck, cv, moved):
    shape = jax.ShapeDtypeStruct(ck.shape, ck.dtype)
    anywhere = pl.BlockSpec(memory_space=pl.ANY)
    nq = len(moved)
    per = moved[0].shape[0] // 2
    return pl.pallas_call(
        functools.partial(refill_kernel, nq),
        out_shape=(shape, shape),
        in_specs=[pl.BlockSpec(memory_space=pltpu.SMEM)] + [anywhere] * (2 + nq),
        out_specs=(anywhere, anywhere),
        scratch_shapes=[
            pltpu.VMEM(moved[0].shape, moved[0].dtype),
            pltpu.SemaphoreType.DMA((per,)),
            pltpu.SemaphoreType.DMA((2 * per,)),
        ],
        input_output_aliases={1: 0, 2: 1},
        name="refill",
    )(source, ck, cv, *moved)


def plan(device, per, slots, size, cache_len, span_len, block_table, window):
    old = slots - per
    c = device % NC
    z = device // NC % NZ
    y = device // (NC * NZ)
    ring = jnp.array([-k for k in SHIFTS], jnp.int32)
    q_dev = ((y + ring) % NY * NZ + z) * NC + c
    pair = jnp.arange(NC, dtype=jnp.int32)
    k_dev = ((y * NZ + (z + ring[:, None]) % NZ) * NC + (c + pair[None, :]) % NC).reshape(-1)
    slot = jnp.arange(slots, dtype=jnp.int32)
    step = jnp.arange(per, dtype=jnp.int32)
    q_ids = (q_dev[:, None] * per + step[None, :]).reshape(-1)
    q_request, q_first = block_start(q_ids, span_len, cache_len, size)
    q_window = lookup(window, q_request)
    within = jnp.tile(slot, k_dev.shape[0])
    owner = jnp.repeat(k_dev, slots)
    is_old = within < old
    o_request, o_logical, o_live = slot_owner(block_table, cache_len // size, owner * slots + within)
    n_request, n_first = block_start(
        owner * per + jnp.maximum(within - old, 0), span_len, cache_len, size
    )
    k_request = jnp.where(is_old, o_request, n_request)
    k_first = jnp.where(is_old, o_logical * size, n_first)
    live = jnp.where(is_old, o_live, True)
    last = q_first + size - 1
    seen = (
        live[None, :]
        & (q_request[:, None] == k_request[None, :])
        & (k_first[None, :] <= last[:, None])
        & (
            (k_first[None, :] < SINK)
            | (q_first[:, None] - (k_first[None, :] + size - 1) < q_window[:, None])
        )
    )
    inside = (k_first[None, :] + size - 1 <= q_first[:, None]) & (
        last[:, None] - k_first[None, :] < q_window[:, None]
    )
    total = k_first.shape[0]
    ids = jnp.arange(total, dtype=jnp.int32)
    hits = seen.astype(jnp.int32)
    rim = (seen & ~inside).astype(jnp.int32)
    count = jnp.sum(hits, axis=1)
    rims = jnp.sum(rim, axis=1)
    odd = count % 2
    before = ids[None, None, :] < ids[None, :, None]
    rim_rank = jnp.sum(jnp.where(before, rim[:, None, :], 0), axis=2)
    rank = jnp.sum(jnp.where(before, hits[:, None, :], 0), axis=2)
    rank = odd[:, None] + jnp.where(rim > 0, rim_rank, rims[:, None] + rank - rim_rank)
    at = seen[:, None, :] & (rank[:, None, :] == ids[None, :, None])
    packed = jnp.sum(jnp.where(at, (k_first * total + ids)[None, None, :] + 1, 0), axis=2)
    chosen = jnp.maximum(packed - 1, 0) % total
    first_key = jnp.where(packed > 0, jnp.maximum(packed - 1, 0) // total, FAR)
    edges = (odd + rims + 1) // 2
    targets = table_entry(block_table, n_request, n_first // size)
    wanted = (q_dev[:, None] * slots + old + step[None, :]).reshape(-1)
    hit = (targets[None, :] == wanted[:, None]) & ~is_old[None, :]
    moves = jnp.sum(jnp.where(hit, ids[None, :], 0), axis=1)
    all_new = jnp.arange(NY * NZ * NC * per, dtype=jnp.int32)
    a_request, a_first = block_start(all_new, span_len, cache_len, size)
    a_target = table_entry(block_table, a_request, a_first // size)
    mine = a_target[None, :] == (device * slots + old + step)[:, None]
    from_y = jnp.sum(jnp.where(mine, (all_new // (per * NC * NZ))[None, :], 0), axis=1)
    source = ring_place(from_y - y)
    meta = (
        count,
        chosen.reshape(-1),
        edges,
        first_key.reshape(-1),
        q_first,
        q_window,
        moves,
    )
    return meta, source


def shards(
    queries,
    new_keys,
    new_values,
    cache_keys,
    cache_values,
    out_weight,
    cache_len,
    span_len,
    block_table,
    window,
):
    device = lax.axis_index("blk")
    head = lax.axis_index("head")
    tokens, heads, width = queries.shape
    slots, size = cache_keys.shape[:2]
    per = tokens // size
    log_scale = math.log2(math.e) / math.sqrt(width)
    ck = cache_keys.reshape(slots, size, width)
    cv = cache_values.reshape(slots, size, width)
    own_q = jnp.transpose(queries, (1, 0, 2))
    w_line = [out_weight] + [shift(out_weight, dz=k) for k in SHIFTS[1:]]
    q_near = [shift(own_q, dy=k) for k in SHIFTS[1:3]]
    own_kv = pack(
        ck, cv, new_keys.reshape(per, size, width), new_values.reshape(per, size, width)
    )
    own_kv = after(own_kv, *w_line[1:], *q_near)
    kv_near = [shift(own_kv, dz=k) for k in SHIFTS[1:3]]
    q_parts = [own_q, *q_near, shift(after(own_q, *q_near), dy=SHIFTS[3])]
    w_four = jnp.stack(w_line)
    w_four = after(w_four, q_parts[3])
    w_near = [shift(w_four, dy=k) for k in SHIFTS[1:3]]
    far = [
        shift(kv_near[0][:slots], dz=SHIFTS[1]),
        shift(kv_near[1][slots:], dz=SHIFTS[2]),
    ]
    w_far = [*w_near, shift(after(w_four, *w_near), dy=SHIFTS[3])]
    kv_parts = []
    for part in (own_kv, *kv_near):
        kv_parts += [part, shift(part, dc=1)]
    kv_parts += far + [shift(part, dc=1) for part in far]
    w_parts = []
    for part in (w_four, *w_near):
        w_parts += [part, shift(part, dc=1)]
    meta, source = plan(device, per, slots, size, cache_len, span_len, block_table, window)
    outs = attend(meta, kv_parts, q_parts, log_scale)
    parts, moved = outs[: len(SHIFTS)], outs[len(SHIFTS) :]
    parts = [parts[0]] + [shift(p, dy=-k) for p, k in zip(parts[1:], SHIFTS[1:])]
    w_far[2] = after(w_far[2], *parts[1:])
    w_parts += [w_far[2], shift(w_far[2], dc=1)]
    pieces = piece_table(device, head, heads * width // out_weight.shape[0])
    shares = finish(pieces, [in_hbm(p) for p in parts], w_parts, heads)
    first, second = shares[:NX], shares[NX:]
    first = [first[0]] + [head_shift(p, dx=k) for p, k in zip(first[1:], SHIFTS[1:])]
    moved = list(moved)
    for r in (1, 2):
        moved[r] = shift(after(moved[r], first[1]), dy=-SHIFTS[r])
    moved[3] = shift(after(moved[3], moved[1]), dy=-SHIFTS[3])
    second_sum = second[0].astype(jnp.float32) + head_shift(second[1], dz=1).astype(jnp.float32)
    first_sum = functools.reduce(jnp.add, [p.astype(jnp.float32) for p in first])
    second_sum = after(second_sum, moved[1], moved[2])
    second_far = [
        head_shift(second_sum[r].astype(jnp.bfloat16), dx=SHIFTS[r]) for r in range(1, NX)
    ]
    second_out = functools.reduce(
        jnp.add, [p.astype(jnp.float32) for p in second_far], second_sum[0]
    )
    first_out = first_sum[0] + head_shift(first_sum[1].astype(jnp.bfloat16), dz=1).astype(
        jnp.float32
    )
    attn_output = jnp.concatenate([first_out, second_out], axis=0).astype(jnp.bfloat16)
    moved[1] = after(moved[1], second_far[0])
    new_ck, new_cv = refill(source, *keep(after(ck, parts[1]), cv), moved)
    return (
        attn_output,
        new_ck.reshape(cache_keys.shape),
        new_cv.reshape(cache_values.shape),
    )


def solution(mesh):
    placed = (
        P("blk", "head", None),
        P("blk", "head", None),
        P("blk", "head", None),
        P("blk", None, "head", None),
        P("blk", None, "head", None),
        P("blk", "head"),
        P(),
        P(),
        P(),
        P(),
    )
    return jax.shard_map(
        shards,
        mesh=mesh,
        in_specs=placed,
        out_specs=(P("blk", "head"), P("blk", None, "head", None), P("blk", None, "head", None)),
        check_vma=False,
    )
```

```python
import functools
import math

import jax
import jax.numpy as jnp
from jax import lax
from jax.experimental import pallas as pl
from jax.experimental.pallas import tpu as pltpu
from jax.sharding import PartitionSpec as P

NY, NZ, NC = 4, 4, 2
NX, NL = 4, 2
SINK = 4
LOWEST = -1e30
FLOOR = -1e25
FAR = 1 << 29
SHIFTS = (0, 1, -1, 2)


def blk_perm(dy, dz, dc):
    pairs = []
    for y in range(NY):
        for z in range(NZ):
            for c in range(NC):
                src = (y * NZ + z) * NC + c
                dst = ((y + dy) % NY * NZ + (z + dz) % NZ) * NC + (c + dc) % NC
                pairs.append((src, dst))
    return pairs


def shift(value, dy=0, dz=0, dc=0):
    return lax.ppermute(value, "blk", blk_perm(dy, dz, dc))


def after(value, *earlier):
    return lax.optimization_barrier((value, *earlier))[0]


def in_hbm(value):
    return pltpu.with_memory_space_constraint(value, pltpu.HBM)


def head_shift(value, dx=0, dz=0):
    pairs = []
    for x in range(NX):
        for z in range(NL):
            pairs.append((x * NL + z, (x + dx) % NX * NL + (z + dz) % NL))
    return lax.ppermute(value, "head", pairs)


def ring_place(distance):
    distance = distance % len(SHIFTS)
    return jnp.where(distance == 3, 2, jnp.where(distance == 2, 3, distance))


def lookup(table_row, wanted):
    places = jnp.arange(table_row.shape[0], dtype=jnp.int32)
    return jnp.sum(jnp.where(places[None, :] == wanted[:, None], table_row[None, :], 0), axis=1)


def block_start(global_block, span_len, cache_len, block_size):
    lower = jnp.arange(span_len.shape[0], dtype=jnp.int32)
    span_end = jnp.sum(jnp.where(lower[:, None] >= lower[None, :], span_len[None, :], 0), axis=1)
    first_token = global_block * block_size
    request = jnp.sum((first_token[:, None] >= span_end[None, :]).astype(jnp.int32), axis=1)
    return (request, lookup(cache_len - span_end + span_len, request) + first_token)


def table_entry(block_table, request, logical):
    row_ids = jnp.arange(block_table.shape[0], dtype=jnp.int32)
    col_ids = jnp.arange(block_table.shape[1], dtype=jnp.int32)
    match = (row_ids[None, :, None] == request[:, None, None]) & (
        col_ids[None, None, :] == logical[:, None, None]
    )
    return jnp.sum(jnp.where(match, block_table[None], 0), axis=(1, 2))


def slot_owner(block_table, limit, slot_ids):
    row_ids = jnp.arange(block_table.shape[0], dtype=jnp.int32)
    col_ids = jnp.arange(block_table.shape[1], dtype=jnp.int32)
    match = (block_table[None] == slot_ids[:, None, None]) & (
        col_ids[None, None, :] < limit[None, :, None]
    )
    packed = row_ids[:, None] * 4096 + col_ids[None, :] + 1
    found = jnp.sum(jnp.where(match, packed[None], 0), axis=(1, 2))
    place = jnp.maximum(found - 1, 0)
    return (place // 4096, place % 4096, found > 0)


def pack_kernel(ck, cv, nk, nv, out):
    new = nk.shape[0]
    old = ck.shape[0] - new
    out[0:old] = ck[0:old]
    out[old : old + new] = nk[...]
    out[old + new : 2 * old + new] = cv[0:old]
    out[2 * old + new :] = nv[...]


def pack(ck, cv, nk, nv):
    return pl.pallas_call(
        pack_kernel,
        out_shape=jax.ShapeDtypeStruct((2 * ck.shape[0],) + ck.shape[1:], ck.dtype),
        name="pack",
    )(ck, cv, nk, nv)


def attend_kernel(
    log_scale,
    nkv,
    nq,
    count,
    chosen,
    edges,
    first_key,
    first_query,
    reach,
    moves,
    *refs,
):
    kv_in = refs[:nkv]
    q_in = refs[nkv : nkv + nq]
    out_refs = refs[nkv + nq : nkv + 2 * nq]
    move_refs = refs[nkv + 2 * nq : nkv + 3 * nq]
    kv, queries, scores, high, total, result, in_sem, out_sem, move_sem = refs[nkv + 3 * nq :]
    slots = kv_in[0].shape[0]
    half = slots // 2
    begins = [sum(ref.shape[0] for ref in kv_in[:a]) for a in range(nkv)]
    heads, rows, width = q_in[0].shape
    size = kv_in[0].shape[1]
    per = rows // size
    wide = heads * size
    longest = chosen.shape[0] // (nq * per)
    loads = []
    for a in range(nkv):
        loads.append(
            pltpu.make_async_copy(
                kv_in[a], kv.at[pl.ds(begins[a], kv_in[a].shape[0])], in_sem.at[a]
            )
        )
    for r in range(nq):
        loads.append(pltpu.make_async_copy(q_in[r], queries.at[r], in_sem.at[nkv + r]))
    for load in loads:
        load.start()
    for load in loads:
        load.wait()

    def place(j):
        return j // half * slots + j % half

    sends = []
    for r in range(nq):
        for s in range(per):
            at = place(moves[r * per + s])
            for side in range(2):
                sends.append(
                    pltpu.make_async_copy(
                        kv.at[at + side * half],
                        move_refs[r].at[2 * s + side],
                        move_sem.at[(r * per + s) * 2 + side],
                    )
                )
    for send in sends:
        send.start()

    row_ids = lax.broadcasted_iota(jnp.int32, (size, width), 0)
    col_ids = lax.broadcasted_iota(jnp.int32, (size, width), 1)
    ones = jnp.ones((2 * size, width), jnp.bfloat16)

    def one_block(i, unused):
        r = i // per
        s = i % per
        begin = pl.multiple_of(s * size, size)
        query = jnp.concatenate(
            [queries[r, h, pl.ds(begin, size), :] for h in range(heads)], axis=0
        )
        pairs = (count[i] + 1) // 2
        high[...] = jnp.full_like(high, LOWEST)

        def raw_scores(t):
            at = i * longest + 2 * t
            keys = jnp.concatenate([kv[place(chosen[at])], kv[place(chosen[at + 1])]], axis=0)
            return lax.dot_general(
                query, keys, (((1,), (1,)), ((), ())), preferred_element_type=jnp.float32
            )

        def score_edge(t, unused):
            raw = raw_scores(t)
            for side in range(2):
                key_pos = first_key[i * longest + 2 * t + side] + col_ids
                distance = first_query[i] + row_ids - key_pos
                allowed = (distance >= 0) & ((distance < reach[i]) | (key_pos < SINK))
                hidden = jnp.where(allowed, 0.0, LOWEST)
                for h in range(heads):
                    lines = slice(h * size, (h + 1) * size)
                    part = raw[lines, side * size : (side + 1) * size]
                    part = jnp.where(hidden < 0.0, LOWEST, part)
                    scores[t, lines, side * size : (side + 1) * size] = part
                    high[lines, :] = jnp.maximum(high[lines, :], part)
            return unused

        def score_full(t, unused):
            raw = raw_scores(t)
            scores[t] = raw
            high[...] = jnp.maximum(high[...], jnp.maximum(raw[:, :size], raw[:, size:]))
            return unused

        def score_two(u, unused):
            t = edges[i] + 2 * u
            one = raw_scores(t)
            two = raw_scores(t + 1)
            scores[t] = one
            scores[t + 1] = two
            best = jnp.maximum(
                jnp.maximum(one[:, :size], one[:, size:]),
                jnp.maximum(two[:, :size], two[:, size:]),
            )
            high[...] = jnp.maximum(high[...], best)
            return unused

        lax.fori_loop(0, edges[i], score_edge, 0)
        lax.fori_loop(0, (pairs - edges[i]) // 2, score_two, 0)
        lax.fori_loop(pairs - (pairs - edges[i]) % 2, pairs, score_full, 0)
        top = jnp.maximum(jnp.max(high[...], axis=1, keepdims=True), FLOOR)
        high[...] = jnp.broadcast_to(top, high.shape)
        total[...] = jnp.zeros_like(total)

        def product(t):
            at = i * longest + 2 * t
            values = jnp.concatenate(
                [kv[place(chosen[at]) + half], kv[place(chosen[at + 1]) + half]], axis=0
            )
            values = jnp.concatenate([values, ones], axis=1)
            level = high[...]
            level = jnp.concatenate([level, level], axis=1)
            weights = jnp.exp2((scores[t] - level) * log_scale).astype(jnp.bfloat16)
            return jnp.dot(weights, values, preferred_element_type=jnp.float32)

        def blend(t, unused):
            total[...] += product(t)
            return unused

        def blend_two(u, unused):
            total[...] += product(2 * u) + product(2 * u + 1)
            return unused

        lax.fori_loop(0, pairs // 2, blend_two, 0)
        lax.fori_loop(pairs - pairs % 2, pairs, blend, 0)
        summed = total[:, width:]
        safe = jnp.where(summed > 0.0, summed, 1.0)
        result[i, 0:wide, :] = (total[:, :width] / safe).astype(jnp.bfloat16)
        line_ids = lax.broadcasted_iota(jnp.int32, (16, width), 0)
        tops = jnp.zeros((16, width), jnp.float32)
        sums = jnp.zeros((16, width), jnp.float32)
        for h in range(heads):
            lines = slice(h * size, (h + 1) * size)
            row = jnp.sum(jnp.where(row_ids == col_ids, high[lines, :], 0.0), axis=0, keepdims=True)
            tops = jnp.where(line_ids % heads == h, row, tops)
            row = jnp.sum(
                jnp.where(row_ids == col_ids, total[lines, width:], 0.0), axis=0, keepdims=True
            )
            sums = jnp.where(line_ids % heads == h, row, sums)
        live = sums > 0.0
        level = tops * log_scale + jnp.log2(jnp.where(live, sums, 1.0))
        level = jnp.where(live, level, LOWEST)
        first = level.astype(jnp.bfloat16).astype(jnp.float32)
        second = (level - first).astype(jnp.bfloat16).astype(jnp.float32)
        third = level - first - second
        stats = jnp.where(line_ids < heads, first, jnp.where(line_ids < 2 * heads, second, third))
        result[i, wide : wide + 16, :] = stats.astype(jnp.bfloat16)
        return unused

    lax.fori_loop(0, nq * per, one_block, 0)
    backs = []
    for r in range(nq):
        backs.append(
            pltpu.make_async_copy(result.at[pl.ds(r * per, per)], out_refs[r], out_sem.at[r])
        )
        backs[-1].start()
    for send in sends:
        send.wait()
    for back in backs:
        back.wait()


def attend(meta, kv_parts, q_parts, log_scale):
    _, size, width = kv_parts[0].shape
    heads, rows, _ = q_parts[0].shape
    nkv, nq, per = len(kv_parts), len(q_parts), rows // size
    wide = heads * size
    longest = meta[1].shape[0] // (nq * per)
    smem = pl.BlockSpec(memory_space=pltpu.SMEM)
    anywhere = pl.BlockSpec(memory_space=pl.ANY)
    parts = jax.ShapeDtypeStruct((per, wide + 16, width), jnp.bfloat16)
    moved = jax.ShapeDtypeStruct((2 * per, size, width), jnp.bfloat16)
    return pl.pallas_call(
        functools.partial(attend_kernel, log_scale, nkv, nq),
        out_shape=(parts,) * nq + (moved,) * nq,
        in_specs=[smem] * len(meta) + [anywhere] * (nkv + nq),
        out_specs=(anywhere,) * (2 * nq),
        scratch_shapes=[
            pltpu.VMEM((sum(p.shape[0] for p in kv_parts), size, width), jnp.bfloat16),
            pltpu.VMEM((nq, heads, rows, width), jnp.bfloat16),
            pltpu.VMEM((longest // 2, wide, 2 * size), jnp.float32),
            pltpu.VMEM((wide, size), jnp.float32),
            pltpu.VMEM((wide, 2 * width), jnp.float32),
            pltpu.VMEM((nq * per, wide + 16, width), jnp.bfloat16),
            pltpu.SemaphoreType.DMA((nkv + nq,)),
            pltpu.SemaphoreType.DMA((nq,)),
            pltpu.SemaphoreType.DMA((2 * nq * per,)),
        ],
        compiler_params=pltpu.CompilerParams(vmem_limit_bytes=56 << 20),
        cost_estimate=pl.CostEstimate(
            flops=5_000_000_000, bytes_accessed=8_000_000, transcendentals=8_000_000
        ),
        name="attend",
    )(*meta, *kv_parts, *q_parts)


def finish_kernel(heads, nparts, nw, pieces, *refs):
    part_in = refs[:nparts]
    w_in = refs[nparts : nparts + nw]
    first_out = refs[nparts + nw : nparts + nw + NX]
    second_out = refs[nparts + nw + NX : nparts + nw + NX + NL]
    parts, weight, mixed_rows, first, second, part_sem, w_sem, a_sem, b_sem = refs[
        nparts + nw + NX + NL :
    ]
    group = w_in[0].shape[0]
    per, lines, width = part_in[0].shape
    size = (lines - 16) // heads
    part_loads = [
        pltpu.make_async_copy(part_in[r], parts.at[r], part_sem.at[r]) for r in range(nparts)
    ]
    w_loads = [
        pltpu.make_async_copy(w_in[a], weight.at[pl.ds(a * group, group)], w_sem.at[a])
        for a in range(nw)
    ]
    for load in part_loads + w_loads:
        load.start()
    for load in part_loads:
        load.wait()
    row_ids = lax.broadcasted_iota(jnp.int32, (size, width), 0)
    col_ids = lax.broadcasted_iota(jnp.int32, (size, width), 1)
    for s in range(per):
        levels = []
        for r in range(nparts):
            stats = parts[r, s, heads * size :, :].astype(jnp.float32)
            levels.append(
                stats[0:heads] + stats[heads : 2 * heads] + stats[2 * heads : 3 * heads]
            )
        top = functools.reduce(jnp.maximum, levels)
        shares = [jnp.exp2(level - top) for level in levels]
        whole = functools.reduce(jnp.add, shares)
        shares = [share / whole for share in shares]
        for h in range(heads):
            mixed = jnp.zeros((size, width), jnp.float32)
            for r in range(nparts):
                spread = jnp.where(row_ids == col_ids, shares[r][h : h + 1, :], 0.0)
                column = jnp.sum(spread, axis=1, keepdims=True)
                mixed += column * parts[r, s, h * size : (h + 1) * size, :].astype(jnp.float32)
            mixed_rows[s * size : (s + 1) * size, h * width : (h + 1) * width] = mixed.astype(
                jnp.bfloat16
            )
    for load in w_loads:
        load.wait()
    sends = []
    for r in reversed(range(NX)):
        for z in range(NL):
            at = (r * NL + z) * group
            rows = jnp.concatenate([weight[pieces[at + q]] for q in range(group)], axis=0)
            product = lax.dot_general(
                mixed_rows[...], rows, (((1,), (1,)), ((), ())), preferred_element_type=jnp.float32
            ).astype(jnp.bfloat16)
            first[r, z] = product[:size]
            second[z, r] = product[size:]
        sends.append(pltpu.make_async_copy(first.at[r], first_out[r], a_sem.at[r]))
        sends[-1].start()
    for z in range(NL):
        sends.append(pltpu.make_async_copy(second.at[z], second_out[z], b_sem.at[z]))
        sends[-1].start()
    for send in sends:
        send.wait()


def finish(pieces, parts, w_parts, heads):
    per, lines, width = parts[0].shape
    size = (lines - 16) // heads
    group, rows, depth = w_parts[0].shape
    columns = group * rows
    nparts, nw = len(parts), len(w_parts)
    anywhere = pl.BlockSpec(memory_space=pl.ANY)
    first = jax.ShapeDtypeStruct((NL, size, columns), jnp.bfloat16)
    second = jax.ShapeDtypeStruct((NX, size, columns), jnp.bfloat16)
    return pl.pallas_call(
        functools.partial(finish_kernel, heads, nparts, nw),
        out_shape=(first,) * NX + (second,) * NL,
        in_specs=[pl.BlockSpec(memory_space=pltpu.SMEM)] + [anywhere] * (nparts + nw),
        out_specs=(anywhere,) * (NX + NL),
        scratch_shapes=[
            pltpu.VMEM((nparts, per, lines, width), jnp.bfloat16),
            pltpu.VMEM((nw * group, rows, depth), jnp.bfloat16),
            pltpu.VMEM((per * size, heads * width), jnp.bfloat16),
            pltpu.VMEM((NX, NL, size, columns), jnp.bfloat16),
            pltpu.VMEM((NL, NX, size, columns), jnp.bfloat16),
            pltpu.SemaphoreType.DMA((nparts,)),
            pltpu.SemaphoreType.DMA((nw,)),
            pltpu.SemaphoreType.DMA((NX,)),
            pltpu.SemaphoreType.DMA((NL,)),
        ],
        compiler_params=pltpu.CompilerParams(vmem_limit_bytes=24 << 20),
        cost_estimate=pl.CostEstimate(
            flops=2_000_000_000, bytes_accessed=12_000_000, transcendentals=10_000
        ),
        name="finish",
    )(pieces, *parts, *w_parts)


def piece_table(device, head, group):
    c = device % NC
    z = device // NC % NZ
    y = device // (NC * NZ)
    steps = jnp.array(SHIFTS, jnp.int32)
    target = (head // NL + steps[:, None]) % NX * NL + (head + jnp.arange(NL)[None, :]) % NL
    owner = (target.reshape(-1)[:, None] * group + jnp.arange(group)[None, :]).reshape(-1)
    place = ring_place(y - owner // (NC * NZ)) * NC + (c + owner) % NC
    return (place * NZ + ring_place(z - owner // NC % NZ)).astype(jnp.int32)


def refill_kernel(nq, source, ck, cv, *refs):
    moved_in = refs[:nq]
    new_ck, new_cv, moved, sem = refs[nq:]
    per = moved_in[0].shape[0] // 2
    old = ck.shape[0] - per
    loads = [pltpu.make_async_copy(moved_in[r], moved.at[r], sem.at[r]) for r in range(nq)]
    for load in loads:
        load.start()
    new_ck[0:old] = ck[0:old]
    new_cv[0:old] = cv[0:old]
    for load in loads:
        load.wait()
    for s in range(per):
        new_ck[old + s] = moved[source[s], 2 * s]
        new_cv[old + s] = moved[source[s], 2 * s + 1]


def refill(source, ck, cv, moved):
    shape = jax.ShapeDtypeStruct(ck.shape, ck.dtype)
    whole = pl.BlockSpec(memory_space=pltpu.VMEM)
    anywhere = pl.BlockSpec(memory_space=pl.ANY)
    nq = len(moved)
    return pl.pallas_call(
        functools.partial(refill_kernel, nq),
        out_shape=(shape, shape),
        in_specs=[pl.BlockSpec(memory_space=pltpu.SMEM)] + [whole] * 2 + [anywhere] * nq,
        out_specs=(whole, whole),
        scratch_shapes=[
            pltpu.VMEM((nq,) + moved[0].shape, moved[0].dtype),
            pltpu.SemaphoreType.DMA((nq,)),
        ],
        name="refill",
    )(source, ck, cv, *moved)


def plan(device, per, slots, size, cache_len, span_len, block_table, window):
    old = slots - per
    c = device % NC
    z = device // NC % NZ
    y = device // (NC * NZ)
    ring = jnp.array([-k for k in SHIFTS], jnp.int32)
    q_dev = ((y + ring) % NY * NZ + z) * NC + c
    pair = jnp.arange(NC, dtype=jnp.int32)
    k_dev = ((y * NZ + (z + ring[:, None]) % NZ) * NC + (c + pair[None, :]) % NC).reshape(-1)
    slot = jnp.arange(slots, dtype=jnp.int32)
    step = jnp.arange(per, dtype=jnp.int32)
    q_ids = (q_dev[:, None] * per + step[None, :]).reshape(-1)
    q_request, q_first = block_start(q_ids, span_len, cache_len, size)
    q_window = lookup(window, q_request)
    within = jnp.tile(slot, k_dev.shape[0])
    owner = jnp.repeat(k_dev, slots)
    is_old = within < old
    o_request, o_logical, o_live = slot_owner(block_table, cache_len // size, owner * slots + within)
    n_request, n_first = block_start(
        owner * per + jnp.maximum(within - old, 0), span_len, cache_len, size
    )
    k_request = jnp.where(is_old, o_request, n_request)
    k_first = jnp.where(is_old, o_logical * size, n_first)
    live = jnp.where(is_old, o_live, True)
    last = q_first + size - 1
    seen = (
        live[None, :]
        & (q_request[:, None] == k_request[None, :])
        & (k_first[None, :] <= last[:, None])
        & (
            (k_first[None, :] < SINK)
            | (q_first[:, None] - (k_first[None, :] + size - 1) < q_window[:, None])
        )
    )
    inside = (k_first[None, :] + size - 1 <= q_first[:, None]) & (
        last[:, None] - k_first[None, :] < q_window[:, None]
    )
    total = k_first.shape[0]
    ids = jnp.arange(total, dtype=jnp.int32)
    hits = seen.astype(jnp.int32)
    rim = (seen & ~inside).astype(jnp.int32)
    count = jnp.sum(hits, axis=1)
    rims = jnp.sum(rim, axis=1)
    odd = count % 2
    before = ids[None, None, :] < ids[None, :, None]
    rim_rank = jnp.sum(jnp.where(before, rim[:, None, :], 0), axis=2)
    rank = jnp.sum(jnp.where(before, hits[:, None, :], 0), axis=2)
    rank = odd[:, None] + jnp.where(rim > 0, rim_rank, rims[:, None] + rank - rim_rank)
    at = seen[:, None, :] & (rank[:, None, :] == ids[None, :, None])
    packed = jnp.sum(jnp.where(at, (k_first * total + ids)[None, None, :] + 1, 0), axis=2)
    chosen = jnp.maximum(packed - 1, 0) % total
    first_key = jnp.where(packed > 0, jnp.maximum(packed - 1, 0) // total, FAR)
    edges = (odd + rims + 1) // 2
    targets = table_entry(block_table, n_request, n_first // size)
    wanted = (q_dev[:, None] * slots + old + step[None, :]).reshape(-1)
    hit = (targets[None, :] == wanted[:, None]) & ~is_old[None, :]
    moves = jnp.sum(jnp.where(hit, ids[None, :], 0), axis=1)
    all_new = jnp.arange(NY * NZ * NC * per, dtype=jnp.int32)
    a_request, a_first = block_start(all_new, span_len, cache_len, size)
    a_target = table_entry(block_table, a_request, a_first // size)
    mine = a_target[None, :] == (device * slots + old + step)[:, None]
    from_y = jnp.sum(jnp.where(mine, (all_new // (per * NC * NZ))[None, :], 0), axis=1)
    source = ring_place(from_y - y)
    meta = (
        count,
        chosen.reshape(-1),
        edges,
        first_key.reshape(-1),
        q_first,
        q_window,
        moves,
    )
    return meta, source


def shards(
    queries,
    new_keys,
    new_values,
    cache_keys,
    cache_values,
    out_weight,
    cache_len,
    span_len,
    block_table,
    window,
):
    device = lax.axis_index("blk")
    head = lax.axis_index("head")
    tokens, heads, width = queries.shape
    slots, size = cache_keys.shape[:2]
    per = tokens // size
    log_scale = math.log2(math.e) / math.sqrt(width)
    ck = cache_keys.reshape(slots, size, width)
    cv = cache_values.reshape(slots, size, width)
    own_q = jnp.transpose(queries, (1, 0, 2))
    w_line = [out_weight] + [shift(out_weight, dz=k) for k in SHIFTS[1:]]
    q_near = [shift(own_q, dy=k) for k in SHIFTS[1:3]]
    own_kv = pack(
        ck, cv, new_keys.reshape(per, size, width), new_values.reshape(per, size, width)
    )
    own_kv = after(own_kv, *w_line[1:], *q_near)
    kv_near = [shift(own_kv, dz=k) for k in SHIFTS[1:3]]
    q_parts = [own_q, *q_near, shift(after(own_q, *q_near), dy=SHIFTS[3])]
    w_four = jnp.stack(w_line)
    w_four = after(w_four, q_parts[3])
    w_near = [shift(w_four, dy=k) for k in SHIFTS[1:3]]
    far = [
        shift(kv_near[0][:slots], dz=SHIFTS[1]),
        shift(kv_near[1][slots:], dz=SHIFTS[2]),
    ]
    w_far = [*w_near, shift(after(w_four, *w_near), dy=SHIFTS[3])]
    kv_parts = []
    for part in (own_kv, *kv_near):
        kv_parts += [part, shift(part, dc=1)]
    kv_parts += far + [shift(part, dc=1) for part in far]
    w_parts = []
    for part in (w_four, *w_near):
        w_parts += [part, shift(part, dc=1)]
    meta, source = plan(device, per, slots, size, cache_len, span_len, block_table, window)
    outs = attend(meta, kv_parts, q_parts, log_scale)
    parts, moved = outs[: len(SHIFTS)], outs[len(SHIFTS) :]
    parts = [parts[0]] + [shift(p, dy=-k) for p, k in zip(parts[1:], SHIFTS[1:])]
    w_far[2] = after(w_far[2], *parts[1:])
    w_parts += [w_far[2], shift(w_far[2], dc=1)]
    pieces = piece_table(device, head, heads * width // out_weight.shape[0])
    shares = finish(pieces, [in_hbm(p) for p in parts], w_parts, heads)
    first, second = shares[:NX], shares[NX:]
    first = [first[0]] + [head_shift(p, dx=k) for p, k in zip(first[1:], SHIFTS[1:])]
    moved = list(moved)
    for r in (1, 2):
        moved[r] = shift(after(moved[r], first[1]), dy=-SHIFTS[r])
    moved[3] = shift(after(moved[3], moved[1]), dy=-SHIFTS[3])
    second_sum = second[0].astype(jnp.float32) + head_shift(second[1], dz=1).astype(jnp.float32)
    first_sum = functools.reduce(jnp.add, [p.astype(jnp.float32) for p in first])
    second_sum = after(second_sum, moved[1], moved[2])
    second_far = [
        head_shift(second_sum[r].astype(jnp.bfloat16), dx=SHIFTS[r]) for r in range(1, NX)
    ]
    second_out = functools.reduce(
        jnp.add, [p.astype(jnp.float32) for p in second_far], second_sum[0]
    )
    first_out = first_sum[0] + head_shift(first_sum[1].astype(jnp.bfloat16), dz=1).astype(
        jnp.float32
    )
    attn_output = jnp.concatenate([first_out, second_out], axis=0).astype(jnp.bfloat16)
    moved[1] = after(moved[1], second_far[0])
    new_ck, new_cv = refill(source, ck, cv, moved)
    return (
        attn_output,
        new_ck.reshape(cache_keys.shape),
        new_cv.reshape(cache_values.shape),
    )


def solution(mesh):
    placed = (
        P("blk", "head", None),
        P("blk", "head", None),
        P("blk", "head", None),
        P("blk", None, "head", None),
        P("blk", None, "head", None),
        P("blk", "head"),
        P(),
        P(),
        P(),
        P(),
    )
    return jax.shard_map(
        shards,
        mesh=mesh,
        in_specs=placed,
        out_specs=(P("blk", "head"), P("blk", None, "head", None), P("blk", None, "head", None)),
        check_vma=False,
    )
```
